32 devices in a mesh: space: 4 (over y, core), vel: 8 (over z, x).
Axes of the slice: x: 2, y: 2, z: 4, core: 2. Of those that a mesh axis runs over, the one named last changes fastest.
Arguments:
- distribution: float32 [6, 1024, 4096], P(None, 'space', 'vel'), may hold values from -4 to 4
- corners: float32 [2, 3, 1024], P(None, None, 'space'), may hold values from -1 to 49, as said below
- neighbour: int32 [3, 1024], P(None, 'space'), may hold values from -1 to 767, as said below
- boundary_faces: int32 [4, 2, 80], P('space'), may hold values from -1 to 767, as said below
- collision_rate: float32 [1024], P('space'), may hold values from 1 to 20
Outputs:
- advanced: float32 [6, 1024, 4096], P(None, 'space', 'vel')
The draws below stay inside these ranges and needn't reach their ends.
Inputs may be any that keep to these rules, and one draw needn't show every extreme that they name: corners[:, k, e] are the coordinates of corner k of triangle e, counterclockwise; triangles sharing an edge hold its two corners at equal coordinates; every det_e is 0.1 or more. neighbour[m, e] = m' 256 + e' names the face of a triangle of the same partition that shares face m of triangle e and runs along it the other way; -1 where the triangle on the other side lies in another partition or the face lies on the domain's two ends. boundary_faces[p, 0] and boundary_faces[p, 1] list local face numbers of partition p whose other side lies in partition p - 1 (for p = 0, the domain's lower end) and p + 1 (for the last partition, the upper end); slot k of p's second list and slot k of p + 1's first list are the two sides of one edge, run the other way; a slot is -1 in both lists or in neither; every face with neighbour -1 stands in exactly one slot; each list's live slots come first; some list has all 80 slots live.
All inputs are finite; a program needn't handle non-finite values. Where the reference program divides by a largest or mean magnitude, that divisor is 1e-20 or more.
Results may differ from the reference program's by a relative error of at most 0.0003.
Values sent between devices are 32-bit elements; how exact they have to be, the bound alone decides.
No kernel may reach another device: no remote copies, remote signals or barrier semaphores. Data moves between devices by JAX's collectives and lax.ppermute only.
A program may use at most 128 MiB of HBM per device.

```python
import math
import jax
import jax.numpy as jnp
import numpy as np
from jax import lax

VGRID = 64
VEL = 4096
MODES = 6
QPTS = 3
HEIGHT = 16
BREADTH = 8
STAGGER = 2
ELEM_DEV = 256
MESH_CELL_TOTAL = 1024
BORDER = 80
N_SPACE = 4


def mesh_layout(key):
    inner = jax.random.randint(jax.random.fold_in(key, 101), (N_SPACE - 1,), 0, STAGGER + 1).astype(jnp.int32)
    chosen = jax.random.randint(jax.random.fold_in(key, 102), (), 0, N_SPACE - 1)
    inner = inner.at[chosen].set(STAGGER)
    zero_end = jnp.zeros((1,), jnp.int32)
    shifts = jnp.concatenate([zero_end, inner, zero_end])
    perm_keys = jax.random.split(jax.random.fold_in(key, 103), N_SPACE)
    orders = jax.vmap(lambda subkey: jax.random.permutation(subkey, ELEM_DEV))(perm_keys).astype(jnp.int32)
    return (shifts, orders)


def locate(quad_col, quad_row, upper_half, shifts, orders):
    quad_col, quad_row = jnp.broadcast_arrays(quad_col, quad_row)
    pattern = 1 - 2 * (quad_row % 2)
    inner_borders = jnp.arange(1, N_SPACE, dtype=jnp.int32) * BREADTH + shifts[1:N_SPACE] * pattern[..., None]
    partition = jnp.sum((quad_col[..., None] >= inner_borders).astype(jnp.int32), axis=-1)
    left_edge = partition * BREADTH + shifts[partition] * pattern
    offset = quad_row * BREADTH + (shifts[partition + 1] - shifts[partition]) * (quad_row % 2)
    canonical = 2 * (offset + quad_col - left_edge) + upper_half
    return (partition, orders[partition, canonical])


def quad_grid():
    columns = N_SPACE * BREADTH
    quad_col = jnp.broadcast_to(jnp.arange(columns, dtype=jnp.int32)[:, None], (columns, HEIGHT))
    quad_row = jnp.broadcast_to(jnp.arange(HEIGHT, dtype=jnp.int32)[None, :], (columns, HEIGHT))
    return (quad_col, quad_row)


def draw_neighbour(key, part):
    shifts, orders = mesh_layout(key)
    columns = N_SPACE * BREADTH
    quad_col, quad_row = quad_grid()
    result = jnp.full((3, MESH_CELL_TOTAL), -1, jnp.int32)
    adjacency = [(0, 0, 0, -1, 1, 1), (0, 1, 1, 0, 1, 2), (0, 2, 0, 0, 1, 0), (1, 0, 0, 0, 0, 2), (1, 1, 0, 1, 0, 0), (1, 2, -1, 0, 0, 1)]
    for upper_half, face_index, step_col, step_row, other_half, other_face in adjacency:
        partition, local_index = locate(quad_col, quad_row, upper_half, shifts, orders)
        target_col = quad_col + step_col
        in_domain = (target_col >= 0) & (target_col < columns)
        target_row = (quad_row + step_row) % HEIGHT
        other_part, other_local = locate(jnp.clip(target_col, 0, columns - 1), target_row, other_half, shifts, orders)
        linked = jnp.where(in_domain & (other_part == partition), other_face * ELEM_DEV + other_local, -1)
        result = result.at[face_index, (partition * ELEM_DEV + local_index).reshape(-1)].set(linked.reshape(-1))
    return result


def draw_boundary_faces(key, part):
    shifts, orders = mesh_layout(key)
    columns = N_SPACE * BREADTH
    result = jnp.full((N_SPACE, 2, BORDER), -1, jnp.int32)
    row_line = jnp.arange(HEIGHT, dtype=jnp.int32)
    pattern = 1 - 2 * (row_line % 2)
    partition = jnp.arange(N_SPACE, dtype=jnp.int32)
    rows_grid = jnp.broadcast_to(row_line[None, :], (N_SPACE, HEIGHT))
    lower_edge = partition[:, None] * BREADTH + shifts[:N_SPACE, None] * pattern[None, :]
    upper_edge = (partition[:, None] + 1) * BREADTH + shifts[1:, None] * pattern[None, :]
    unused_part, lower_local = locate(lower_edge, rows_grid, 1, shifts, orders)
    unused_other, upper_local = locate(upper_edge - 1, rows_grid, 0, shifts, orders)
    result = result.at[:, 0, :HEIGHT].set(2 * ELEM_DEV + lower_local)
    result = result.at[:, 1, :HEIGHT].set(ELEM_DEV + upper_local)
    step_line = jnp.arange(2 * STAGGER, dtype=jnp.int32)
    for side_index in range(2):
        border_index = partition + side_index
        amount = shifts[border_index][:, None, None]
        quad_col = border_index[:, None, None] * BREADTH - amount + step_line[None, None, :]
        quad_col = jnp.broadcast_to(quad_col, (N_SPACE, HEIGHT, 2 * STAGGER))
        row_three = jnp.broadcast_to(row_line[None, :, None], (N_SPACE, HEIGHT, 2 * STAGGER))
        even_row = row_three % 2 == 0
        use_lower = even_row if side_index == 0 else jnp.logical_not(even_row)
        valid_slot = step_line[None, None, :] < 2 * amount
        safe_col = jnp.clip(quad_col, 0, columns - 1)
        unused_a, below_local = locate(safe_col, (row_three + 1) % HEIGHT, 0, shifts, orders)
        unused_b, above_local = locate(safe_col, row_three, 1, shifts, orders)
        face_id = jnp.where(use_lower, below_local, ELEM_DEV + above_local)
        slot_index = jnp.where(valid_slot, HEIGHT + row_three * 2 * amount + step_line[None, None, :], BORDER)
        part_three = jnp.broadcast_to(partition[:, None, None], (N_SPACE, HEIGHT, 2 * STAGGER))
        result = result.at[part_three, side_index, slot_index].set(face_id, mode='drop')
    return result


def draw_corners(key, part):
    shifts, orders = mesh_layout(key)
    columns = N_SPACE * BREADTH
    spread = 0.12
    jitter = jax.random.uniform(jax.random.fold_in(key, 104), (2, columns + 1, HEIGHT), jnp.float32, -spread, spread)
    quad_col, quad_row = quad_grid()
    result = jnp.zeros((2, 3, MESH_CELL_TOTAL), jnp.float32)
    shapes = [(0, [(0, 0), (1, 0), (1, 1)]), (1, [(0, 0), (1, 1), (0, 1)])]
    for upper_half, vertex_list in shapes:
        partition, local_index = locate(quad_col, quad_row, upper_half, shifts, orders)
        global_id = (partition * ELEM_DEV + local_index).reshape(-1)
        for corner_index, (step_col, step_row) in enumerate(vertex_list):
            node_col = quad_col + step_col
            node_row = quad_row + step_row
            wrapped = node_row % HEIGHT
            x_value = node_col.astype(jnp.float32) + jitter[0, node_col, wrapped]
            y_value = node_row.astype(jnp.float32) + jitter[1, node_col, wrapped]
            result = result.at[0, corner_index, global_id].set(x_value.reshape(-1))
            result = result.at[1, corner_index, global_id].set(y_value.reshape(-1))
    return result


def draw_distribution(key, part):
    gas_concentration = jnp.exp(jax.random.uniform(jax.random.fold_in(key, 201), (MESH_CELL_TOTAL,), jnp.float32, math.log(0.05), math.log(2.0)))
    drift = jax.random.uniform(jax.random.fold_in(key, 202), (2, MESH_CELL_TOTAL), jnp.float32, -1.0, 1.0)
    pointwise_kelvin = jnp.exp(jax.random.uniform(jax.random.fold_in(key, 203), (MESH_CELL_TOTAL,), jnp.float32, math.log(0.12), math.log(12.0)))
    noise = jnp.clip(jax.random.normal(jax.random.fold_in(key, 206), (MODES, MESH_CELL_TOTAL, VEL), jnp.float32), -3.0, 3.0)
    velocity_index = jnp.arange(VEL, dtype=jnp.int32)
    spacing = 12.0 / VGRID
    along_x = -6.0 + ((velocity_index // VGRID).astype(jnp.float32) + 0.5) * spacing
    along_y = -6.0 + ((velocity_index % VGRID).astype(jnp.float32) + 0.5) * spacing
    peculiar_motion_first = along_x[None, :] - drift[0][:, None]
    peculiar_motion_second = along_y[None, :] - drift[1][:, None]
    gentle_taper_profile = gas_concentration[:, None] / (2.0 * math.pi * pointwise_kelvin[:, None]) * jnp.exp(-(peculiar_motion_first * peculiar_motion_first + peculiar_motion_second * peculiar_motion_second) / (2.0 * pointwise_kelvin[:, None]))
    mean_part = gentle_taper_profile[None] * (1.0 + 0.3 * noise[0:1]) / math.sqrt(2.0)
    high_part = gentle_taper_profile[None] * 0.12 * noise[1:]
    return jnp.concatenate([mean_part, high_part], axis=0)


def level_of(own_key, shape, cuts, smallest, largest):
    def one(position, parts):
        steps = jax.random.uniform(jax.random.fold_in(jax.random.fold_in(own_key, 6), position), (parts,), jnp.float32, smallest / len(cuts), largest / len(cuts))
        return jnp.repeat(jnp.exp(steps), shape[position] // parts).reshape((-1,) + (1,) * (len(shape) - position - 1))

    gain = one(*cuts[0])
    for cut in cuts[1:]:
        gain = gain * one(*cut)
    return gain


def setup_inputs(seed: int = 0) -> dict:
    splits = jax.random.split(jax.random.key(seed), 6)
    return {
        "distribution": draw_distribution(jax.random.fold_in(splits[5], 71), 0),
        "corners": draw_corners(jax.random.fold_in(splits[5], 71), 0),
        "neighbour": draw_neighbour(jax.random.fold_in(splits[5], 71), 0),
        "boundary_faces": draw_boundary_faces(jax.random.fold_in(splits[5], 71), 0),
        "collision_rate": jnp.clip(jnp.exp(math.log(20.0) - 2.9957323 * jax.random.uniform(splits[4], (MESH_CELL_TOTAL,), jnp.float32) ** level_of(splits[4], (MESH_CELL_TOTAL,), ((0, 4),), -0.2, 0.2)), 1.0, 20.0),
    }


velocity_limit = 6.0
time_step = 0.012
viscous_conductive_ratio = 2.0 / 3.0
density_floor = 0.1
kelvin_lower_limit = 0.2
skew_multiplier_limit = 0.9
slope_floor = 0.01
highest = lax.Precision.HIGHEST

def monomial_integral(power_r, power_s):
    return math.factorial(power_r) * math.factorial(power_s) / math.factorial(power_r + power_s + 2)

def lower_factor(matrix):
    order = matrix.shape[0]
    factor = np.zeros((order, order))
    for row in range(order):
        for column in range(row + 1):
            total = matrix[row, column] - sum((factor[row, inner] * factor[column, inner] for inner in range(column)))
            if row == column:
                factor[row, column] = math.sqrt(total)
            else:
                factor[row, column] = total / factor[column, column]
    return factor

def plain_inverse(matrix):
    order = matrix.shape[0]
    work = np.concatenate([np.array(matrix) * 1.0, np.eye(order)], axis=1)
    for pivot_index in range(order):
        work[pivot_index] = work[pivot_index] / work[pivot_index, pivot_index]
        for other in range(order):
            if other != pivot_index:
                work[other] = work[other] - work[other, pivot_index] * work[pivot_index]
    return work[:, order:]

def dg_tables():
    powers = [(0, 0), (1, 0), (0, 1), (2, 0), (1, 1), (0, 2)]
    gram_matrix = np.array([[monomial_integral(left_pow[0] + right_pow[0], left_pow[1] + right_pow[1]) for right_pow in powers] for left_pow in powers])
    factor = lower_factor(gram_matrix)
    coeffs = plain_inverse(factor)
    deriv_r = np.zeros((6, 6))
    deriv_s = np.zeros((6, 6))
    for left_index, left_pow in enumerate(powers):
        for right_index, right_pow in enumerate(powers):
            if left_pow[0] > 0:
                deriv_r[left_index, right_index] = left_pow[0] * monomial_integral(left_pow[0] - 1 + right_pow[0], left_pow[1] + right_pow[1])
            if left_pow[1] > 0:
                deriv_s[left_index, right_index] = left_pow[1] * monomial_integral(left_pow[0] + right_pow[0], left_pow[1] - 1 + right_pow[1])
    stiff_r = coeffs @ deriv_r @ coeffs.T
    stiff_s = coeffs @ deriv_s @ coeffs.T

    def monomials(location):
        return np.array([location[0] ** exponent[0] * location[1] ** exponent[1] for exponent in powers])

    def evaluate(location):
        return coeffs @ monomials(location)
    vertices = np.array([[0.0, 0.0], [1.0, 0.0], [0.0, 1.0]])
    offset = math.sqrt(0.15)
    positions = [0.5 - offset, 0.5, 0.5 + offset]
    weights = np.array([5.0, 8.0, 5.0]) / 18.0
    traces = np.zeros((3, 3, 6))
    for face_index in range(3):
        for point_index in range(3):
            along = positions[point_index]
            location = (1.0 - along) * vertices[face_index] + along * vertices[(face_index + 1) % 3]
            traces[face_index, point_index] = evaluate(location)
    lifting = traces * weights[None, :, None]
    node_list = [(0.0, 0.0), (1.0, 0.0), (0.0, 1.0), (0.5, 0.0), (0.5, 0.5), (0.0, 0.5)]
    nodal = np.array([evaluate(np.array(location)) for location in node_list])
    vander = np.array([monomials(np.array(location)) for location in node_list])
    inverse = factor.T @ plain_inverse(vander)
    return tuple((jnp.asarray(matrix, dtype=jnp.float32) for matrix in (stiff_r, stiff_s, traces, lifting, nodal, inverse)))

def velocity_grid(first_index, vel_count):
    velocity_index = first_index + jnp.arange(vel_count, dtype=jnp.int32)
    spacing = 2.0 * velocity_limit / VGRID
    along_x = -velocity_limit + ((velocity_index // VGRID).astype(jnp.float32) + 0.5) * spacing
    along_y = -velocity_limit + ((velocity_index % VGRID).astype(jnp.float32) + 0.5) * spacing
    return (along_x, along_y, spacing)

def moment_weights(along_x, along_y, spacing):
    peculiar_norm_square = along_x * along_x + along_y * along_y
    all_ones = jnp.ones_like(along_x)
    stacked = jnp.stack([all_ones, along_x, along_y, along_x * along_x, along_x * along_y, along_y * along_y, along_x * peculiar_norm_square, along_y * peculiar_norm_square])
    return spacing * spacing * stacked

def shakhov_parameters(moments, rate_values, nodal):
    values = jnp.einsum('nj,kje->kne', nodal, moments, precision=highest)
    zeroth, mass_x, mass_y, flux_xx, flux_xy, flux_yy, third_x, third_y = [values[statistic_position] for statistic_position in range(8)]
    gas_concentration = jnp.maximum(zeroth, density_floor)
    bulk_drift_first = mass_x / gas_concentration
    bulk_drift_second = mass_y / gas_concentration
    drift_sq = bulk_drift_first * bulk_drift_first + bulk_drift_second * bulk_drift_second
    drift_mass = bulk_drift_first * mass_x + bulk_drift_second * mass_y
    flux_trace = flux_xx + flux_yy
    agitation_magnitude = flux_trace - 2.0 * drift_mass + drift_sq * zeroth
    pointwise_kelvin = jnp.maximum(agitation_magnitude / (2.0 * gas_concentration), kelvin_lower_limit)
    energy_current_first = 0.5 * (third_x - 2.0 * (flux_xx * bulk_drift_first + flux_xy * bulk_drift_second) + mass_x * drift_sq - bulk_drift_first * flux_trace + 2.0 * bulk_drift_first * drift_mass - bulk_drift_first * drift_sq * zeroth)
    energy_current_second = 0.5 * (third_y - 2.0 * (flux_xy * bulk_drift_first + flux_yy * bulk_drift_second) + mass_y * drift_sq - bulk_drift_second * flux_trace + 2.0 * bulk_drift_second * drift_mass - bulk_drift_second * drift_sq * zeroth)
    collision_inverse_period = rate_values[None, :] * gas_concentration
    return jnp.stack([gas_concentration, bulk_drift_first, bulk_drift_second, pointwise_kelvin, energy_current_first, energy_current_second, collision_inverse_period])

def collision(coefficients, kinetic_settings, along_x, along_y, nodal, inverse):
    values = jnp.einsum('nj,jev->nev', nodal, coefficients, precision=highest)
    gas_concentration, bulk_drift_first, bulk_drift_second, pointwise_kelvin, energy_current_first, energy_current_second, collision_inverse_period = [kinetic_settings[statistic_position][:, :, None] for statistic_position in range(7)]
    peculiar_motion_first = along_x - bulk_drift_first
    peculiar_motion_second = along_y - bulk_drift_second
    peculiar_norm_square = peculiar_motion_first * peculiar_motion_first + peculiar_motion_second * peculiar_motion_second
    equilibrium_distribution = gas_concentration / (2.0 * math.pi * pointwise_kelvin) * jnp.exp(-peculiar_norm_square / (2.0 * pointwise_kelvin))
    conductive_adjustment = jnp.clip((1.0 - viscous_conductive_ratio) * (peculiar_motion_first * energy_current_first + peculiar_motion_second * energy_current_second) * (peculiar_norm_square / pointwise_kelvin - 4.0) / (4.0 * gas_concentration * pointwise_kelvin * pointwise_kelvin), -skew_multiplier_limit, skew_multiplier_limit)
    return jnp.einsum('in,nev->iev', inverse, collision_inverse_period * (equilibrium_distribution * (1.0 + conductive_adjustment) - values), precision=highest)

def geometry(corners, along_x, along_y):
    corner_x = corners[0]
    corner_y = corners[1]
    edge_x = jnp.roll(corner_x, -1, axis=0) - corner_x
    edge_y = jnp.roll(corner_y, -1, axis=0) - corner_y
    jacobian = (corner_x[1] - corner_x[0]) * (corner_y[2] - corner_y[0]) - (corner_x[2] - corner_x[0]) * (corner_y[1] - corner_y[0])
    ref_r = ((corner_y[2] - corner_y[0])[:, None] * along_x - (corner_x[2] - corner_x[0])[:, None] * along_y) / jacobian[:, None]
    ref_s = ((corner_x[1] - corner_x[0])[:, None] * along_y - (corner_y[1] - corner_y[0])[:, None] * along_x) / jacobian[:, None]
    normal_flow = edge_y[:, :, None] * along_x - edge_x[:, :, None] * along_y
    return (ref_r, ref_s, normal_flow, jacobian)

def residual(coefficients, inside, outside, geometry_terms, kinetic_settings, along_x, along_y, tables):
    stiff_r, stiff_s, traces, lifting, nodal, inverse = tables
    ref_r, ref_s, normal_flow, jacobian = geometry_terms
    volume = ref_r * jnp.einsum('ij,jev->iev', stiff_r, coefficients, precision=highest) + ref_s * jnp.einsum('ij,jev->iev', stiff_s, coefficients, precision=highest)
    upwind = jnp.maximum(normal_flow, 0.0)[:, :, None, :] * inside + jnp.minimum(normal_flow, 0.0)[:, :, None, :] * outside
    surface = jnp.einsum('mqi,meqv->iev', lifting, upwind, precision=highest)
    return volume - surface / jacobian[:, None] + collision(coefficients, kinetic_settings, along_x, along_y, nodal, inverse)

def limiter(coefficients, beside_all, tables):
    traces = tables[2]
    centre = coefficients[0]
    mean_bound = math.sqrt(2.0) * lax.optimization_barrier(jnp.max(jnp.abs(beside_all - centre[None]), axis=0))
    linear = lax.optimization_barrier(jnp.max(jnp.abs(jnp.einsum('mqj,jev->mqev', traces[:, :, 1:3], coefficients[1:3], precision=highest)), axis=(0, 1)))
    quadric = lax.optimization_barrier(jnp.max(jnp.abs(jnp.einsum('mqj,jev->mqev', traces[:, :, 3:6], coefficients[3:6], precision=highest)), axis=(0, 1)))
    first_scale = jnp.minimum(1.0, mean_bound / jnp.maximum(linear, slope_floor))
    second_scale = jnp.minimum(first_scale, mean_bound / jnp.maximum(quadric, slope_floor))
    return jnp.concatenate([coefficients[0:1], coefficients[1:3] * first_scale[None], coefficients[3:6] * second_scale[None]], axis=0)

def reference(distribution, corners, neighbour, boundary_faces, collision_rate):
    tables = dg_tables()
    along_x, along_y, spacing = velocity_grid(0, VEL)
    weights = moment_weights(along_x, along_y, spacing)
    faces_dev = 3 * ELEM_DEV
    blank_slot = N_SPACE * faces_dev
    local_faces = neighbour.reshape(3, N_SPACE, ELEM_DEV).transpose(1, 0, 2).reshape(N_SPACE, faces_dev)
    offsets = (jnp.arange(N_SPACE, dtype=jnp.int32) * faces_dev)[:, None]
    face_source = jnp.where(local_faces >= 0, offsets + local_faces, blank_slot).reshape(-1)
    lower_list = boundary_faces[:, 0]
    upper_list = boundary_faces[:, 1]
    lower_target = jnp.where(lower_list[1:] >= 0, offsets[1:] + lower_list[1:], blank_slot)
    face_source = face_source.at[lower_target.reshape(-1)].set((offsets[:-1] + upper_list[:-1]).reshape(-1), mode='drop')
    upper_target = jnp.where(upper_list[:-1] >= 0, offsets[:-1] + upper_list[:-1], blank_slot)
    face_source = face_source.at[upper_target.reshape(-1)].set((offsets[1:] + lower_list[1:]).reshape(-1), mode='drop')
    element_source = face_source // faces_dev * ELEM_DEV + face_source % ELEM_DEV

    def split_blocks(field):
        return field.reshape(MODES, MESH_CELL_TOTAL, VGRID, VGRID).transpose(2, 0, 1, 3)

    def join_blocks(blocked):
        return blocked.transpose(1, 2, 0, 3).reshape(MODES, MESH_CELL_TOTAL, VEL)

    def advance(base, current, keep_weight):
        moments = jnp.einsum('kv,jev->kje', weights, current, precision=highest)
        kinetic_settings = shakhov_parameters(moments, collision_rate, tables[4])

        def advance_block(inputs):
            block_index, base_block, current_block = inputs
            block_x, block_y, unused_spacing = velocity_grid(block_index * VGRID, VGRID)
            geometry_terms = geometry(corners, block_x, block_y)
            inside = jnp.einsum('mqj,jev->meqv', tables[2], current_block, precision=highest)
            flat_traces = inside.reshape(3, N_SPACE, ELEM_DEV, QPTS, VGRID).transpose(1, 0, 2, 3, 4).reshape(N_SPACE * faces_dev, QPTS, VGRID)
            padded = jnp.concatenate([flat_traces, jnp.zeros((1, QPTS, VGRID), jnp.float32)], axis=0)
            outside = jnp.take(padded, face_source, axis=0)[:, ::-1, :]
            outside = outside.reshape(N_SPACE, 3, ELEM_DEV, QPTS, VGRID).transpose(1, 0, 2, 3, 4).reshape(3, MESH_CELL_TOTAL, QPTS, VGRID)
            change = residual(current_block, inside, outside, geometry_terms, kinetic_settings, block_x, block_y, tables)
            updated = keep_weight * base_block + (1.0 - keep_weight) * (current_block + time_step * change)
            centre = updated[0]
            mean_table = jnp.concatenate([centre, jnp.zeros((1, VGRID), jnp.float32)], axis=0)
            beside_all = jnp.take(mean_table, element_source, axis=0)
            beside_all = beside_all.reshape(N_SPACE, 3, ELEM_DEV, VGRID).transpose(1, 0, 2, 3).reshape(3, MESH_CELL_TOTAL, VGRID)
            return limiter(updated, beside_all, tables)
        block_ids = jnp.arange(VGRID, dtype=jnp.int32)
        return join_blocks(lax.map(advance_block, (block_ids, split_blocks(base), split_blocks(current))))
    section = advance(distribution, distribution, 0.0)
    return advance(distribution, section, 0.5)
```

```python
import math

import jax
import jax.numpy as jnp
import numpy as np
from jax import lax
from jax.experimental import pallas as pl
from jax.experimental.pallas import tpu as pltpu
from jax.sharding import PartitionSpec as P

VGRID = 64
velocity_limit = 6.0
time_step = 0.012
viscous_conductive_ratio = 2.0 / 3.0
density_floor = 0.1
kelvin_lower_limit = 0.2
skew_multiplier_limit = 0.9
slope_floor = 0.01

LANE = 128
SUB = 8
PITCH = 16
MODES = 6
TERMS = 32
f32 = jnp.float32
bf16 = jnp.bfloat16


def monomial_integral(power_r, power_s):
    return math.factorial(power_r) * math.factorial(power_s) / math.factorial(power_r + power_s + 2)


def dg_tables():
    powers = [(0, 0), (1, 0), (0, 1), (2, 0), (1, 1), (0, 2)]
    gram = np.array(
        [[monomial_integral(a[0] + b[0], a[1] + b[1]) for b in powers] for a in powers]
    )
    coeffs = np.linalg.inv(np.linalg.cholesky(gram))
    deriv_r = np.zeros((6, 6))
    deriv_s = np.zeros((6, 6))
    for i, a in enumerate(powers):
        for j, b in enumerate(powers):
            if a[0] > 0:
                deriv_r[i, j] = a[0] * monomial_integral(a[0] - 1 + b[0], a[1] + b[1])
            if a[1] > 0:
                deriv_s[i, j] = a[1] * monomial_integral(a[0] + b[0], a[1] - 1 + b[1])
    stiff_r = coeffs @ deriv_r @ coeffs.T
    stiff_s = coeffs @ deriv_s @ coeffs.T

    def evaluate(location):
        return coeffs @ np.array([location[0] ** p[0] * location[1] ** p[1] for p in powers])

    vertices = np.array([[0.0, 0.0], [1.0, 0.0], [0.0, 1.0]])
    offset = math.sqrt(0.15)
    positions = np.array([0.5 - offset, 0.5, 0.5 + offset])
    weights = np.array([5.0, 8.0, 5.0]) / 18.0
    traces = np.zeros((3, 3, 6))
    for m in range(3):
        for q in range(3):
            along = positions[q]
            traces[m, q] = evaluate((1.0 - along) * vertices[m] + along * vertices[(m + 1) % 3])
    legendre = np.stack(
        [
            np.ones(3),
            math.sqrt(3.0) * (2.0 * positions - 1.0),
            math.sqrt(5.0) * (6.0 * positions**2 - 6.0 * positions + 1.0),
        ]
    )
    edge = np.einsum("lq,q,mqj->mlj", legendre, weights, traces)
    node_list = [(0.0, 0.0), (1.0, 0.0), (0.0, 1.0), (0.5, 0.0), (0.5, 0.5), (0.0, 0.5)]
    nodal = np.array([evaluate(np.array(n)) for n in node_list])
    inverse = np.linalg.inv(nodal)
    return stiff_r, stiff_s, traces, edge, nodal, inverse


KR, KS, TR, EDGE, NODAL, INVERSE = dg_tables()


def k(value):
    return float(np.float32(value))


def edge_parts(z):
    z0, z1, z2, z3, z4, z5 = z
    b = EDGE[0]
    a0 = z0 * k(b[0, 0])
    even = (
        a0 + z1 * k(b[0, 1]) + z3 * k(b[0, 3]) + z5 * k(b[0, 5]),
        z1 * k(b[1, 1]) + z3 * k(b[1, 3]) + z5 * k(b[1, 5]),
        z3 * k(b[2, 3]) + z5 * k(b[2, 5]),
    )
    odd = (
        z2 * k(-b[0, 2]) + z4 * k(-b[0, 4]),
        z2 * k(-b[1, 2]) + z4 * k(-b[1, 4]),
        z4 * k(-b[2, 4]),
    )
    c = EDGE[2]
    last = (
        a0 + z1 * k(c[0, 1]) + z3 * k(c[0, 3]),
        z2 * k(c[1, 2]) + z4 * k(c[1, 4]),
        z5 * k(c[2, 5]),
    )
    return a0, even, odd, last


def table_values(z):
    _, even, odd, last = edge_parts(z)
    return (
        (even[0] - odd[0], odd[1] - even[1], even[2] - odd[2]),
        (even[0] + odd[0], even[1] + odd[1], even[2] + odd[2]),
        (last[0], -last[1], last[2]),
    )


def tile(ref, row, chunk):
    return ref[pl.ds(row, SUB), pl.ds(chunk * LANE, LANE)]


def put_table(tbl, z, row, elems, chunk):
    for m, values in enumerate(table_values(z)):
        for level, value in enumerate(values):
            start = (m * elems + row) * PITCH + level * 4 + chunk
            tbl[pl.ds(start, SUB, stride=PITCH), :] = value


def fetch_rows(tbl, stage, base, index_of, pitch):
    for i in range(SUB):
        start = pl.multiple_of(index_of(i) * pitch, pitch)
        stage[pl.ds(base + i * pitch, pitch), :] = tbl[pl.ds(start, pitch), :]


def pack_faces(tbl, stage, lists, outs, slots):
    chunks = outs[0].shape[2] // LANE
    for side, out in enumerate(outs):

        def body(g, _, side=side, out=out):
            row = pl.multiple_of(g * SUB, SUB)
            fetch_rows(tbl, stage, 0, lambda i: jnp.maximum(lists[side, row + i], 0), PITCH)
            for level in range(3):
                for c in range(chunks):
                    out[level, pl.ds(row, SUB), pl.ds(c * LANE, LANE)] = stage[
                        pl.ds(level * 4 + c, SUB, stride=PITCH), :
                    ]
            return 0

        lax.fori_loop(0, slots // SUB, body, 0)


def grid_rows(first, shape):
    index = first + lax.broadcasted_iota(jnp.int32, shape, len(shape) - 1)
    spacing = 2.0 * velocity_limit / VGRID
    x = -velocity_limit + ((index // VGRID).astype(f32) + 0.5) * spacing
    y = -velocity_limit + ((index % VGRID).astype(f32) + 0.5) * spacing
    return x, y, spacing


def split3(value):
    high = value.astype(bf16).astype(f32)
    rest = value - high
    middle = rest.astype(bf16).astype(f32)
    return high, middle, (rest - middle).astype(bf16).astype(f32)


def put_moments(first, read_mode, out):
    vel = read_mode(0).shape[1]
    x, y, spacing = grid_rows(first, (SUB, vel))
    row = lax.broadcasted_iota(jnp.int32, (SUB, vel), 0)
    square = x * x + y * y
    weights = jnp.ones_like(x)
    for index, value in enumerate((x, y, x * x, x * y, y * y, x * square, y * square)):
        weights = jnp.where(row == index + 1, value, weights)
    weights = weights * (spacing * spacing)
    parts = split3(weights)
    stacked = jnp.concatenate([*parts, jnp.zeros_like(x)], axis=0).astype(bf16)
    for j in range(MODES):
        value = read_mode(j)
        high = value.astype(bf16)
        low = (value - high.astype(f32)).astype(bf16)
        dims = (((1,), (1,)), ((), ()))
        total = lax.dot_general(stacked, high, dims, preferred_element_type=f32)
        total = total + lax.dot_general(stacked, low, dims, preferred_element_type=f32)
        out[pl.ds(j * SUB, SUB), :] = total[0:8] + total[8:16] + total[16:24]


def open_kernel(lists, first, z_ref, neigh_ref, mom, low, up, src, tbl, stage):
    elems = z_ref.shape[1]
    chunks = z_ref.shape[2] // LANE
    slots = lists.shape[1]
    faces = 3 * elems

    def fill(g, _):
        row = pl.multiple_of(g * SUB, SUB)
        for c in range(chunks):
            z = [z_ref[j, pl.ds(row, SUB), pl.ds(c * LANE, LANE)] for j in range(MODES)]
            put_table(tbl, z, row, elems, c)
        return 0

    lax.fori_loop(0, elems // SUB, fill, 0)
    pack_faces(tbl, stage, lists, (low, up), slots)
    put_moments(first[0], lambda j: z_ref[j], mom)

    shape = neigh_ref.shape
    face = lax.broadcasted_iota(jnp.int32, shape, 0) * elems + lax.broadcasted_iota(jnp.int32, shape, 1)

    def mark(slot, found):
        found = jnp.where(face == lists[0, slot], faces + slot, found)
        return jnp.where(face == lists[1, slot], faces + slots + slot, found)

    src[...] = lax.fori_loop(0, slots, mark, neigh_ref[...])


def node_parameters(mom, rate, elems):
    shape = (SUB, elems)
    row = lax.broadcasted_iota(jnp.int32, shape, 0)

    def column(values):
        out = jnp.full(shape, k(values[0]), f32)
        for n in range(1, MODES):
            out = jnp.where(row == n, k(values[n]), out)
        return out

    columns = [column(NODAL[:, j]) for j in range(MODES)]
    R = []
    for index in range(8):
        total = columns[0] * mom[index : index + 1, :]
        for j in range(1, MODES):
            total = total + columns[j] * mom[j * SUB + index : j * SUB + index + 1, :]
        R.append(total)
    zeroth, mass_x, mass_y, flux_xx, flux_xy, flux_yy, third_x, third_y = R
    density = jnp.maximum(zeroth, density_floor)
    ux = mass_x / density
    uy = mass_y / density
    drift_sq = ux * ux + uy * uy
    drift_mass = ux * mass_x + uy * mass_y
    trace = flux_xx + flux_yy
    kelvin = jnp.maximum(
        (trace - 2.0 * drift_mass + drift_sq * zeroth) / (2.0 * density), kelvin_lower_limit
    )
    qx = 0.5 * (
        third_x
        - 2.0 * (flux_xx * ux + flux_xy * uy)
        + mass_x * drift_sq
        - ux * trace
        + 2.0 * ux * drift_mass
        - ux * drift_sq * zeroth
    )
    qy = 0.5 * (
        third_y
        - 2.0 * (flux_xy * ux + flux_yy * uy)
        + mass_y * drift_sq
        - uy * trace
        + 2.0 * uy * drift_mass
        - uy * drift_sq * zeroth
    )
    nu = time_step * rate * density
    over = 1.0 / kelvin
    weight = (1.0 - viscous_conductive_ratio) / (4.0 * density * kelvin * kelvin)
    qx = qx * weight
    qy = qy * weight
    excess = (over * drift_sq - 4.0, -2.0 * over * ux, -2.0 * over * uy, over, over)
    amplitude = jnp.log(nu * density * over * k(1.0 / (2.0 * math.pi)))
    exponent = (
        amplitude - 0.5 * over * drift_sq,
        over * ux,
        over * uy,
        -0.5 * over,
        -0.5 * over,
    )
    skew = (-(qx * ux + qy * uy), qx, qy)
    return nu, excess, exponent, skew, row


def put_basis(first, basis, vel):
    rows = TERMS * SUB
    x, y, _ = grid_rows(first, (1, vel))
    xx = x * x
    yy = y * y
    xx_high = xx.astype(bf16).astype(f32)
    yy_high = yy.astype(bf16).astype(f32)
    monomials = (jnp.ones_like(x), x, y, xx_high, xx - xx_high, yy_high, yy - yy_high)
    row = lax.broadcasted_iota(jnp.int32, (SUB, vel), 0)
    zero = jnp.zeros((2 * SUB, vel), bf16)
    for n in range(SUB):
        mine = row == n
        for pair in range(rows // (2 * SUB)):
            halves = []
            for term in (2 * pair, 2 * pair + 1):
                which = term // 3
                halves.append(
                    jnp.where(mine, monomials[which], 0.0)
                    if which < len(monomials)
                    else jnp.zeros((SUB, vel), f32)
                )
            value = jnp.concatenate(halves, axis=0).astype(bf16) if 2 * pair // 3 < 7 else zero
            basis[pl.ds(pair * 2 * SUB, 2 * SUB), pl.ds(n * vel, vel)] = value


def spread(form, elems):
    pieces = []
    for index, value in enumerate(form):
        parts = split3(value)
        pieces += parts
        if index >= 3:
            pieces += parts
    pieces.append(jnp.zeros((TERMS * SUB - SUB * len(pieces), elems), f32))
    return jnp.concatenate(pieces, axis=0).T.astype(bf16)


def update_kernel(src, lists, first, *refs, section):
    if section == 0:
        z_ref, low, up, m0, m1, m2, m3, rate, corner, out, mlow, mup = refs[:12]
        base_ref = None
        scratch = refs[12:]
    else:
        base_ref, z_ref, low, up, m0, m1, m2, m3, rate, corner, out, mlow, mup = refs[:13]
        scratch = refs[13:]
    tbl, stage, mtbl, basis, qn, qa, ql, nus = scratch
    elems, vel = z_ref.shape[1:]
    chunks = vel // LANE
    slots = lists.shape[1]
    faces = 3 * elems

    def fill(g, _):
        row = pl.multiple_of(g * SUB, SUB)
        for c in range(chunks):
            z = [z_ref[j, pl.ds(row, SUB), pl.ds(c * LANE, LANE)] for j in range(MODES)]
            put_table(tbl, z, row, elems, c)
        return 0

    lax.fori_loop(0, elems // SUB, fill, 0)

    def fill_border(g, _):
        row = pl.multiple_of(g * SUB, SUB)
        for side, halo in enumerate((low, up)):
            for level in range(3):
                for c in range(chunks):
                    start = (faces + side * slots + row) * PITCH + level * 4 + c
                    tbl[pl.ds(start, SUB, stride=PITCH), :] = halo[
                        level, pl.ds(row, SUB), pl.ds(c * LANE, LANE)
                    ]
        return 0

    lax.fori_loop(0, slots // SUB, fill_border, 0)

    put_basis(first[0], basis, vel)
    moments = (m0[...] + m1[...]) + (m2[...] + m3[...])
    nu, excess, exponent, skew, row8 = node_parameters(moments, rate[...], elems)
    cx = [corner[i : i + 1, :] for i in range(3)]
    cy = [corner[3 + i : 4 + i, :] for i in range(3)]
    det = (cx[1] - cx[0]) * (cy[2] - cy[0]) - (cx[2] - cx[0]) * (cy[1] - cy[0])
    step = time_step / det
    flow0 = (-step * (cy[1] - cy[0]), step * (cx[1] - cx[0]))
    flow2 = (-step * (cy[0] - cy[2]), step * (cx[0] - cx[2]))
    linear = [
        jnp.where(row8 == 6, f0, jnp.where(row8 == 7, f2, s))
        for f0, f2, s in zip((0.0, *flow0), (0.0, *flow2), skew)
    ]
    for form, target in ((excess, qn), (exponent, qa), (linear, ql)):
        target[...] = jnp.dot(
            spread(form, elems), basis[:, pl.ds(0, target.shape[1])], preferred_element_type=f32
        )
    nus[...] = jnp.concatenate([nu, jnp.zeros((LANE - SUB, elems), f32)], axis=0).T

    B0, B2, V = EDGE[0], EDGE[2], INVERSE

    def group(g, _):
        row = pl.multiple_of(g * SUB, SUB)
        for m in range(3):
            fetch_rows(tbl, stage, m * SUB * PITCH, lambda i: src[m, row + i], PITCH)
        nu_cols = [jnp.broadcast_to(nus[pl.ds(row, SUB), n : n + 1], (SUB, LANE)) for n in range(MODES)]
        for c in range(chunks):
            lanes = pl.ds(c * LANE, LANE)
            z = [z_ref[j, pl.ds(row, SUB), lanes] for j in range(MODES)]
            z0, z1, z2, z3, z4, z5 = z

            def beside(m, level):
                return stage[pl.ds(m * SUB * PITCH + level * 4 + c, SUB, stride=PITCH), :]

            def form(ref, n):
                return ref[pl.ds(row, SUB), pl.ds(n * vel + c * LANE, LANE)]

            a0, even, odd, last = edge_parts(z)
            gs = form(ql, 6)
            gr = form(ql, 7)
            g1 = -(gs + gr)
            out0 = gs < 0.0
            out1 = g1 < 0.0
            out2 = gr < 0.0
            V0 = [gs * jnp.where(out0, even[i] - odd[i], beside(0, i)) for i in range(3)]
            W0 = [
                g1 * jnp.where(out1, even[0] + odd[0], beside(1, 0)),
                g1 * jnp.where(out1, even[1] + odd[1], -beside(1, 1)),
                g1 * jnp.where(out1, even[2] + odd[2], beside(1, 2)),
            ]
            X = [gr * jnp.where(out2, last[i], beside(2, i)) for i in range(3)]
            S = [a + b for a, b in zip(V0, W0)]
            D = [b - a for a, b in zip(V0, W0)]

            h = gr + 2.0 * gs
            vol1 = (gr * z0) * k(KR[1, 0])
            vol2 = (h * z0) * k(KR[2, 0])
            vol3 = gr * (z0 * k(KR[3, 0]) + z1 * k(KR[3, 1]))
            vol4 = h * (z0 * k(KR[4, 0]) + z1 * k(KR[4, 1])) + gr * (z2 * k(KR[4, 2]))
            vol5 = gr * (z0 * k(KR[5, 0]) + z1 * k(KR[5, 1])) + h * (z2 * k(KR[5, 2]))

            N = NODAL
            e02 = last[0] + z5 * k(N[0, 5])
            o02 = z2 * k(N[2, 2]) + z4 * k(N[2, 4])
            e34 = a0 + z1 * k(N[3, 1]) + z3 * k(N[3, 3]) + z5 * k(N[3, 5])
            o34 = z2 * k(N[4, 2]) + z4 * k(N[4, 4])
            F = [
                e02 - o02,
                a0 + z1 * k(N[1, 1]) + z3 * k(N[1, 3]),
                e02 + o02,
                e34 - o34,
                e34 + o34,
                last[0] + z5 * k(N[5, 5]),
            ]
            H = []
            for n in range(MODES):
                skewed = jnp.minimum(
                    jnp.maximum(form(ql, n) * form(qn, n), -skew_multiplier_limit), skew_multiplier_limit
                )
                H.append(jnp.exp(form(qa, n)) * (1.0 + skewed) - nu_cols[n] * F[n])
            s02 = H[0] + H[2]
            d20 = H[2] - H[0]
            s34 = H[3] + H[4]
            d43 = H[4] - H[3]
            col0 = (s34 + H[5]) * k(V[0, 3])
            col1 = s02 * k(V[1, 0]) + H[1] * k(V[1, 1]) + s34 * k(V[1, 3]) + H[5] * k(V[1, 5])
            col2 = d20 * k(V[2, 2]) + d43 * k(V[2, 4])
            col3 = (s02 + H[5]) * k(V[3, 0]) + (H[1] - s34) * k(V[3, 1])
            col4 = d20 * k(V[4, 2]) + d43 * k(V[4, 4])
            col5 = s02 * k(V[5, 0]) + H[5] * k(V[5, 5])

            new = [
                z0 + (S[0] + X[0]) * k(B0[0, 0]) + col0,
                z1 + S[0] * k(B0[0, 1]) + S[1] * k(B0[1, 1]) + X[0] * k(B2[0, 1]) + vol1 + col1,
                z2 + D[0] * k(-B0[0, 2]) + D[1] * k(-B0[1, 2]) + X[1] * k(B2[1, 2]) + vol2 + col2,
                z3
                + S[0] * k(B0[0, 3])
                + S[1] * k(B0[1, 3])
                + S[2] * k(B0[2, 3])
                + X[0] * k(B2[0, 3])
                + vol3
                + col3,
                z4
                + D[0] * k(-B0[0, 4])
                + D[1] * k(-B0[1, 4])
                + D[2] * k(-B0[2, 4])
                + X[1] * k(B2[1, 4])
                + vol4
                + col4,
                z5
                + S[0] * k(B0[0, 5])
                + S[1] * k(B0[1, 5])
                + S[2] * k(B0[2, 5])
                + X[2] * k(B2[2, 5])
                + vol5
                + col5,
            ]
            for j in range(MODES):
                value = new[j]
                if section == 1:
                    value = 0.5 * (base_ref[j, pl.ds(row, SUB), lanes] + value)
                out[j, pl.ds(row, SUB), lanes] = value
                if j == 0:
                    mtbl[pl.ds(row * SUB + c, SUB, stride=SUB), :] = value
        return 0

    lax.fori_loop(0, elems // SUB, group, 0)

    for side, target in enumerate((mlow, mup)):

        def pack(g, _, side=side, target=target):
            row = pl.multiple_of(g * SUB, SUB)
            fetch_rows(
                mtbl, stage, 0, lambda i: jnp.maximum(lists[side, row + i], 0) % elems, SUB
            )
            for c in range(chunks):
                target[pl.ds(row, SUB), pl.ds(c * LANE, LANE)] = stage[pl.ds(c, SUB, stride=SUB), :]
            return 0

        lax.fori_loop(0, slots // SUB, pack, 0)


def limit_kernel(src, lists, first, z_ref, mlow, mup, out, *refs, section):
    if section == 0:
        mom, low, up, mtbl, stage, tbl = refs
    else:
        mtbl, stage = refs
    elems, vel = z_ref.shape[1:]
    chunks = vel // LANE
    slots = lists.shape[1]
    faces = 3 * elems

    def fill(g, _):
        row = pl.multiple_of(g * SUB, SUB)
        for c in range(chunks):
            mtbl[pl.ds(row * SUB + c, SUB, stride=SUB), :] = z_ref[
                0, pl.ds(row, SUB), pl.ds(c * LANE, LANE)
            ]
        return 0

    lax.fori_loop(0, elems // SUB, fill, 0)

    def fill_border(g, _):
        row = pl.multiple_of(g * SUB, SUB)
        for side, halo in enumerate((mlow, mup)):
            for c in range(chunks):
                start = (elems + side * slots + row) * SUB + c
                mtbl[pl.ds(start, SUB, stride=SUB), :] = tile(halo, row, c)
        return 0

    lax.fori_loop(0, slots // SUB, fill_border, 0)

    def source(value):
        return jnp.where(value < faces, value % elems, value - 2 * elems)

    def group(g, _):
        row = pl.multiple_of(g * SUB, SUB)
        for m in range(3):
            fetch_rows(mtbl, stage, m * SUB * SUB, lambda i: source(src[m, row + i]), SUB)
        for c in range(chunks):
            lanes = pl.ds(c * LANE, LANE)
            z = [z_ref[j, pl.ds(row, SUB), lanes] for j in range(MODES)]
            gaps = [
                jnp.abs(stage[pl.ds(m * SUB * SUB + c, SUB, stride=SUB), :] - z[0]) for m in range(3)
            ]
            bound = k(math.sqrt(2.0)) * jnp.maximum(jnp.maximum(gaps[0], gaps[1]), gaps[2])
            size1 = jnp.abs(z[1])
            size2 = jnp.abs(z[2])
            size4 = jnp.abs(z[4])
            linear = None
            quadric = None
            for m, q in ((0, 0), (0, 1), (0, 2), (2, 0), (2, 1)):
                t = TR[m, q]
                if q != 1:
                    value = size1 * k(abs(t[1])) + size2 * k(abs(t[2]))
                    linear = value if linear is None else jnp.maximum(linear, value)
                value = jnp.abs(z[3] * k(t[3]) + z[5] * k(t[5]))
                if abs(t[4]) > 1e-9:
                    value = value + size4 * k(abs(t[4]))
                quadric = value if quadric is None else jnp.maximum(quadric, value)
            theta1 = jnp.minimum(1.0, bound / jnp.maximum(linear, slope_floor))
            theta2 = jnp.minimum(theta1, bound / jnp.maximum(quadric, slope_floor))
            z = [z[0], z[1] * theta1, z[2] * theta1, z[3] * theta2, z[4] * theta2, z[5] * theta2]
            for j in range(MODES):
                out[j, pl.ds(row, SUB), lanes] = z[j]
            if section == 0:
                put_table(tbl, z, row, elems, c)
        return 0

    lax.fori_loop(0, elems // SUB, group, 0)
    if section == 0:
        pack_faces(tbl, stage, lists, (low, up), slots)
        put_moments(first[0], lambda j: out[j], mom)


def passed_along(value, axis, by):
    peers = lax.axis_size(axis)
    pairs = [(i, i + by) for i in range(peers) if 0 <= i + by < peers]
    return lax.ppermute(value, axis, pairs)


def swapped(value, bits):
    peers = lax.axis_size("vel")
    return lax.ppermute(value, "vel", [(i, i ^ bits) for i in range(peers)])


def moment_parts(partial):
    paired = partial + swapped(partial, 1)
    return [paired, swapped(paired, 2), swapped(paired, 4), swapped(paired, 6)]


def on_device(distribution, corners, neighbour, boundary_faces, collision_rate):
    modes, elems, vel = distribution.shape
    slots = boundary_faces.shape[2]
    lists = boundary_faces[0]
    first = (lax.axis_index("vel") * vel).astype(jnp.int32).reshape(1)
    rows = 3 * elems + 2 * slots
    S = jax.ShapeDtypeStruct
    state = S((modes, elems, vel), f32)
    halo = S((3, slots, vel), f32)
    means = S((slots, vel), f32)
    mom = S((modes * SUB, elems), f32)
    smem = pl.BlockSpec(memory_space=pltpu.SMEM)
    vmem = pl.BlockSpec(memory_space=pltpu.VMEM)
    params = pltpu.CompilerParams(vmem_limit_bytes=58 << 20)

    def table(count, pitch):
        return pltpu.VMEM((count * pitch, LANE), f32)

    stage = pltpu.VMEM((3 * SUB * PITCH, LANE), f32)

    mom1, low1, up1, src = pl.pallas_call(
        open_kernel,
        out_shape=(mom, halo, halo, S(neighbour.shape, jnp.int32)),
        in_specs=[smem, smem, vmem, vmem],
        out_specs=(vmem,) * 4,
        scratch_shapes=[table(3 * elems, PITCH), stage],
        compiler_params=params,
        name="open",
    )(lists, first, distribution, neighbour)

    rate = collision_rate.reshape(1, elems)
    flat_corners = corners.reshape(6, elems)

    def update(section, current, low, up, partial):
        from_lower = passed_along(up, "space", 1)
        from_upper = passed_along(low, "space", -1)
        arrays = [distribution] if section else []
        arrays += [current, from_lower, from_upper, *moment_parts(partial), rate, flat_corners]
        out, mlow, mup = pl.pallas_call(
            lambda *refs: update_kernel(*refs, section=section),
            out_shape=(state, means, means),
            in_specs=[smem, smem, smem] + [vmem] * len(arrays),
            out_specs=(vmem,) * 3,
            scratch_shapes=[
                table(rows, PITCH),
                stage,
                table(elems, SUB),
                pltpu.VMEM((TERMS * SUB, SUB * vel), bf16),
                pltpu.VMEM((elems, MODES * vel), f32),
                pltpu.VMEM((elems, MODES * vel), f32),
                pltpu.VMEM((elems, SUB * vel), f32),
                pltpu.VMEM((elems, LANE), f32),
            ],
            compiler_params=params,
            name=f"update{section}",
        )(src, lists, first, *arrays)
        return out, passed_along(mup, "space", 1), passed_along(mlow, "space", -1)

    def limit(section, updated, from_lower, from_upper):
        shapes = (state, mom, halo, halo) if section == 0 else (state,)
        scratch = [table(elems + 2 * slots, SUB), stage]
        if section == 0:
            scratch.append(table(3 * elems, PITCH))
        return pl.pallas_call(
            lambda *refs: limit_kernel(*refs, section=section),
            out_shape=shapes,
            in_specs=[smem, smem, smem] + [vmem] * 3,
            out_specs=(vmem,) * len(shapes),
            scratch_shapes=scratch,
            compiler_params=params,
            name=f"limit{section}",
        )(src, lists, first, updated, from_lower, from_upper)

    section, mom2, low2, up2 = limit(0, *update(0, distribution, low1, up1, mom1))
    (advanced,) = limit(1, *update(1, section, low2, up2, mom2))
    return advanced


def solution(mesh):
    in_specs = (
        P(None, "space", "vel"),
        P(None, None, "space"),
        P(None, "space"),
        P("space", None, None),
        P("space"),
    )
    return jax.shard_map(
        on_device, mesh=mesh, in_specs=in_specs, out_specs=P(None, "space", "vel"), check_vma=False
    )
```

```python
import math

import jax
import jax.numpy as jnp
import numpy as np
from jax import lax
from jax.experimental import pallas as pl
from jax.experimental.pallas import tpu as pltpu
from jax.sharding import PartitionSpec as P

VGRID = 64
velocity_limit = 6.0
time_step = 0.012
viscous_conductive_ratio = 2.0 / 3.0
density_floor = 0.1
kelvin_lower_limit = 0.2
skew_multiplier_limit = 0.9
slope_floor = 0.01

LANE = 128
SUB = 8
MODES = 6
TERMS = 32
f32 = jnp.float32
bf16 = jnp.bfloat16


def monomial_integral(power_r, power_s):
    return math.factorial(power_r) * math.factorial(power_s) / math.factorial(power_r + power_s + 2)


def dg_tables():
    powers = [(0, 0), (1, 0), (0, 1), (2, 0), (1, 1), (0, 2)]
    gram = np.array(
        [[monomial_integral(a[0] + b[0], a[1] + b[1]) for b in powers] for a in powers]
    )
    coeffs = np.linalg.inv(np.linalg.cholesky(gram))
    deriv_r = np.zeros((6, 6))
    deriv_s = np.zeros((6, 6))
    for i, a in enumerate(powers):
        for j, b in enumerate(powers):
            if a[0] > 0:
                deriv_r[i, j] = a[0] * monomial_integral(a[0] - 1 + b[0], a[1] + b[1])
            if a[1] > 0:
                deriv_s[i, j] = a[1] * monomial_integral(a[0] + b[0], a[1] - 1 + b[1])
    stiff_r = coeffs @ deriv_r @ coeffs.T
    stiff_s = coeffs @ deriv_s @ coeffs.T

    def evaluate(location):
        return coeffs @ np.array([location[0] ** p[0] * location[1] ** p[1] for p in powers])

    vertices = np.array([[0.0, 0.0], [1.0, 0.0], [0.0, 1.0]])
    offset = math.sqrt(0.15)
    positions = np.array([0.5 - offset, 0.5, 0.5 + offset])
    weights = np.array([5.0, 8.0, 5.0]) / 18.0
    traces = np.zeros((3, 3, 6))
    for m in range(3):
        for q in range(3):
            along = positions[q]
            traces[m, q] = evaluate((1.0 - along) * vertices[m] + along * vertices[(m + 1) % 3])
    legendre = np.stack(
        [
            np.ones(3),
            math.sqrt(3.0) * (2.0 * positions - 1.0),
            math.sqrt(5.0) * (6.0 * positions**2 - 6.0 * positions + 1.0),
        ]
    )
    edge = np.einsum("lq,q,mqj->mlj", legendre, weights, traces)
    node_list = [(0.0, 0.0), (1.0, 0.0), (0.0, 1.0), (0.5, 0.0), (0.5, 0.5), (0.0, 0.5)]
    nodal = np.array([evaluate(np.array(n)) for n in node_list])
    inverse = np.linalg.inv(nodal)
    return stiff_r, stiff_s, traces, edge, nodal, inverse


KR, KS, TR, EDGE, NODAL, INVERSE = dg_tables()


def k(value):
    return float(np.float32(value))


def edge_parts(z):
    z0, z1, z2, z3, z4, z5 = z
    b = EDGE[0]
    a0 = z0 * k(b[0, 0])
    even = (
        a0 + z1 * k(b[0, 1]) + z3 * k(b[0, 3]) + z5 * k(b[0, 5]),
        z1 * k(b[1, 1]) + z3 * k(b[1, 3]) + z5 * k(b[1, 5]),
        z3 * k(b[2, 3]) + z5 * k(b[2, 5]),
    )
    odd = (
        z2 * k(-b[0, 2]) + z4 * k(-b[0, 4]),
        z2 * k(-b[1, 2]) + z4 * k(-b[1, 4]),
        z4 * k(-b[2, 4]),
    )
    c = EDGE[2]
    last = (
        a0 + z1 * k(c[0, 1]) + z3 * k(c[0, 3]),
        z2 * k(c[1, 2]) + z4 * k(c[1, 4]),
        z5 * k(c[2, 5]),
    )
    return even, odd, last


def level0(z):
    z0, z1, z2, z3, z4, z5 = z
    b, c = EDGE[0], EDGE[2]
    a0 = z0 * k(b[0, 0])
    even = a0 + z1 * k(b[0, 1]) + z3 * k(b[0, 3]) + z5 * k(b[0, 5])
    odd = z2 * k(-b[0, 2]) + z4 * k(-b[0, 4])
    return even - odd, even + odd, a0 + z1 * k(c[0, 1]) + z3 * k(c[0, 3])


def table_values(z):
    even, odd, last = edge_parts(z)
    return (
        (even[0] - odd[0], odd[1] - even[1], even[2] - odd[2]),
        (even[0] + odd[0], even[1] + odd[1], even[2] + odd[2]),
        (last[0], -last[1], last[2]),
    )


def at(row, chunk):
    return pl.ds(row, SUB), pl.ds(chunk * LANE, LANE)


def modes_at(ref, row, chunk):
    return [ref[(j, *at(row, chunk))] for j in range(ref.shape[0])]


def over_groups(count, body):
    def step(g, _):
        body(pl.multiple_of(g * SUB, SUB))
        return 0

    lax.fori_loop(0, count // SUB, step, 0)


def copy_rows(source, target, start, to, count):
    for piece in range(0, count, SUB):
        rows = min(SUB, count - piece)
        target[pl.ds(to + piece, rows), :] = source[pl.ds(start + piece, rows), :]


def pipelined_groups(count, stages, fetch, compute):
    last = count - SUB
    fetch(0, stages[0])

    def step(pair, _):
        row = pl.multiple_of(pair * (2 * SUB), 2 * SUB)
        after = pl.multiple_of(row + SUB, SUB)
        fetch(after, stages[1])
        compute(row, stages[0])
        fetch(pl.multiple_of(jnp.minimum(row + 2 * SUB, last), SUB), stages[0])
        compute(after, stages[1])
        return 0

    lax.fori_loop(0, count // (2 * SUB), step, 0)


def grid_rows(first, shape):
    index = first + lax.broadcasted_iota(jnp.int32, shape, len(shape) - 1)
    spacing = 2.0 * velocity_limit / VGRID
    x = -velocity_limit + ((index // VGRID).astype(f32) + 0.5) * spacing
    y = -velocity_limit + ((index % VGRID).astype(f32) + 0.5) * spacing
    return x, y, spacing


def split3(value):
    high = value.astype(bf16).astype(f32)
    rest = value - high
    middle = rest.astype(bf16).astype(f32)
    return high, middle, (rest - middle).astype(bf16).astype(f32)


def weight_rows(first, vel):
    x, y, spacing = grid_rows(first, (SUB, vel))
    row = lax.broadcasted_iota(jnp.int32, (SUB, vel), 0)
    square = x * x + y * y
    weights = jnp.ones_like(x)
    for index, value in enumerate((x, y, x * x, x * y, y * y, x * square, y * square)):
        weights = jnp.where(row == index + 1, value, weights)
    weights = weights * (spacing * spacing)
    return jnp.concatenate([*split3(weights), jnp.zeros_like(x)], axis=0).astype(bf16)


def mode_moments(weights, value):
    high = value.astype(bf16)
    low = (value - high.astype(f32)).astype(bf16)
    dims = (((1,), (1,)), ((), ()))
    total = lax.dot_general(weights, high, dims, preferred_element_type=f32)
    total = total + lax.dot_general(weights, low, dims, preferred_element_type=f32)
    return total[0:8] + total[8:16] + total[16:24]


def first_kernel(info, z_ref, mom):
    weights = weight_rows(info[0], z_ref.shape[2])
    for j in range(MODES):
        mom[pl.ds(j * SUB, SUB), :] = mode_moments(weights, z_ref[j])


def put_index(neigh_ref, rows_ref, lists, src, away, offsets, elems, chunks):
    slots = rows_ref.shape[1]
    faces = 3 * elems
    shape = neigh_ref.shape
    face = lax.broadcasted_iota(jnp.int32, shape, 0) * elems + lax.broadcasted_iota(jnp.int32, shape, 1)

    def mark(slot, found):
        found = jnp.where(face == lists[0, slot], faces + slot, found)
        return jnp.where(face == lists[1, slot], faces + slots + slot, found)

    found = jnp.maximum(lax.fori_loop(0, slots, mark, neigh_ref[...]), 0)
    src[...] = found * chunks
    away[...] = jnp.where(found < faces, found % elems, found - 2 * elems) * chunks
    known = jnp.maximum(rows_ref[...], 0)
    offsets[pl.ds(0, 2), :] = known * chunks
    offsets[pl.ds(2, 2), :] = known % elems * chunks


def put_flows(corner, cols):
    cx = [corner[i, 0:1, :] for i in range(3)]
    cy = [corner[i, 1:2, :] for i in range(3)]
    det = (cx[1] - cx[0]) * (cy[2] - cy[0]) - (cx[2] - cx[0]) * (cy[1] - cy[0])
    step = time_step / det
    rows = [-step * (cy[1] - cy[0]), step * (cx[1] - cx[0]), -step * (cy[0] - cy[2]), step * (cx[0] - cx[2])]
    cols[...] = jnp.concatenate([*rows, jnp.zeros((LANE - 4, cols.shape[0]), f32)], axis=0).T


def sides(info):
    parity = info[1]
    return (1 - parity, parity)


def prepare_kernel(lists, info, neigh_ref, rows_ref, corner, src, away, offsets, basis, cols):
    vel = basis.shape[1] // MODES
    put_index(neigh_ref, rows_ref, lists, src, away, offsets, cols.shape[0], vel // LANE)
    put_flows(corner, cols)
    put_basis(info[0], basis, vel)


def trace_kernel(offsets, info, z_ref, tbl0, tbl12, near, far, stage0, stage12):
    elems, vel = z_ref.shape[1:]
    chunks = vel // LANE
    slots = offsets.shape[1]

    def fill(row):
        for c in range(chunks):
            for m, values in enumerate(table_values(modes_at(z_ref, row, c))):
                start = (m * elems + row) * chunks + c
                tbl0[pl.ds(start, SUB, stride=chunks), :] = values[0]
                for level in (1, 2):
                    start = ((m * elems + row) * 2 + level - 1) * chunks + c
                    tbl12[pl.ds(start, SUB, stride=2 * chunks), :] = values[level]

    over_groups(elems, fill)

    def take(row):
        for place, side in enumerate(sides(info)):
            for i in range(SUB):
                start = offsets[side, row + i]
                to = (place * slots + row + i) * chunks
                copy_rows(tbl0, stage0, start, to, chunks)
                copy_rows(tbl12, stage12, 2 * start, 2 * to, 2 * chunks)

    over_groups(slots, take)

    def pack(row):
        for place, out in enumerate((near, far)):
            for c in range(chunks):
                start = (place * slots + row) * chunks
                out[(0, *at(row, c))] = stage0[pl.ds(start + c, SUB, stride=chunks), :]
                for level in range(2):
                    out[(level + 1, *at(row, c))] = stage12[
                        pl.ds(2 * start + level * chunks + c, SUB, stride=2 * chunks), :
                    ]

    over_groups(slots, pack)


def flow_forms(cols, grid, row):
    col = [jnp.broadcast_to(cols[pl.ds(row, SUB), n : n + 1], (SUB, LANE)) for n in range(4)]
    flows = []
    for x, y in grid:
        g0 = col[0] * x + col[1] * y
        g2 = col[2] * x + col[3] * y
        flows.append((g0, -(g0 + g2), g2))
    return flows


def chunk_grid(first, chunks):
    return [grid_rows(first + c * LANE, (1, LANE))[:2] for c in range(chunks)]


def put_basis(first, basis, vel):
    x, y, _ = grid_rows(first, (1, vel))
    xx = x * x
    yy = y * y
    xx_high = xx.astype(bf16).astype(f32)
    yy_high = yy.astype(bf16).astype(f32)
    monomials = (jnp.ones_like(x), x, y, xx_high, xx - xx_high, yy_high, yy - yy_high)
    row = lax.broadcasted_iota(jnp.int32, (SUB, vel), 0)
    zero = jnp.zeros((SUB, vel), f32)
    for n in range(MODES):
        mine = row == n
        for pair in range(TERMS // 2):
            halves = []
            for term in (2 * pair, 2 * pair + 1):
                which = term // 3
                halves.append(jnp.where(mine, monomials[which], 0.0) if which < len(monomials) else zero)
            basis[pl.ds(pair * 2 * SUB, 2 * SUB), pl.ds(n * vel, vel)] = jnp.concatenate(
                halves, axis=0
            ).astype(bf16)


def node_parameters(mom, rate, elems, scale):
    shape = (SUB, elems)
    row = lax.broadcasted_iota(jnp.int32, shape, 0)

    def column(values):
        out = jnp.full(shape, k(values[0]), f32)
        for n in range(1, MODES):
            out = jnp.where(row == n, k(values[n]), out)
        return out

    columns = [column(NODAL[:, j]) for j in range(MODES)]
    R = []
    for index in range(8):
        total = columns[0] * mom[index : index + 1, :]
        for j in range(1, MODES):
            total = total + columns[j] * mom[j * SUB + index : j * SUB + index + 1, :]
        R.append(total)
    zeroth, mass_x, mass_y, flux_xx, flux_xy, flux_yy, third_x, third_y = R
    density = jnp.maximum(zeroth, density_floor)
    ux = mass_x / density
    uy = mass_y / density
    drift_sq = ux * ux + uy * uy
    drift_mass = ux * mass_x + uy * mass_y
    trace = flux_xx + flux_yy
    kelvin = jnp.maximum(
        (trace - 2.0 * drift_mass + drift_sq * zeroth) / (2.0 * density), kelvin_lower_limit
    )
    qx = 0.5 * (
        third_x
        - 2.0 * (flux_xx * ux + flux_xy * uy)
        + mass_x * drift_sq
        - ux * trace
        + 2.0 * ux * drift_mass
        - ux * drift_sq * zeroth
    )
    qy = 0.5 * (
        third_y
        - 2.0 * (flux_xy * ux + flux_yy * uy)
        + mass_y * drift_sq
        - uy * trace
        + 2.0 * uy * drift_mass
        - uy * drift_sq * zeroth
    )
    nu = scale * rate * density
    over = 1.0 / kelvin
    weight = (1.0 - viscous_conductive_ratio) / (4.0 * density * kelvin * kelvin)
    qx = qx * weight
    qy = qy * weight
    excess = (over * drift_sq - 4.0, -2.0 * over * ux, -2.0 * over * uy, over, over)
    amplitude = jnp.log(nu * density * over * k(1.0 / (2.0 * math.pi)))
    exponent = (
        amplitude - 0.5 * over * drift_sq,
        over * ux,
        over * uy,
        -0.5 * over,
        -0.5 * over,
    )
    skew = (-(qx * ux + qy * uy), qx, qy)
    return nu, (excess, exponent, skew)


def spread(form, elems):
    pieces = []
    for index, value in enumerate(form):
        parts = split3(value)
        pieces += parts
        if index >= 3:
            pieces += parts
    pieces.append(jnp.zeros((TERMS * SUB - SUB * len(pieces), elems), f32))
    return jnp.concatenate(pieces, axis=0).T.astype(bf16)


def relaxed(forms, slot, row, chunk, vel, nu, inside):
    def form(i):
        return forms[i][pl.ds(row, SUB), pl.ds(slot * vel + chunk * LANE, LANE)]

    skewed = jnp.minimum(jnp.maximum(form(2) * form(0), -skew_multiplier_limit), skew_multiplier_limit)
    return jnp.exp(form(1)) * (1.0 + skewed) - nu * inside


def form_kernel(*refs, parts, section):
    mom_refs = refs[:parts]
    rate, basis, spreads, nus, *forms = refs[parts:]
    elems = rate.shape[1]
    half = basis.shape[1] // 2
    scale = time_step if section == 0 else 0.5 * time_step
    moments = mom_refs[0][...]
    for ref in mom_refs[1:]:
        moments = moments + ref[...]
    nu, coefficients = node_parameters(moments, rate[...], elems, scale)
    nus[...] = jnp.concatenate([nu, jnp.zeros((LANE - SUB, elems), f32)], axis=0).T
    for i, form in enumerate(coefficients):
        spreads[i] = spread(form, elems)
        forms[i][...] = jnp.dot(spreads[i], basis[:, pl.ds(half, half)], preferred_element_type=f32)


def mean_kernel(offsets, src, info, _, z_ref, near_in, far_in, cols, nus, *refs, section):
    forms = refs[:3]
    refs = refs[3:]
    base_ref = None
    if section == 1:
        base_ref = refs[0]
        refs = refs[1:]
    tbl, centre, high, near, far, mtbl, stage_a, stage_b, stage = refs
    elems, vel = z_ref.shape[1:]
    chunks = vel // LANE
    slots = offsets.shape[1]
    faces = 3 * elems

    def fill_border(row):
        for side, halo in zip(sides(info), (near_in, far_in)):
            for c in range(chunks):
                start = (faces + side * slots + row) * chunks + c
                tbl[pl.ds(start, SUB, stride=chunks), :] = halo[(0, *at(row, c))]

    over_groups(slots, fill_border)

    N, V = NODAL, INVERSE
    grid = chunk_grid(info[0], chunks)

    def fetch(row, stage):
        for m in range(3):
            for i in range(SUB):
                copy_rows(tbl, stage, src[m, row + i], (m * SUB + i) * chunks, chunks)

    def compute(row, stage):
        flows = flow_forms(cols, grid, row)
        nu_cols = [jnp.broadcast_to(nus[pl.ds(row, SUB), n : n + 1], (SUB, LANE)) for n in range(3, MODES)]
        for c in range(chunks):
            z0, z1, z2, z3, z4, z5 = modes_at(z_ref, row, c)
            own = level0((z0, z1, z2, z3, z4, z5))
            through = None
            for m in range(3):
                g = flows[c][m]
                value = g * jnp.where(
                    g < 0.0, own[m], stage[pl.ds(m * SUB * chunks + c, SUB, stride=chunks), :]
                )
                through = value if through is None else through + value
            moved = z0 + through * k(EDGE[0, 0, 0])
            if section == 1:
                moved = 0.5 * (base_ref[(0, *at(row, c))] + moved)
            a0 = z0 * k(N[0, 0])
            e34 = a0 + z1 * k(N[3, 1]) + z3 * k(N[3, 3]) + z5 * k(N[3, 5])
            o34 = z2 * k(N[4, 2]) + z4 * k(N[4, 4])
            inside = (
                e34 - o34,
                e34 + o34,
                a0 + z1 * k(N[5, 1]) + z3 * k(N[5, 3]) + z5 * k(N[5, 5]),
            )
            H = [relaxed(forms, n, row, c, vel, nu_cols[n], inside[n]) for n in range(3)]
            value = moved + (H[0] + H[1] + H[2]) * k(V[0, 3])
            centre[at(row, c)] = value
            mtbl[pl.ds(row * chunks + c, SUB, stride=chunks), :] = value
            for n in range(3):
                high[(n, *at(row, c))] = H[n]

    pipelined_groups(elems, (stage_a, stage_b), fetch, compute)

    def take(row):
        for place, side in enumerate(sides(info)):
            for i in range(SUB):
                copy_rows(mtbl, stage, offsets[2 + side, row + i], (place * slots + row + i) * chunks, chunks)

    over_groups(slots, take)

    def pack(row):
        for place, out in enumerate((near, far)):
            for c in range(chunks):
                start = (place * slots + row) * chunks + c
                out[at(row, c)] = stage[pl.ds(start, SUB, stride=chunks), :]

    over_groups(slots, pack)


def rest_kernel(src, info, tbl0, _, z_ref, near, far, high, spreads, nus, basis, cols, *refs, section):
    base_ref = None
    if section == 1:
        base_ref = refs[0]
        refs = refs[1:]
    tbl, out, sizes, stage_a, stage_b, *forms = refs
    elems, vel = z_ref.shape[1:]
    chunks = vel // LANE
    pitch = 3 * chunks
    slots = near.shape[1]
    faces = 3 * elems

    def fill_border(row):
        for side, halo in zip(sides(info), (near, far)):
            for level in range(2):
                for c in range(chunks):
                    start = ((faces + side * slots + row) * 2 + level) * chunks + c
                    tbl[pl.ds(start, SUB, stride=2 * chunks), :] = halo[(level + 1, *at(row, c))]

    over_groups(slots, fill_border)

    for i in range(3):
        forms[i][...] = jnp.dot(
            spreads[i], basis[:, pl.ds(0, 3 * vel)], preferred_element_type=f32
        )
    N, V, B0, B2 = NODAL, INVERSE, EDGE[0], EDGE[2]
    grid = chunk_grid(info[0], chunks)

    def fetch(row, stage):
        for m in range(3):
            for i in range(SUB):
                start = src[m, row + i]
                to = (m * SUB + i) * pitch
                copy_rows(tbl0, stage, start, to, chunks)
                copy_rows(tbl, stage, 2 * start, to + chunks, 2 * chunks)

    def compute(row, stage):
        flows = flow_forms(cols, grid, row)
        nu_cols = [jnp.broadcast_to(nus[pl.ds(row, SUB), n : n + 1], (SUB, LANE)) for n in range(3)]
        for c in range(chunks):
            z = modes_at(z_ref, row, c)
            z0, z1, z2, z3, z4, z5 = z

            def beside(m, level):
                return stage[pl.ds(m * SUB * pitch + level * chunks + c, SUB, stride=pitch), :]

            even, odd, last = edge_parts(z)
            gs, g1, gr = flows[c]
            out0 = gs < 0.0
            out1 = g1 < 0.0
            out2 = gr < 0.0
            V0 = [gs * jnp.where(out0, even[i] - odd[i], beside(0, i)) for i in range(3)]
            W0 = [
                g1 * jnp.where(out1, even[0] + odd[0], beside(1, 0)),
                g1 * jnp.where(out1, even[1] + odd[1], -beside(1, 1)),
                g1 * jnp.where(out1, even[2] + odd[2], beside(1, 2)),
            ]
            X = [gr * jnp.where(out2, last[i], beside(2, i)) for i in range(3)]
            S = [a + b for a, b in zip(V0, W0)]
            D = [b - a for a, b in zip(V0, W0)]
            h = gr + 2.0 * gs
            moved = [
                z1 + S[0] * k(B0[0, 1]) + S[1] * k(B0[1, 1]) + X[0] * k(B2[0, 1]) + (gr * z0) * k(KR[1, 0]),
                z2 + D[0] * k(-B0[0, 2]) + D[1] * k(-B0[1, 2]) + X[1] * k(B2[1, 2]) + (h * z0) * k(KR[2, 0]),
                z3
                + S[0] * k(B0[0, 3])
                + S[1] * k(B0[1, 3])
                + S[2] * k(B0[2, 3])
                + X[0] * k(B2[0, 3])
                + gr * (z0 * k(KR[3, 0]) + z1 * k(KR[3, 1])),
                z4
                + D[0] * k(-B0[0, 4])
                + D[1] * k(-B0[1, 4])
                + D[2] * k(-B0[2, 4])
                + X[1] * k(B2[1, 4])
                + h * (z0 * k(KR[4, 0]) + z1 * k(KR[4, 1]))
                + gr * (z2 * k(KR[4, 2])),
                z5
                + S[0] * k(B0[0, 5])
                + S[1] * k(B0[1, 5])
                + S[2] * k(B0[2, 5])
                + X[2] * k(B2[2, 5])
                + gr * (z0 * k(KR[5, 0]) + z1 * k(KR[5, 1]))
                + h * (z2 * k(KR[5, 2])),
            ]
            if section == 1:
                moved = [0.5 * (base_ref[(j + 1, *at(row, c))] + moved[j]) for j in range(5)]
            e02 = last[0] + z5 * k(N[0, 5])
            o02 = z2 * k(N[2, 2]) + z4 * k(N[2, 4])
            inside = (e02 - o02, z0 * k(N[0, 0]) + z1 * k(N[1, 1]) + z3 * k(N[1, 3]), e02 + o02)
            H = [relaxed(forms, n, row, c, vel, nu_cols[n], inside[n]) for n in range(3)]
            H += [high[(n, *at(row, c))] for n in range(3)]
            s02 = H[0] + H[2]
            d20 = H[2] - H[0]
            s34 = H[3] + H[4]
            d43 = H[4] - H[3]
            change = (
                s02 * k(V[1, 0]) + H[1] * k(V[1, 1]) + s34 * k(V[1, 3]) + H[5] * k(V[1, 5]),
                d20 * k(V[2, 2]) + d43 * k(V[2, 4]),
                (s02 + H[5]) * k(V[3, 0]) + (H[1] - s34) * k(V[3, 1]),
                d20 * k(V[4, 2]) + d43 * k(V[4, 4]),
                s02 * k(V[5, 0]) + H[5] * k(V[5, 5]),
            )
            z = [moved[j] + change[j] for j in range(5)]
            for j in range(5):
                out[(j, *at(row, c))] = z[j]
            size1 = jnp.abs(z[0])
            size2 = jnp.abs(z[1])
            size4 = jnp.abs(z[3])
            linear = None
            quadric = None
            for m, q in ((0, 0), (0, 1), (0, 2), (2, 0), (2, 1)):
                t = TR[m, q]
                if q != 1:
                    value = size1 * k(abs(t[1])) + size2 * k(abs(t[2]))
                    linear = value if linear is None else jnp.maximum(linear, value)
                value = jnp.abs(z[2] * k(t[3]) + z[4] * k(t[5]))
                if abs(t[4]) > 1e-9:
                    value = value + size4 * k(abs(t[4]))
                quadric = value if quadric is None else jnp.maximum(quadric, value)
            linear = jnp.maximum(linear, slope_floor)
            quadric = jnp.maximum(quadric, slope_floor)
            over = k(math.sqrt(2.0)) / (linear * quadric)
            sizes[(0, *at(row, c))] = over * quadric
            sizes[(1, *at(row, c))] = over * linear

    pipelined_groups(elems, (stage_a, stage_b), fetch, compute)


def limit_kernel(away, info, centre, rest, sizes, near, far, out, *refs, section):
    if section == 0:
        mom, mtbl, stage_a, stage_b = refs
        target = out
    else:
        mtbl, stage_a, stage_b, target, sems = refs
    elems, vel = centre.shape
    chunks = vel // LANE
    slots = near.shape[0]

    def fill(row):
        for c in range(chunks):
            mtbl[pl.ds(row * chunks + c, SUB, stride=chunks), :] = centre[at(row, c)]

    over_groups(elems, fill)

    def fill_border(row):
        for side, halo in zip(sides(info), (near, far)):
            for c in range(chunks):
                start = (elems + side * slots + row) * chunks + c
                mtbl[pl.ds(start, SUB, stride=chunks), :] = halo[at(row, c)]

    over_groups(slots, fill_border)

    def fetch(row, stage):
        for m in range(3):
            for i in range(SUB):
                copy_rows(mtbl, stage, away[m, row + i], (m * SUB + i) * chunks, chunks)

    def compute(row, stage):
        for c in range(chunks):
            z0 = centre[at(row, c)]
            gaps = [
                jnp.abs(stage[pl.ds(m * SUB * chunks + c, SUB, stride=chunks), :] - z0) for m in range(3)
            ]
            gap = jnp.maximum(jnp.maximum(gaps[0], gaps[1]), gaps[2])
            theta1 = jnp.minimum(1.0, gap * sizes[(0, *at(row, c))])
            theta2 = jnp.minimum(theta1, gap * sizes[(1, *at(row, c))])
            target[(0, *at(row, c))] = z0
            for j in range(1, MODES):
                target[(j, *at(row, c))] = rest[(j - 1, *at(row, c))] * (theta1 if j < 3 else theta2)

    if section == 0:
        pipelined_groups(elems, (stage_a, stage_b), fetch, compute)
        weights = weight_rows(info[0], vel)
        for j in range(MODES):
            mom[pl.ds(j * SUB, SUB), :] = mode_moments(weights, target[j])
    else:
        pieces = sems.shape[0]
        size = elems // pieces
        copies = []
        for piece in range(pieces):
            begin = piece * size

            def fetch_piece(row, stage, begin=begin):
                fetch(row + begin, stage)

            def compute_piece(row, stage, begin=begin):
                compute(pl.multiple_of(row + begin, SUB), stage)

            pipelined_groups(size, (stage_a, stage_b), fetch_piece, compute_piece)
            part = pl.ds(begin, size)
            copy = pltpu.make_async_copy(target.at[:, part, :], out.at[:, part, :], sems.at[piece])
            copy.start()
            copies.append(copy)
        for copy in copies:
            copy.wait()


def traded(value, near):
    peers = lax.axis_size("space")
    pairs = []
    for i in range(0 if near else 1, peers - 1, 2):
        pairs += [(i, i + 1), (i + 1, i)]
    return lax.ppermute(value, "space", pairs)


def swapped(value, bits):
    peers = lax.axis_size("vel")
    return lax.ppermute(value, "vel", [(i, i ^ bits) for i in range(peers)])


def moment_parts(paired):
    peers = lax.axis_size("vel")
    done = 2
    while True:
        width = min(4, peers // done)
        parts = [paired] + [swapped(paired, bits * done) for bits in range(1, width)]
        done *= width
        if done >= peers:
            return parts
        paired = sum(parts[1:], parts[0])


def on_device(distribution, corners, neighbour, boundary_faces, collision_rate):
    modes, elems, vel = distribution.shape
    chunks = vel // LANE
    slots = boundary_faces.shape[2]
    lists = boundary_faces[0]
    info = jnp.stack([lax.axis_index("vel") * vel, lax.axis_index("space") % 2]).astype(jnp.int32)
    faces = 3 * elems
    rows = faces + 2 * slots
    S = jax.ShapeDtypeStruct
    state = S((modes, elems, vel), f32)
    one = S((slots, vel), f32)
    halo = S((3, slots, vel), f32)
    mom = S((modes * SUB, elems), f32)
    columns = S((elems, LANE), f32)
    smem = pl.BlockSpec(memory_space=pltpu.SMEM)
    vmem = pl.BlockSpec(memory_space=pltpu.VMEM)
    hbm = pl.BlockSpec(memory_space=pltpu.HBM)

    def params(mib):
        return pltpu.CompilerParams(vmem_limit_bytes=mib << 20)

    def buffer(count):
        return pltpu.VMEM((count, LANE), f32)

    def evaluated():
        return [pltpu.VMEM((elems, 3 * vel), f32) for _ in range(3)]

    rate = collision_rate.reshape(1, elems)
    index = S(neighbour.shape, jnp.int32)
    src, away, offsets, basis, cols = pl.pallas_call(
        prepare_kernel,
        out_shape=(
            index,
            index,
            S((4, slots), jnp.int32),
            S((TERMS * SUB, modes * vel), bf16),
            columns,
        ),
        in_specs=[smem, smem] + [vmem] * 3,
        out_specs=(vmem,) * 5,
        compiler_params=params(8),
        name="prepare",
    )(lists, info, neighbour, lists, corners.transpose(1, 0, 2))

    current = start = distribution
    partial = pl.pallas_call(
        first_kernel,
        out_shape=mom,
        in_specs=[smem, vmem],
        out_specs=vmem,
        compiler_params=params(8),
        name="first",
    )(info, current)

    for section in range(2):
        opening = section == 0
        paired = partial + swapped(partial, 1)
        tbl0, tbl12, near, far = pl.pallas_call(
            trace_kernel,
            out_shape=(S((rows * chunks, LANE), f32), S((2 * rows * chunks, LANE), f32), halo, halo),
            in_specs=[smem, smem, vmem],
            out_specs=(vmem,) * 4,
            scratch_shapes=[buffer(2 * slots * chunks), buffer(4 * slots * chunks)],
            compiler_params=params(8),
            name="trace",
        )(offsets, info, current)
        near, far, paired = lax.optimization_barrier((near, far, paired))
        far = traded(far, False)
        near = traded(near, True)
        parts = moment_parts(paired)

        base = [] if opening else [start]
        spreads, nus, *forms = pl.pallas_call(
            lambda *refs, section=section: form_kernel(*refs, parts=len(parts), section=section),
            out_shape=(S((3, elems, TERMS * SUB), bf16), columns) + (S((elems, 3 * vel), f32),) * 3,
            in_specs=[vmem] * (len(parts) + 2),
            out_specs=(vmem,) * 5,
            compiler_params=params(16),
            name=f"form{section}",
        )(*parts, rate, basis)

        tbl0, centre, high, near_mean, far_mean = pl.pallas_call(
            lambda *refs, section=section: mean_kernel(*refs, section=section),
            out_shape=(S((rows * chunks, LANE), f32), S((elems, vel), f32), S((3, elems, vel), f32), one, one),
            input_output_aliases={3: 0},
            in_specs=[smem] * 3 + [vmem] * (9 + len(base)),
            out_specs=(vmem,) * 5,
            scratch_shapes=[buffer(elems * chunks)]
            + [buffer(3 * SUB * chunks)] * 2
            + [buffer(2 * slots * chunks)],
            compiler_params=params(16),
            name=f"mean{section}",
        )(offsets, src, info, tbl0, current, near, far, cols, nus, *forms, *base)
        far_mean = traded(far_mean, False)
        near_mean = traded(near_mean, True)

        _, rest, sizes = pl.pallas_call(
            lambda *refs, section=section: rest_kernel(*refs, section=section),
            out_shape=(S((2 * rows * chunks, LANE), f32), S((5, elems, vel), f32), S((2, elems, vel), f32)),
            input_output_aliases={3: 0},
            in_specs=[smem] * 2 + [vmem] * (10 + len(base)),
            out_specs=(vmem,) * 3,
            scratch_shapes=[buffer(9 * SUB * chunks)] * 2 + evaluated(),
            compiler_params=params(20),
            name=f"rest{section}",
        )(src, info, tbl0, tbl12, current, near, far, high, spreads, nus, basis, cols, *base)

        scratch = [buffer((elems + 2 * slots) * chunks)] + [buffer(3 * SUB * chunks)] * 2
        if not opening:
            scratch += [pltpu.VMEM(state.shape, f32), pltpu.SemaphoreType.DMA((4,))]
        made = pl.pallas_call(
            lambda *refs, section=section: limit_kernel(*refs, section=section),
            out_shape=(state, mom) if opening else (state,),
            in_specs=[smem, smem] + [vmem] * 5,
            out_specs=(vmem, vmem) if opening else (hbm,),
            scratch_shapes=scratch,
            compiler_params=params(8),
            name=f"limit{section}",
        )(away, info, centre, rest, sizes, near_mean, far_mean)
        if opening:
            current, partial = made
    return made[0]


def solution(mesh):
    in_specs = (
        P(None, "space", "vel"),
        P(None, None, "space"),
        P(None, "space"),
        P("space", None, None),
        P("space"),
    )
    return jax.shard_map(
        on_device, mesh=mesh, in_specs=in_specs, out_specs=P(None, "space", "vel"), check_vma=False
    )
```

```python
import math

import jax
import jax.numpy as jnp
import numpy as np
from jax import lax
from jax.experimental import pallas as pl
from jax.experimental.pallas import tpu as pltpu
from jax.sharding import PartitionSpec as P

VGRID = 64
velocity_limit = 6.0
time_step = 0.012
viscous_conductive_ratio = 2.0 / 3.0
density_floor = 0.1
kelvin_lower_limit = 0.2
skew_multiplier_limit = 0.9
slope_floor = 0.01

LANE = 128
SUB = 8
MODES = 6
TERMS = 32
f32 = jnp.float32
bf16 = jnp.bfloat16


def monomial_integral(power_r, power_s):
    return math.factorial(power_r) * math.factorial(power_s) / math.factorial(power_r + power_s + 2)


def dg_tables():
    powers = [(0, 0), (1, 0), (0, 1), (2, 0), (1, 1), (0, 2)]
    gram = np.array(
        [[monomial_integral(a[0] + b[0], a[1] + b[1]) for b in powers] for a in powers]
    )
    coeffs = np.linalg.inv(np.linalg.cholesky(gram))
    deriv_r = np.zeros((6, 6))
    deriv_s = np.zeros((6, 6))
    for i, a in enumerate(powers):
        for j, b in enumerate(powers):
            if a[0] > 0:
                deriv_r[i, j] = a[0] * monomial_integral(a[0] - 1 + b[0], a[1] + b[1])
            if a[1] > 0:
                deriv_s[i, j] = a[1] * monomial_integral(a[0] + b[0], a[1] - 1 + b[1])
    stiff_r = coeffs @ deriv_r @ coeffs.T
    stiff_s = coeffs @ deriv_s @ coeffs.T

    def evaluate(location):
        return coeffs @ np.array([location[0] ** p[0] * location[1] ** p[1] for p in powers])

    vertices = np.array([[0.0, 0.0], [1.0, 0.0], [0.0, 1.0]])
    offset = math.sqrt(0.15)
    positions = np.array([0.5 - offset, 0.5, 0.5 + offset])
    weights = np.array([5.0, 8.0, 5.0]) / 18.0
    traces = np.zeros((3, 3, 6))
    for m in range(3):
        for q in range(3):
            along = positions[q]
            traces[m, q] = evaluate((1.0 - along) * vertices[m] + along * vertices[(m + 1) % 3])
    legendre = np.stack(
        [
            np.ones(3),
            math.sqrt(3.0) * (2.0 * positions - 1.0),
            math.sqrt(5.0) * (6.0 * positions**2 - 6.0 * positions + 1.0),
        ]
    )
    edge = np.einsum("lq,q,mqj->mlj", legendre, weights, traces)
    node_list = [(0.0, 0.0), (1.0, 0.0), (0.0, 1.0), (0.5, 0.0), (0.5, 0.5), (0.0, 0.5)]
    nodal = np.array([evaluate(np.array(n)) for n in node_list])
    inverse = np.linalg.inv(nodal)
    return stiff_r, stiff_s, traces, edge, nodal, inverse


KR, KS, TR, EDGE, NODAL, INVERSE = dg_tables()


def k(value):
    return float(np.float32(value))


def edge_parts(z):
    z0, z1, z2, z3, z4, z5 = z
    b = EDGE[0]
    a0 = z0 * k(b[0, 0])
    even = (
        a0 + z1 * k(b[0, 1]) + z3 * k(b[0, 3]) + z5 * k(b[0, 5]),
        z1 * k(b[1, 1]) + z3 * k(b[1, 3]) + z5 * k(b[1, 5]),
        z3 * k(b[2, 3]) + z5 * k(b[2, 5]),
    )
    odd = (
        z2 * k(-b[0, 2]) + z4 * k(-b[0, 4]),
        z2 * k(-b[1, 2]) + z4 * k(-b[1, 4]),
        z4 * k(-b[2, 4]),
    )
    c = EDGE[2]
    last = (
        a0 + z1 * k(c[0, 1]) + z3 * k(c[0, 3]),
        z2 * k(c[1, 2]) + z4 * k(c[1, 4]),
        z5 * k(c[2, 5]),
    )
    return even, odd, last


def table_values(z):
    even, odd, last = edge_parts(z)
    return (
        (even[0] - odd[0], odd[1] - even[1], even[2] - odd[2]),
        (even[0] + odd[0], even[1] + odd[1], even[2] + odd[2]),
        (last[0], -last[1], last[2]),
    )


def at(row, chunk):
    return pl.ds(row, SUB), pl.ds(chunk * LANE, LANE)


def modes_at(ref, row, chunk):
    return [ref[(j, *at(row, chunk))] for j in range(ref.shape[0])]


def over_groups(count, body, together=1):
    def step(g, _):
        for i in range(together):
            body(pl.multiple_of(g * (SUB * together) + i * SUB, SUB))
        return 0

    lax.fori_loop(0, count // (SUB * together), step, 0)


def copy_rows(source, target, start, to, count):
    for piece in range(0, count, SUB):
        rows = min(SUB, count - piece)
        target[pl.ds(to + piece, rows), :] = source[pl.ds(start + piece, rows), :]


def pipelined_groups(count, stages, fetch, compute):
    last = count - SUB
    fetch(0, stages[0])

    def step(pair, _):
        row = pl.multiple_of(pair * (2 * SUB), 2 * SUB)
        after = pl.multiple_of(row + SUB, SUB)
        fetch(after, stages[1])
        compute(row, stages[0])
        fetch(pl.multiple_of(jnp.minimum(row + 2 * SUB, last), SUB), stages[0])
        compute(after, stages[1])
        return 0

    lax.fori_loop(0, count // (2 * SUB), step, 0)


def grid_rows(first, shape):
    index = first + lax.broadcasted_iota(jnp.int32, shape, len(shape) - 1)
    spacing = 2.0 * velocity_limit / VGRID
    x = -velocity_limit + ((index // VGRID).astype(f32) + 0.5) * spacing
    y = -velocity_limit + ((index % VGRID).astype(f32) + 0.5) * spacing
    return x, y, spacing


def split3(value):
    high = value.astype(bf16).astype(f32)
    rest = value - high
    middle = rest.astype(bf16).astype(f32)
    return high, middle, (rest - middle).astype(bf16).astype(f32)


def weight_rows(first, vel):
    x, y, spacing = grid_rows(first, (SUB, vel))
    row = lax.broadcasted_iota(jnp.int32, (SUB, vel), 0)
    square = x * x + y * y
    weights = jnp.ones_like(x)
    for index, value in enumerate((x, y, x * x, x * y, y * y, x * square, y * square)):
        weights = jnp.where(row == index + 1, value, weights)
    weights = weights * (spacing * spacing)
    return jnp.concatenate([*split3(weights), jnp.zeros_like(x)], axis=0).astype(bf16)


def mode_moments(weights, value):
    high = value.astype(bf16)
    low = (value - high.astype(f32)).astype(bf16)
    dims = (((1,), (1,)), ((), ()))
    total = lax.dot_general(weights, high, dims, preferred_element_type=f32)
    total = total + lax.dot_general(weights, low, dims, preferred_element_type=f32)
    return total[0:8] + total[8:16] + total[16:24]


def first_kernel(info, z_ref, mom):
    weights = weight_rows(info[0], z_ref.shape[2])
    for j in range(MODES):
        mom[pl.ds(j * SUB, SUB), :] = mode_moments(weights, z_ref[j])


def put_index(neigh_ref, rows_ref, lists, src, away, offsets, elems, chunks):
    slots = rows_ref.shape[1]
    faces = 3 * elems
    shape = neigh_ref.shape
    face = lax.broadcasted_iota(jnp.int32, shape, 0) * elems + lax.broadcasted_iota(jnp.int32, shape, 1)

    def mark(slot, found):
        found = jnp.where(face == lists[0, slot], faces + slot, found)
        return jnp.where(face == lists[1, slot], faces + slots + slot, found)

    found = jnp.maximum(lax.fori_loop(0, slots, mark, neigh_ref[...]), 0)
    src[...] = found * chunks
    away[...] = jnp.where(found < faces, found % elems, found - 2 * elems) * chunks
    known = jnp.maximum(rows_ref[...], 0)
    offsets[pl.ds(0, 2), :] = known * chunks
    offsets[pl.ds(2, 2), :] = known % elems * chunks


def put_columns(rows, out):
    elems = out.shape[1]
    turned = jnp.concatenate([*rows, jnp.zeros((LANE - out.shape[0], elems), f32)], axis=0).T
    for n in range(out.shape[0]):
        out[n] = jnp.broadcast_to(turned[:, n : n + 1], (elems, LANE))


def put_flows(corner, cols):
    cx = [corner[i, 0:1, :] for i in range(3)]
    cy = [corner[i, 1:2, :] for i in range(3)]
    det = (cx[1] - cx[0]) * (cy[2] - cy[0]) - (cx[2] - cx[0]) * (cy[1] - cy[0])
    step = time_step / det
    rows = [-step * (cy[1] - cy[0]), step * (cx[1] - cx[0]), -step * (cy[0] - cy[2]), step * (cx[0] - cx[2])]
    put_columns(rows, cols)


def sides(info):
    parity = info[1]
    return (1 - parity, parity)


def prepare_kernel(lists, info, neigh_ref, rows_ref, corner, src, away, offsets, basis, cols):
    vel = basis.shape[1] // MODES
    put_index(neigh_ref, rows_ref, lists, src, away, offsets, cols.shape[1], vel // LANE)
    put_flows(corner, cols)
    put_basis(info[0], basis, vel)


def trace_kernel(offsets, info, z_ref, tbl0, tbl12, near, far, stage0, stage12):
    elems, vel = z_ref.shape[1:]
    chunks = vel // LANE
    slots = offsets.shape[1]

    def fill(row):
        for c in range(chunks):
            for m, values in enumerate(table_values(modes_at(z_ref, row, c))):
                start = (m * elems + row) * chunks + c
                tbl0[pl.ds(start, SUB, stride=chunks), :] = values[0]
                for level in (1, 2):
                    start = ((m * elems + row) * 2 + level - 1) * chunks + c
                    tbl12[pl.ds(start, SUB, stride=2 * chunks), :] = values[level]

    over_groups(elems, fill)

    def take(row):
        for place, side in enumerate(sides(info)):
            for i in range(SUB):
                start = offsets[side, row + i]
                to = (place * slots + row + i) * chunks
                copy_rows(tbl0, stage0, start, to, chunks)
                copy_rows(tbl12, stage12, 2 * start, 2 * to, 2 * chunks)

    over_groups(slots, take)

    def pack(row):
        for place, out in enumerate((near, far)):
            for c in range(chunks):
                start = (place * slots + row) * chunks
                out[(0, *at(row, c))] = stage0[pl.ds(start + c, SUB, stride=chunks), :]
                for level in range(2):
                    out[(level + 1, *at(row, c))] = stage12[
                        pl.ds(2 * start + level * chunks + c, SUB, stride=2 * chunks), :
                    ]

    over_groups(slots, pack)


def flow_forms(cols, grid, row, half=False):
    col = [cols[n, pl.ds(row, SUB), :] for n in range(4)]
    if half:
        col = [0.5 * value for value in col]
    flows = []
    for x, y in grid:
        g0 = col[0] * x + col[1] * y
        g2 = col[2] * x + col[3] * y
        flows.append((g0, -(g0 + g2), g2))
    return flows


def chunk_grid(first, chunks):
    return [grid_rows(first + c * LANE, (1, LANE))[:2] for c in range(chunks)]


def put_basis(first, basis, vel):
    x, y, _ = grid_rows(first, (1, vel))
    xx = x * x
    yy = y * y
    xx_high = xx.astype(bf16).astype(f32)
    yy_high = yy.astype(bf16).astype(f32)
    monomials = (jnp.ones_like(x), x, y, xx_high, xx - xx_high, yy_high, yy - yy_high)
    row = lax.broadcasted_iota(jnp.int32, (SUB, vel), 0)
    zero = jnp.zeros((SUB, vel), f32)
    for n in range(MODES):
        mine = row == n
        for pair in range(TERMS // 2):
            halves = []
            for term in (2 * pair, 2 * pair + 1):
                which = term // 3
                halves.append(jnp.where(mine, monomials[which], 0.0) if which < len(monomials) else zero)
            basis[pl.ds(pair * 2 * SUB, 2 * SUB), pl.ds(n * vel, vel)] = jnp.concatenate(
                halves, axis=0
            ).astype(bf16)


def node_parameters(mom, rate, elems, scale):
    shape = (SUB, elems)
    row = lax.broadcasted_iota(jnp.int32, shape, 0)

    def column(values):
        out = jnp.full(shape, k(values[0]), f32)
        for n in range(1, MODES):
            out = jnp.where(row == n, k(values[n]), out)
        return out

    columns = [column(NODAL[:, j]) for j in range(MODES)]
    R = []
    for index in range(8):
        total = columns[0] * mom[index : index + 1, :]
        for j in range(1, MODES):
            total = total + columns[j] * mom[j * SUB + index : j * SUB + index + 1, :]
        R.append(total)
    zeroth, mass_x, mass_y, flux_xx, flux_xy, flux_yy, third_x, third_y = R
    density = jnp.maximum(zeroth, density_floor)
    ux = mass_x / density
    uy = mass_y / density
    drift_sq = ux * ux + uy * uy
    drift_mass = ux * mass_x + uy * mass_y
    trace = flux_xx + flux_yy
    kelvin = jnp.maximum(
        (trace - 2.0 * drift_mass + drift_sq * zeroth) / (2.0 * density), kelvin_lower_limit
    )
    qx = 0.5 * (
        third_x
        - 2.0 * (flux_xx * ux + flux_xy * uy)
        + mass_x * drift_sq
        - ux * trace
        + 2.0 * ux * drift_mass
        - ux * drift_sq * zeroth
    )
    qy = 0.5 * (
        third_y
        - 2.0 * (flux_xy * ux + flux_yy * uy)
        + mass_y * drift_sq
        - uy * trace
        + 2.0 * uy * drift_mass
        - uy * drift_sq * zeroth
    )
    nu = scale * rate * density
    over = 1.0 / kelvin
    weight = (1.0 - viscous_conductive_ratio) / (4.0 * density * kelvin * kelvin)
    qx = qx * weight
    qy = qy * weight
    excess = (over * drift_sq - 4.0, -2.0 * over * ux, -2.0 * over * uy, over, over)
    amplitude = jnp.log(nu * density * over * k(1.0 / (2.0 * math.pi)))
    exponent = (
        amplitude - 0.5 * over * drift_sq,
        over * ux,
        over * uy,
        -0.5 * over,
        -0.5 * over,
    )
    skew = (-(qx * ux + qy * uy), qx, qy)
    return nu, (excess, exponent, skew)


def spread(form, elems):
    pieces = []
    for index, value in enumerate(form):
        parts = split3(value)
        pieces += parts
        if index >= 3:
            pieces += parts
    pieces.append(jnp.zeros((TERMS * SUB - SUB * len(pieces), elems), f32))
    return jnp.concatenate(pieces, axis=0).T.astype(bf16)


def relaxed(forms, slot, row, chunk, vel, nu, inside):
    def form(i):
        return forms[i][pl.ds(row, SUB), pl.ds(slot * vel + chunk * LANE, LANE)]

    skewed = jnp.minimum(jnp.maximum(form(2) * form(0), -skew_multiplier_limit), skew_multiplier_limit)
    return jnp.exp(form(1)) * (1.0 + skewed) - nu * inside


def form_kernel(*refs, parts, section):
    mom_refs = refs[:parts]
    rate, basis, spreads, nus, *forms = refs[parts:]
    elems = rate.shape[1]
    half = basis.shape[1] // 2
    scale = time_step if section == 0 else 0.5 * time_step
    moments = mom_refs[0][...]
    for ref in mom_refs[1:]:
        moments = moments + ref[...]
    nu, coefficients = node_parameters(moments, rate[...], elems, scale)
    put_columns([nu[n : n + 1, :] for n in range(MODES)], nus)
    for i, form in enumerate(coefficients):
        spreads[i] = spread(form, elems)
        forms[i][...] = jnp.dot(spreads[i], basis[:, pl.ds(half, half)], preferred_element_type=f32)


def lifted(V, W, X):
    B0, B2 = EDGE[0], EDGE[2]
    S = [a + b for a, b in zip(V, W)]
    D = [b - a for a, b in zip(V, W)]
    return (
        (S[0] + X[0]) * k(B0[0, 0]),
        S[0] * k(B0[0, 1]) + S[1] * k(B0[1, 1]) + X[0] * k(B2[0, 1]),
        D[0] * k(-B0[0, 2]) + D[1] * k(-B0[1, 2]) + X[1] * k(B2[1, 2]),
        S[0] * k(B0[0, 3]) + S[1] * k(B0[1, 3]) + S[2] * k(B0[2, 3]) + X[0] * k(B2[0, 3]),
        D[0] * k(-B0[0, 4]) + D[1] * k(-B0[1, 4]) + D[2] * k(-B0[2, 4]) + X[1] * k(B2[1, 4]),
        S[0] * k(B0[0, 5]) + S[1] * k(B0[1, 5]) + S[2] * k(B0[2, 5]) + X[2] * k(B2[2, 5]),
    )


def own_kernel(info, z_ref, cols, *refs, section):
    if section == 1:
        base_ref, out = refs
    else:
        (out,) = refs
    elems, vel = z_ref.shape[1:]
    chunks = vel // LANE
    grid = chunk_grid(info[0], chunks)

    def compute(row):
        flows = flow_forms(cols, grid, row)
        for c in range(chunks):
            z = modes_at(z_ref, row, c)
            z0, z1, z2, z3, z4, z5 = z
            even, odd, last = edge_parts(z)
            gs, g1, gr = flows[c]
            out0, out1, out2 = [jnp.minimum(g, 0.0) for g in flows[c]]
            V = [out0 * (even[i] - odd[i]) for i in range(3)]
            W = [out1 * (even[i] + odd[i]) for i in range(3)]
            X = [out2 * last[i] for i in range(3)]
            h = gr + 2.0 * gs
            volume = (
                None,
                (gr * z0) * k(KR[1, 0]),
                (h * z0) * k(KR[2, 0]),
                gr * (z0 * k(KR[3, 0]) + z1 * k(KR[3, 1])),
                h * (z0 * k(KR[4, 0]) + z1 * k(KR[4, 1])) + gr * (z2 * k(KR[4, 2])),
                gr * (z0 * k(KR[5, 0]) + z1 * k(KR[5, 1])) + h * (z2 * k(KR[5, 2])),
            )
            surface = lifted(V, W, X)
            for j in range(MODES):
                value = z[j] + surface[j]
                if j:
                    value = value + volume[j]
                if section == 1:
                    value = 0.5 * (base_ref[(j, *at(row, c))] + value)
                out[(j, *at(row, c))] = value

    over_groups(elems, compute, 2)


def mean_kernel(offsets, src, info, _, z_ref, own, near_in, far_in, cols, nus, *refs, section):
    forms = refs[:3]
    refs = refs[3:]
    tbl, mtbl, centre, high, near, far, stage_a, stage_b, stage = refs
    elems, vel = z_ref.shape[1:]
    chunks = vel // LANE
    slots = offsets.shape[1]
    faces = 3 * elems

    def fill_border(row):
        for side, halo in zip(sides(info), (near_in, far_in)):
            for c in range(chunks):
                start = (faces + side * slots + row) * chunks + c
                tbl[pl.ds(start, SUB, stride=chunks), :] = halo[(0, *at(row, c))]

    over_groups(slots, fill_border)

    N, V = NODAL, INVERSE
    grid = chunk_grid(info[0], chunks)

    def fetch(row, stage):
        for m in range(3):
            for i in range(SUB):
                copy_rows(tbl, stage, src[m, row + i], (m * SUB + i) * chunks, chunks)

    def compute(row, stage):
        flows = flow_forms(cols, grid, row, section == 1)
        nu_cols = [nus[n, pl.ds(row, SUB), :] for n in range(3, MODES)]
        for c in range(chunks):
            z0, z1, z2, z3, z4, z5 = modes_at(z_ref, row, c)
            through = None
            for m in range(3):
                value = jnp.maximum(flows[c][m], 0.0) * stage[
                    pl.ds(m * SUB * chunks + c, SUB, stride=chunks), :
                ]
                through = value if through is None else through + value
            moved = own[(0, *at(row, c))] + through * k(EDGE[0, 0, 0])
            a0 = z0 * k(N[0, 0])
            e34 = a0 + z1 * k(N[3, 1]) + z3 * k(N[3, 3]) + z5 * k(N[3, 5])
            o34 = z2 * k(N[4, 2]) + z4 * k(N[4, 4])
            inside = (
                e34 - o34,
                e34 + o34,
                a0 + z1 * k(N[5, 1]) + z3 * k(N[5, 3]) + z5 * k(N[5, 5]),
            )
            H = [relaxed(forms, n, row, c, vel, nu_cols[n], inside[n]) for n in range(3)]
            value = moved + (H[0] + H[1] + H[2]) * k(V[0, 3])
            centre[at(row, c)] = value
            mtbl[pl.ds(row * chunks + c, SUB, stride=chunks), :] = value
            for n in range(3):
                high[(n, *at(row, c))] = H[n]

    pipelined_groups(elems, (stage_a, stage_b), fetch, compute)

    def take(row):
        for place, side in enumerate(sides(info)):
            for i in range(SUB):
                copy_rows(mtbl, stage, offsets[2 + side, row + i], (place * slots + row + i) * chunks, chunks)

    over_groups(slots, take)

    def pack(row):
        for place, out in enumerate((near, far)):
            for c in range(chunks):
                start = (place * slots + row) * chunks + c
                out[at(row, c)] = stage[pl.ds(start, SUB, stride=chunks), :]

    over_groups(slots, pack)


def rest_kernel(src, info, tbl0, _, z_ref, own, near, far, high, spreads, nus, basis, cols, *refs, section):
    tbl, out, sizes, stage_a, stage_b, *forms = refs
    elems, vel = z_ref.shape[1:]
    chunks = vel // LANE
    pitch = 3 * chunks
    slots = near.shape[1]
    faces = 3 * elems

    def fill_border(row):
        for side, halo in zip(sides(info), (near, far)):
            for level in range(2):
                for c in range(chunks):
                    start = ((faces + side * slots + row) * 2 + level) * chunks + c
                    tbl[pl.ds(start, SUB, stride=2 * chunks), :] = halo[(level + 1, *at(row, c))]

    over_groups(slots, fill_border)

    for i in range(3):
        forms[i][...] = jnp.dot(
            spreads[i], basis[:, pl.ds(0, 3 * vel)], preferred_element_type=f32
        )
    N, V = NODAL, INVERSE
    grid = chunk_grid(info[0], chunks)

    def fetch(row, stage):
        for m in range(3):
            for i in range(SUB):
                start = src[m, row + i]
                to = (m * SUB + i) * pitch
                copy_rows(tbl0, stage, start, to, chunks)
                copy_rows(tbl, stage, 2 * start, to + chunks, 2 * chunks)

    def compute(row, stage):
        flows = flow_forms(cols, grid, row, section == 1)
        nu_cols = [nus[n, pl.ds(row, SUB), :] for n in range(3)]
        for c in range(chunks):
            z = modes_at(z_ref, row, c)
            z0, z1, z2, z3, z4, z5 = z

            def beside(m, level):
                return stage[pl.ds(m * SUB * pitch + level * chunks + c, SUB, stride=pitch), :]

            in0, in1, in2 = [jnp.maximum(g, 0.0) for g in flows[c]]
            V_in = [in0 * beside(0, i) for i in range(3)]
            W_in = [in1 * beside(1, 0), -(in1 * beside(1, 1)), in1 * beside(1, 2)]
            X_in = [in2 * beside(2, i) for i in range(3)]
            surface = lifted(V_in, W_in, X_in)
            moved = [own[(j + 1, *at(row, c))] + surface[j + 1] for j in range(5)]
            a0 = z0 * k(N[0, 0])
            e02 = a0 + z1 * k(N[0, 1]) + z3 * k(N[0, 3]) + z5 * k(N[0, 5])
            o02 = z2 * k(N[2, 2]) + z4 * k(N[2, 4])
            inside = (e02 - o02, a0 + z1 * k(N[1, 1]) + z3 * k(N[1, 3]), e02 + o02)
            H = [relaxed(forms, n, row, c, vel, nu_cols[n], inside[n]) for n in range(3)]
            H += [high[(n, *at(row, c))] for n in range(3)]
            s02 = H[0] + H[2]
            d20 = H[2] - H[0]
            s34 = H[3] + H[4]
            d43 = H[4] - H[3]
            change = (
                s02 * k(V[1, 0]) + H[1] * k(V[1, 1]) + s34 * k(V[1, 3]) + H[5] * k(V[1, 5]),
                d20 * k(V[2, 2]) + d43 * k(V[2, 4]),
                (s02 + H[5]) * k(V[3, 0]) + (H[1] - s34) * k(V[3, 1]),
                d20 * k(V[4, 2]) + d43 * k(V[4, 4]),
                s02 * k(V[5, 0]) + H[5] * k(V[5, 5]),
            )
            z = [moved[j] + change[j] for j in range(5)]
            for j in range(5):
                out[(j, *at(row, c))] = z[j]
            size1 = jnp.abs(z[0])
            size2 = jnp.abs(z[1])
            size4 = jnp.abs(z[3])
            linear = None
            quadric = None
            for m, q in ((0, 0), (0, 1), (0, 2), (2, 0), (2, 1)):
                t = TR[m, q]
                if q != 1:
                    value = size1 * k(abs(t[1])) + size2 * k(abs(t[2]))
                    linear = value if linear is None else jnp.maximum(linear, value)
                value = jnp.abs(z[2] * k(t[3]) + z[4] * k(t[5]))
                if abs(t[4]) > 1e-9:
                    value = value + size4 * k(abs(t[4]))
                quadric = value if quadric is None else jnp.maximum(quadric, value)
            linear = jnp.maximum(linear, slope_floor)
            quadric = jnp.maximum(quadric, slope_floor)
            over = k(math.sqrt(2.0)) / (linear * quadric)
            sizes[(0, *at(row, c))] = over * quadric
            sizes[(1, *at(row, c))] = over * linear

    pipelined_groups(elems, (stage_a, stage_b), fetch, compute)


def limit_kernel(away, info, _, centre, rest, sizes, near, far, mtbl, out, *refs, section):
    if section == 0:
        mom, stage_a, stage_b = refs
        target = out
    else:
        stage_a, stage_b, target, sems = refs
    elems, vel = centre.shape
    chunks = vel // LANE
    slots = near.shape[0]

    def fill_border(row):
        for side, halo in zip(sides(info), (near, far)):
            for c in range(chunks):
                start = (elems + side * slots + row) * chunks + c
                mtbl[pl.ds(start, SUB, stride=chunks), :] = halo[at(row, c)]

    over_groups(slots, fill_border)

    def fetch(row, stage):
        for m in range(3):
            for i in range(SUB):
                copy_rows(mtbl, stage, away[m, row + i], (m * SUB + i) * chunks, chunks)

    def compute(row, stage):
        for c in range(chunks):
            z0 = centre[at(row, c)]
            gaps = [
                jnp.abs(stage[pl.ds(m * SUB * chunks + c, SUB, stride=chunks), :] - z0) for m in range(3)
            ]
            gap = jnp.maximum(jnp.maximum(gaps[0], gaps[1]), gaps[2])
            theta1 = jnp.minimum(1.0, gap * sizes[(0, *at(row, c))])
            theta2 = jnp.minimum(theta1, gap * sizes[(1, *at(row, c))])
            target[(0, *at(row, c))] = z0
            for j in range(1, MODES):
                target[(j, *at(row, c))] = rest[(j - 1, *at(row, c))] * (theta1 if j < 3 else theta2)

    if section == 0:
        pipelined_groups(elems, (stage_a, stage_b), fetch, compute)
        weights = weight_rows(info[0], vel)
        for j in range(MODES):
            mom[pl.ds(j * SUB, SUB), :] = mode_moments(weights, target[j])
    else:
        pieces = sems.shape[0]
        size = elems // pieces
        copies = []
        for piece in range(pieces):
            begin = piece * size

            def fetch_piece(row, stage, begin=begin):
                fetch(row + begin, stage)

            def compute_piece(row, stage, begin=begin):
                compute(pl.multiple_of(row + begin, SUB), stage)

            pipelined_groups(size, (stage_a, stage_b), fetch_piece, compute_piece)
            part = pl.ds(begin, size)
            copy = pltpu.make_async_copy(target.at[:, part, :], out.at[:, part, :], sems.at[piece])
            copy.start()
            copies.append(copy)
        for copy in copies:
            copy.wait()


def traded(value, near):
    peers = lax.axis_size("space")
    pairs = []
    for i in range(0 if near else 1, peers - 1, 2):
        pairs += [(i, i + 1), (i + 1, i)]
    return lax.ppermute(value, "space", pairs)


def swapped(value, bits):
    peers = lax.axis_size("vel")
    return lax.ppermute(value, "vel", [(i, i ^ bits) for i in range(peers)])


def moment_parts(paired):
    peers = lax.axis_size("vel")
    done = 2
    while True:
        width = min(4, peers // done)
        parts = [paired] + [swapped(paired, bits * done) for bits in range(1, width)]
        done *= width
        if done >= peers:
            return parts
        paired = sum(parts[1:], parts[0])


def on_device(distribution, corners, neighbour, boundary_faces, collision_rate):
    modes, elems, vel = distribution.shape
    chunks = vel // LANE
    slots = boundary_faces.shape[2]
    lists = boundary_faces[0]
    info = jnp.stack([lax.axis_index("vel") * vel, lax.axis_index("space") % 2]).astype(jnp.int32)
    faces = 3 * elems
    rows = faces + 2 * slots
    S = jax.ShapeDtypeStruct
    state = S((modes, elems, vel), f32)
    one = S((slots, vel), f32)
    halo = S((3, slots, vel), f32)
    mom = S((modes * SUB, elems), f32)
    smem = pl.BlockSpec(memory_space=pltpu.SMEM)
    vmem = pl.BlockSpec(memory_space=pltpu.VMEM)
    hbm = pl.BlockSpec(memory_space=pltpu.HBM)

    def params(mib):
        return pltpu.CompilerParams(vmem_limit_bytes=mib << 20)

    def buffer(count):
        return pltpu.VMEM((count, LANE), f32)

    def evaluated():
        return [pltpu.VMEM((elems, 3 * vel), f32) for _ in range(3)]

    rate = collision_rate.reshape(1, elems)
    index = S(neighbour.shape, jnp.int32)
    src, away, offsets, basis, cols = pl.pallas_call(
        prepare_kernel,
        out_shape=(
            index,
            index,
            S((4, slots), jnp.int32),
            S((TERMS * SUB, modes * vel), bf16),
            S((4, elems, LANE), f32),
        ),
        in_specs=[smem, smem] + [vmem] * 3,
        out_specs=(vmem,) * 5,
        compiler_params=params(8),
        name="prepare",
    )(lists, info, neighbour, lists, corners.transpose(1, 0, 2))

    current = start = distribution
    partial = pl.pallas_call(
        first_kernel,
        out_shape=mom,
        in_specs=[smem, vmem],
        out_specs=vmem,
        compiler_params=params(8),
        name="first",
    )(info, current)

    for section in range(2):
        opening = section == 0
        paired = partial + swapped(partial, 1)
        tbl0, tbl12, near, far = pl.pallas_call(
            trace_kernel,
            out_shape=(S((rows * chunks, LANE), f32), S((2 * rows * chunks, LANE), f32), halo, halo),
            in_specs=[smem, smem, vmem],
            out_specs=(vmem,) * 4,
            scratch_shapes=[buffer(2 * slots * chunks), buffer(4 * slots * chunks)],
            compiler_params=params(8),
            name="trace",
        )(offsets, info, current)
        near, far, paired = lax.optimization_barrier((near, far, paired))
        near = traded(near, True)
        far = traded(far, False)
        parts = moment_parts(paired)

        base = [] if opening else [start]
        own = pl.pallas_call(
            lambda *refs, section=section: own_kernel(*refs, section=section),
            out_shape=state,
            in_specs=[smem] + [vmem] * (2 + len(base)),
            out_specs=vmem,
            compiler_params=params(4),
            name=f"own{section}",
        )(info, current, cols, *base)
        spreads, nus, *forms = pl.pallas_call(
            lambda *refs, section=section: form_kernel(*refs, parts=len(parts), section=section),
            out_shape=(S((3, elems, TERMS * SUB), bf16), S((modes, elems, LANE), f32)) + (S((elems, 3 * vel), f32),) * 3,
            in_specs=[vmem] * (len(parts) + 2),
            out_specs=(vmem,) * 5,
            compiler_params=params(16),
            name=f"form{section}",
        )(*parts, rate, basis)

        tbl0, mean_table, centre, high, near_mean, far_mean = pl.pallas_call(
            lambda *refs, section=section: mean_kernel(*refs, section=section),
            out_shape=(
                S((rows * chunks, LANE), f32),
                S(((elems + 2 * slots) * chunks, LANE), f32),
                S((elems, vel), f32),
                S((3, elems, vel), f32),
                one,
                one,
            ),
            input_output_aliases={3: 0},
            in_specs=[smem] * 3 + [vmem] * 10,
            out_specs=(vmem,) * 6,
            scratch_shapes=[buffer(3 * SUB * chunks)] * 2 + [buffer(2 * slots * chunks)],
            compiler_params=params(16),
            name=f"mean{section}",
        )(offsets, src, info, tbl0, current, own, near, far, cols, nus, *forms)
        near_mean = traded(near_mean, True)
        far_mean = traded(far_mean, False)

        _, rest, sizes = pl.pallas_call(
            lambda *refs, section=section: rest_kernel(*refs, section=section),
            out_shape=(S((2 * rows * chunks, LANE), f32), S((5, elems, vel), f32), S((2, elems, vel), f32)),
            input_output_aliases={3: 0},
            in_specs=[smem] * 2 + [vmem] * 11,
            out_specs=(vmem,) * 3,
            scratch_shapes=[buffer(9 * SUB * chunks)] * 2 + evaluated(),
            compiler_params=params(20),
            name=f"rest{section}",
        )(src, info, tbl0, tbl12, current, own, near, far, high, spreads, nus, basis, cols)

        scratch = [buffer(3 * SUB * chunks)] * 2
        if not opening:
            scratch += [pltpu.VMEM(state.shape, f32), pltpu.SemaphoreType.DMA((4,))]
        made = pl.pallas_call(
            lambda *refs, section=section: limit_kernel(*refs, section=section),
            out_shape=(S(mean_table.shape, f32), state) + ((mom,) if opening else ()),
            in_specs=[smem, smem] + [vmem] * 6,
            out_specs=(vmem,) * 3 if opening else (vmem, hbm),
            input_output_aliases={2: 0},
            scratch_shapes=scratch,
            compiler_params=params(8),
            name=f"limit{section}",
        )(away, info, mean_table, centre, rest, sizes, near_mean, far_mean)
        if opening:
            _, current, partial = made
    return made[1]


def solution(mesh):
    in_specs = (
        P(None, "space", "vel"),
        P(None, None, "space"),
        P(None, "space"),
        P("space", None, None),
        P("space"),
    )
    return jax.shard_map(
        on_device, mesh=mesh, in_specs=in_specs, out_specs=P(None, "space", "vel"), check_vma=False
    )
```

```python
import math

import jax
import jax.numpy as jnp
import numpy as np
from jax import lax
from jax.experimental import pallas as pl
from jax.experimental.pallas import tpu as pltpu
from jax.sharding import PartitionSpec as P

VGRID = 64
velocity_limit = 6.0
time_step = 0.012
viscous_conductive_ratio = 2.0 / 3.0
density_floor = 0.1
kelvin_lower_limit = 0.2
skew_multiplier_limit = 0.9
slope_floor = 0.01

LANE = 128
SUB = 8
MODES = 6
TERMS = 32
f32 = jnp.float32
bf16 = jnp.bfloat16


def monomial_integral(power_r, power_s):
    return math.factorial(power_r) * math.factorial(power_s) / math.factorial(power_r + power_s + 2)


def dg_tables():
    powers = [(0, 0), (1, 0), (0, 1), (2, 0), (1, 1), (0, 2)]
    gram = np.array(
        [[monomial_integral(a[0] + b[0], a[1] + b[1]) for b in powers] for a in powers]
    )
    coeffs = np.linalg.inv(np.linalg.cholesky(gram))
    deriv_r = np.zeros((6, 6))
    deriv_s = np.zeros((6, 6))
    for i, a in enumerate(powers):
        for j, b in enumerate(powers):
            if a[0] > 0:
                deriv_r[i, j] = a[0] * monomial_integral(a[0] - 1 + b[0], a[1] + b[1])
            if a[1] > 0:
                deriv_s[i, j] = a[1] * monomial_integral(a[0] + b[0], a[1] - 1 + b[1])
    stiff_r = coeffs @ deriv_r @ coeffs.T
    stiff_s = coeffs @ deriv_s @ coeffs.T

    def evaluate(location):
        return coeffs @ np.array([location[0] ** p[0] * location[1] ** p[1] for p in powers])

    vertices = np.array([[0.0, 0.0], [1.0, 0.0], [0.0, 1.0]])
    offset = math.sqrt(0.15)
    positions = np.array([0.5 - offset, 0.5, 0.5 + offset])
    weights = np.array([5.0, 8.0, 5.0]) / 18.0
    traces = np.zeros((3, 3, 6))
    for m in range(3):
        for q in range(3):
            along = positions[q]
            traces[m, q] = evaluate((1.0 - along) * vertices[m] + along * vertices[(m + 1) % 3])
    legendre = np.stack(
        [
            np.ones(3),
            math.sqrt(3.0) * (2.0 * positions - 1.0),
            math.sqrt(5.0) * (6.0 * positions**2 - 6.0 * positions + 1.0),
        ]
    )
    edge = np.einsum("lq,q,mqj->mlj", legendre, weights, traces)
    node_list = [(0.0, 0.0), (1.0, 0.0), (0.0, 1.0), (0.5, 0.0), (0.5, 0.5), (0.0, 0.5)]
    nodal = np.array([evaluate(np.array(n)) for n in node_list])
    inverse = np.linalg.inv(nodal)
    return stiff_r, stiff_s, traces, edge, nodal, inverse


KR, KS, TR, EDGE, NODAL, INVERSE = dg_tables()


def k(value):
    return float(np.float32(value))


def edge_parts(z):
    z0, z1, z2, z3, z4, z5 = z
    b = EDGE[0]
    a0 = z0 * k(b[0, 0])
    even = (
        a0 + z1 * k(b[0, 1]) + z3 * k(b[0, 3]) + z5 * k(b[0, 5]),
        z1 * k(b[1, 1]) + z3 * k(b[1, 3]) + z5 * k(b[1, 5]),
        z3 * k(b[2, 3]) + z5 * k(b[2, 5]),
    )
    odd = (
        z2 * k(-b[0, 2]) + z4 * k(-b[0, 4]),
        z2 * k(-b[1, 2]) + z4 * k(-b[1, 4]),
        z4 * k(-b[2, 4]),
    )
    c = EDGE[2]
    last = (
        a0 + z1 * k(c[0, 1]) + z3 * k(c[0, 3]),
        z2 * k(c[1, 2]) + z4 * k(c[1, 4]),
        z5 * k(c[2, 5]),
    )
    return even, odd, last


def table_values(z):
    even, odd, last = edge_parts(z)
    return (
        (even[0] - odd[0], odd[1] - even[1], even[2] - odd[2]),
        (even[0] + odd[0], even[1] + odd[1], even[2] + odd[2]),
        (last[0], -last[1], last[2]),
    )


def at(row, chunk):
    return pl.ds(row, SUB), pl.ds(chunk * LANE, LANE)


def modes_at(ref, row, chunk):
    return [ref[(j, *at(row, chunk))] for j in range(ref.shape[0])]


def over_groups(count, body, together=5):
    while count // SUB % together:
        together -= 1

    def step(g, _):
        for i in range(together):
            body(pl.multiple_of(g * (SUB * together) + i * SUB, SUB))
        return 0

    lax.fori_loop(0, count // (SUB * together), step, 0)


def copy_rows(source, target, start, to, count):
    for piece in range(0, count, SUB):
        rows = min(SUB, count - piece)
        target[pl.ds(to + piece, rows), :] = source[pl.ds(start + piece, rows), :]


def pipelined_groups(count, stages, fetch, compute, pairs=4):
    last = count - SUB
    span = 2 * SUB * pairs
    fetch(0, stages[0])

    def step(g, _):
        start = pl.multiple_of(g * span, span)
        for i in range(2 * pairs):
            row = pl.multiple_of(start + i * SUB, SUB)
            after = row + SUB
            if i + 1 == 2 * pairs:
                after = jnp.minimum(after, last)
            fetch(pl.multiple_of(after, SUB), stages[(i + 1) % 2])
            compute(row, stages[i % 2])
        return 0

    lax.fori_loop(0, count // span, step, 0)


def grid_rows(first, shape):
    index = first + lax.broadcasted_iota(jnp.int32, shape, len(shape) - 1)
    spacing = 2.0 * velocity_limit / VGRID
    x = -velocity_limit + ((index // VGRID).astype(f32) + 0.5) * spacing
    y = -velocity_limit + ((index % VGRID).astype(f32) + 0.5) * spacing
    return x, y, spacing


def split3(value):
    high = value.astype(bf16).astype(f32)
    rest = value - high
    middle = rest.astype(bf16).astype(f32)
    return high, middle, (rest - middle).astype(bf16).astype(f32)


def weight_rows(first, vel):
    x, y, spacing = grid_rows(first, (SUB, vel))
    row = lax.broadcasted_iota(jnp.int32, (SUB, vel), 0)
    square = x * x + y * y
    weights = jnp.ones_like(x)
    for index, value in enumerate((x, y, x * x, x * y, y * y, x * square, y * square)):
        weights = jnp.where(row == index + 1, value, weights)
    weights = weights * (spacing * spacing)
    return jnp.concatenate([*split3(weights), jnp.zeros_like(x)], axis=0).astype(bf16)


def mode_moments(weights, value):
    high = value.astype(bf16)
    low = (value - high.astype(f32)).astype(bf16)
    dims = (((1,), (1,)), ((), ()))
    total = lax.dot_general(weights, high, dims, preferred_element_type=f32)
    total = total + lax.dot_general(weights, low, dims, preferred_element_type=f32)
    return total[0:8] + total[8:16] + total[16:24]


def first_kernel(info, z_ref, mom):
    weights = weight_rows(info[0], z_ref.shape[2])
    for j in range(MODES):
        mom[pl.ds(j * SUB, SUB), :] = mode_moments(weights, z_ref[j])


def put_index(neigh_ref, rows_ref, lists, src, away, offsets, elems, chunks):
    slots = rows_ref.shape[1]
    faces = 3 * elems
    shape = neigh_ref.shape
    face = lax.broadcasted_iota(jnp.int32, shape, 0) * elems + lax.broadcasted_iota(jnp.int32, shape, 1)

    def mark(slot, found):
        found = jnp.where(face == lists[0, slot], faces + slot, found)
        return jnp.where(face == lists[1, slot], faces + slots + slot, found)

    found = jnp.maximum(lax.fori_loop(0, slots, mark, neigh_ref[...]), 0)
    src[...] = found * chunks
    away[...] = jnp.where(found < faces, found % elems, found - 2 * elems) * chunks
    known = jnp.maximum(rows_ref[...], 0)
    offsets[pl.ds(0, 2), :] = known * chunks
    offsets[pl.ds(2, 2), :] = known % elems * chunks


def put_columns(rows, out):
    elems = out.shape[1]
    turned = jnp.concatenate([*rows, jnp.zeros((LANE - out.shape[0], elems), f32)], axis=0).T
    for n in range(out.shape[0]):
        out[n] = jnp.broadcast_to(turned[:, n : n + 1], (elems, LANE))


def put_flows(corner, cols):
    cx = [corner[i, 0:1, :] for i in range(3)]
    cy = [corner[i, 1:2, :] for i in range(3)]
    det = (cx[1] - cx[0]) * (cy[2] - cy[0]) - (cx[2] - cx[0]) * (cy[1] - cy[0])
    step = time_step / det
    rows = [-step * (cy[1] - cy[0]), step * (cx[1] - cx[0]), -step * (cy[0] - cy[2]), step * (cx[0] - cx[2])]
    put_columns(rows, cols)


def sides(info):
    parity = info[1]
    return (1 - parity, parity)


def prepare_kernel(lists, info, neigh_ref, rows_ref, corner, src, away, offsets, basis, cols):
    vel = basis.shape[1] // MODES
    put_index(neigh_ref, rows_ref, lists, src, away, offsets, cols.shape[1], vel // LANE)
    put_flows(corner, cols)
    put_basis(info[0], basis, vel)


def trace_kernel(offsets, info, z_ref, tbl0, tbl12, near, far, stage0, stage12):
    elems, vel = z_ref.shape[1:]
    chunks = vel // LANE
    slots = offsets.shape[1]

    def fill(row):
        for c in range(chunks):
            for m, values in enumerate(table_values(modes_at(z_ref, row, c))):
                start = (m * elems + row) * chunks + c
                tbl0[pl.ds(start, SUB, stride=chunks), :] = values[0]
                for level in (1, 2):
                    start = ((m * elems + row) * 2 + level - 1) * chunks + c
                    tbl12[pl.ds(start, SUB, stride=2 * chunks), :] = values[level]

    over_groups(elems, fill, 2)

    def take(row):
        for place, side in enumerate(sides(info)):
            for i in range(SUB):
                start = offsets[side, row + i]
                to = (place * slots + row + i) * chunks
                copy_rows(tbl0, stage0, start, to, chunks)
                copy_rows(tbl12, stage12, 2 * start, 2 * to, 2 * chunks)

    over_groups(slots, take)

    def pack(row):
        for place, out in enumerate((near, far)):
            for c in range(chunks):
                start = (place * slots + row) * chunks
                out[(0, *at(row, c))] = stage0[pl.ds(start + c, SUB, stride=chunks), :]
                for level in range(2):
                    out[(level + 1, *at(row, c))] = stage12[
                        pl.ds(2 * start + level * chunks + c, SUB, stride=2 * chunks), :
                    ]

    over_groups(slots, pack)


def flow_forms(cols, grid, row, half=False):
    col = [cols[n, pl.ds(row, SUB), :] for n in range(4)]
    if half:
        col = [0.5 * value for value in col]
    flows = []
    for x, y in grid:
        g0 = col[0] * x + col[1] * y
        g2 = col[2] * x + col[3] * y
        flows.append((g0, -(g0 + g2), g2))
    return flows


def chunk_grid(first, chunks):
    return [grid_rows(first + c * LANE, (1, LANE))[:2] for c in range(chunks)]


def put_basis(first, basis, vel):
    x, y, _ = grid_rows(first, (1, vel))
    xx = x * x
    yy = y * y
    xx_high = xx.astype(bf16).astype(f32)
    yy_high = yy.astype(bf16).astype(f32)
    monomials = (jnp.ones_like(x), x, y, xx_high, xx - xx_high, yy_high, yy - yy_high)
    row = lax.broadcasted_iota(jnp.int32, (SUB, vel), 0)
    zero = jnp.zeros((SUB, vel), f32)
    for n in range(MODES):
        mine = row == n
        for pair in range(TERMS // 2):
            halves = []
            for term in (2 * pair, 2 * pair + 1):
                which = term // 3
                halves.append(jnp.where(mine, monomials[which], 0.0) if which < len(monomials) else zero)
            basis[pl.ds(pair * 2 * SUB, 2 * SUB), pl.ds(n * vel, vel)] = jnp.concatenate(
                halves, axis=0
            ).astype(bf16)


def node_parameters(mom, rate, elems, scale):
    shape = (SUB, elems)
    row = lax.broadcasted_iota(jnp.int32, shape, 0)

    def column(values):
        out = jnp.full(shape, k(values[0]), f32)
        for n in range(1, MODES):
            out = jnp.where(row == n, k(values[n]), out)
        return out

    columns = [column(NODAL[:, j]) for j in range(MODES)]
    R = []
    for index in range(8):
        total = columns[0] * mom[index : index + 1, :]
        for j in range(1, MODES):
            total = total + columns[j] * mom[j * SUB + index : j * SUB + index + 1, :]
        R.append(total)
    zeroth, mass_x, mass_y, flux_xx, flux_xy, flux_yy, third_x, third_y = R
    density = jnp.maximum(zeroth, density_floor)
    ux = mass_x / density
    uy = mass_y / density
    drift_sq = ux * ux + uy * uy
    drift_mass = ux * mass_x + uy * mass_y
    trace = flux_xx + flux_yy
    kelvin = jnp.maximum(
        (trace - 2.0 * drift_mass + drift_sq * zeroth) / (2.0 * density), kelvin_lower_limit
    )
    qx = 0.5 * (
        third_x
        - 2.0 * (flux_xx * ux + flux_xy * uy)
        + mass_x * drift_sq
        - ux * trace
        + 2.0 * ux * drift_mass
        - ux * drift_sq * zeroth
    )
    qy = 0.5 * (
        third_y
        - 2.0 * (flux_xy * ux + flux_yy * uy)
        + mass_y * drift_sq
        - uy * trace
        + 2.0 * uy * drift_mass
        - uy * drift_sq * zeroth
    )
    nu = scale * rate * density
    over = 1.0 / kelvin
    weight = (1.0 - viscous_conductive_ratio) / (4.0 * density * kelvin * kelvin)
    qx = qx * weight
    qy = qy * weight
    excess = (over * drift_sq - 4.0, -2.0 * over * ux, -2.0 * over * uy, over, over)
    amplitude = jnp.log(nu * density * over * k(1.0 / (2.0 * math.pi)))
    exponent = (
        amplitude - 0.5 * over * drift_sq,
        over * ux,
        over * uy,
        -0.5 * over,
        -0.5 * over,
    )
    skew = (-(qx * ux + qy * uy), qx, qy)
    return nu, (excess, exponent, skew)


def spread(form, elems):
    pieces = []
    for index, value in enumerate(form):
        parts = split3(value)
        pieces += parts
        if index >= 3:
            pieces += parts
    pieces.append(jnp.zeros((TERMS * SUB - SUB * len(pieces), elems), f32))
    return jnp.concatenate(pieces, axis=0).T.astype(bf16)


def relaxed(forms, slot, row, chunk, vel, nu, inside):
    def form(i):
        return forms[i][pl.ds(row, SUB), pl.ds(slot * vel + chunk * LANE, LANE)]

    skewed = jnp.minimum(jnp.maximum(form(2) * form(0), -skew_multiplier_limit), skew_multiplier_limit)
    return jnp.exp(form(1)) * (1.0 + skewed) - nu * inside


def form_kernel(*refs, parts, section):
    mom_refs = refs[:parts]
    rate, basis, spreads, nus, *forms = refs[parts:]
    elems = rate.shape[1]
    half = basis.shape[1] // 2
    scale = time_step if section == 0 else 0.5 * time_step
    moments = mom_refs[0][...]
    for ref in mom_refs[1:]:
        moments = moments + ref[...]
    nu, coefficients = node_parameters(moments, rate[...], elems, scale)
    put_columns([nu[n : n + 1, :] for n in range(MODES)], nus)
    for i, form in enumerate(coefficients):
        spreads[i] = spread(form, elems)
        forms[i][...] = jnp.dot(spreads[i], basis[:, pl.ds(half, half)], preferred_element_type=f32)


def lifted(V, W, X):
    B0, B2 = EDGE[0], EDGE[2]
    S = [a + b for a, b in zip(V, W)]
    D = [b - a for a, b in zip(V, W)]
    return (
        (S[0] + X[0]) * k(B0[0, 0]),
        S[0] * k(B0[0, 1]) + S[1] * k(B0[1, 1]) + X[0] * k(B2[0, 1]),
        D[0] * k(-B0[0, 2]) + D[1] * k(-B0[1, 2]) + X[1] * k(B2[1, 2]),
        S[0] * k(B0[0, 3]) + S[1] * k(B0[1, 3]) + S[2] * k(B0[2, 3]) + X[0] * k(B2[0, 3]),
        D[0] * k(-B0[0, 4]) + D[1] * k(-B0[1, 4]) + D[2] * k(-B0[2, 4]) + X[1] * k(B2[1, 4]),
        S[0] * k(B0[0, 5]) + S[1] * k(B0[1, 5]) + S[2] * k(B0[2, 5]) + X[2] * k(B2[2, 5]),
    )


def own_kernel(info, z_ref, cols, *refs, section):
    if section == 1:
        base_ref, out = refs
    else:
        (out,) = refs
    elems, vel = z_ref.shape[1:]
    chunks = vel // LANE
    grid = chunk_grid(info[0], chunks)

    def compute(row):
        flows = flow_forms(cols, grid, row)
        for c in range(chunks):
            z = modes_at(z_ref, row, c)
            z0, z1, z2, z3, z4, z5 = z
            even, odd, last = edge_parts(z)
            gs, g1, gr = flows[c]
            out0, out1, out2 = [jnp.minimum(g, 0.0) for g in flows[c]]
            V = [out0 * (even[i] - odd[i]) for i in range(3)]
            W = [out1 * (even[i] + odd[i]) for i in range(3)]
            X = [out2 * last[i] for i in range(3)]
            h = gr + 2.0 * gs
            volume = (
                None,
                (gr * z0) * k(KR[1, 0]),
                (h * z0) * k(KR[2, 0]),
                gr * (z0 * k(KR[3, 0]) + z1 * k(KR[3, 1])),
                h * (z0 * k(KR[4, 0]) + z1 * k(KR[4, 1])) + gr * (z2 * k(KR[4, 2])),
                gr * (z0 * k(KR[5, 0]) + z1 * k(KR[5, 1])) + h * (z2 * k(KR[5, 2])),
            )
            surface = lifted(V, W, X)
            for j in range(MODES):
                value = z[j] + surface[j]
                if j:
                    value = value + volume[j]
                if section == 1:
                    value = 0.5 * (base_ref[(j, *at(row, c))] + value)
                out[(j, *at(row, c))] = value

    over_groups(elems, compute, 2)


def mean_kernel(offsets, src, info, _, z_ref, own, near_in, far_in, cols, nus, *refs, section):
    forms = refs[:3]
    refs = refs[3:]
    tbl, mtbl, centre, high, near, far, stage_a, stage_b, stage = refs
    elems, vel = z_ref.shape[1:]
    chunks = vel // LANE
    slots = offsets.shape[1]
    faces = 3 * elems

    def fill_border(row):
        for side, halo in zip(sides(info), (near_in, far_in)):
            for c in range(chunks):
                start = (faces + side * slots + row) * chunks + c
                tbl[pl.ds(start, SUB, stride=chunks), :] = halo[(0, *at(row, c))]

    over_groups(slots, fill_border)

    N, V = NODAL, INVERSE
    grid = chunk_grid(info[0], chunks)

    def fetch(row, stage):
        for m in range(3):
            for i in range(SUB):
                copy_rows(tbl, stage, src[m, row + i], (m * SUB + i) * chunks, chunks)

    def compute(row, stage):
        flows = flow_forms(cols, grid, row, section == 1)
        nu_cols = [nus[n, pl.ds(row, SUB), :] for n in range(3, MODES)]
        for c in range(chunks):
            z0, z1, z2, z3, z4, z5 = modes_at(z_ref, row, c)
            through = None
            for m in range(3):
                value = jnp.maximum(flows[c][m], 0.0) * stage[
                    pl.ds(m * SUB * chunks + c, SUB, stride=chunks), :
                ]
                through = value if through is None else through + value
            moved = own[(0, *at(row, c))] + through * k(EDGE[0, 0, 0])
            a0 = z0 * k(N[0, 0])
            e34 = a0 + z1 * k(N[3, 1]) + z3 * k(N[3, 3]) + z5 * k(N[3, 5])
            o34 = z2 * k(N[4, 2]) + z4 * k(N[4, 4])
            inside = (
                e34 - o34,
                e34 + o34,
                a0 + z1 * k(N[5, 1]) + z3 * k(N[5, 3]) + z5 * k(N[5, 5]),
            )
            H = [relaxed(forms, n, row, c, vel, nu_cols[n], inside[n]) for n in range(3)]
            value = moved + (H[0] + H[1] + H[2]) * k(V[0, 3])
            centre[at(row, c)] = value
            mtbl[pl.ds(row * chunks + c, SUB, stride=chunks), :] = value
            for n in range(3):
                high[(n, *at(row, c))] = H[n]

    pipelined_groups(elems, (stage_a, stage_b), fetch, compute)

    def take(row):
        for place, side in enumerate(sides(info)):
            for i in range(SUB):
                copy_rows(mtbl, stage, offsets[2 + side, row + i], (place * slots + row + i) * chunks, chunks)

    over_groups(slots, take)

    def pack(row):
        for place, out in enumerate((near, far)):
            for c in range(chunks):
                start = (place * slots + row) * chunks + c
                out[at(row, c)] = stage[pl.ds(start, SUB, stride=chunks), :]

    over_groups(slots, pack)


def rest_kernel(src, info, tbl0, _, z_ref, own, near, far, high, spreads, nus, basis, cols, *refs, section):
    tbl, out, sizes, stage_a, stage_b, *forms = refs
    elems, vel = z_ref.shape[1:]
    chunks = vel // LANE
    pitch = 3 * chunks
    slots = near.shape[1]
    faces = 3 * elems

    def fill_border(row):
        for side, halo in zip(sides(info), (near, far)):
            for level in range(2):
                for c in range(chunks):
                    start = ((faces + side * slots + row) * 2 + level) * chunks + c
                    tbl[pl.ds(start, SUB, stride=2 * chunks), :] = halo[(level + 1, *at(row, c))]

    over_groups(slots, fill_border)

    for i in range(3):
        forms[i][...] = jnp.dot(
            spreads[i], basis[:, pl.ds(0, 3 * vel)], preferred_element_type=f32
        )
    N, V = NODAL, INVERSE
    grid = chunk_grid(info[0], chunks)

    def fetch(row, stage):
        for m in range(3):
            for i in range(SUB):
                start = src[m, row + i]
                to = (m * SUB + i) * pitch
                copy_rows(tbl0, stage, start, to, chunks)
                copy_rows(tbl, stage, 2 * start, to + chunks, 2 * chunks)

    def compute(row, stage):
        flows = flow_forms(cols, grid, row, section == 1)
        nu_cols = [nus[n, pl.ds(row, SUB), :] for n in range(3)]
        for c in range(chunks):
            z = modes_at(z_ref, row, c)
            z0, z1, z2, z3, z4, z5 = z

            def beside(m, level):
                return stage[pl.ds(m * SUB * pitch + level * chunks + c, SUB, stride=pitch), :]

            in0, in1, in2 = [jnp.maximum(g, 0.0) for g in flows[c]]
            V_in = [in0 * beside(0, i) for i in range(3)]
            W_in = [in1 * beside(1, 0), -(in1 * beside(1, 1)), in1 * beside(1, 2)]
            X_in = [in2 * beside(2, i) for i in range(3)]
            surface = lifted(V_in, W_in, X_in)
            moved = [own[(j + 1, *at(row, c))] + surface[j + 1] for j in range(5)]
            a0 = z0 * k(N[0, 0])
            e02 = a0 + z1 * k(N[0, 1]) + z3 * k(N[0, 3]) + z5 * k(N[0, 5])
            o02 = z2 * k(N[2, 2]) + z4 * k(N[2, 4])
            inside = (e02 - o02, a0 + z1 * k(N[1, 1]) + z3 * k(N[1, 3]), e02 + o02)
            H = [relaxed(forms, n, row, c, vel, nu_cols[n], inside[n]) for n in range(3)]
            H += [high[(n, *at(row, c))] for n in range(3)]
            s02 = H[0] + H[2]
            d20 = H[2] - H[0]
            s34 = H[3] + H[4]
            d43 = H[4] - H[3]
            change = (
                s02 * k(V[1, 0]) + H[1] * k(V[1, 1]) + s34 * k(V[1, 3]) + H[5] * k(V[1, 5]),
                d20 * k(V[2, 2]) + d43 * k(V[2, 4]),
                (s02 + H[5]) * k(V[3, 0]) + (H[1] - s34) * k(V[3, 1]),
                d20 * k(V[4, 2]) + d43 * k(V[4, 4]),
                s02 * k(V[5, 0]) + H[5] * k(V[5, 5]),
            )
            z = [moved[j] + change[j] for j in range(5)]
            for j in range(5):
                out[(j, *at(row, c))] = z[j]
            size1 = jnp.abs(z[0])
            size2 = jnp.abs(z[1])
            size4 = jnp.abs(z[3])
            linear = None
            quadric = None
            for m, q in ((0, 0), (0, 1), (0, 2), (2, 0), (2, 1)):
                t = TR[m, q]
                if q != 1:
                    value = size1 * k(abs(t[1])) + size2 * k(abs(t[2]))
                    linear = value if linear is None else jnp.maximum(linear, value)
                value = jnp.abs(z[2] * k(t[3]) + z[4] * k(t[5]))
                if abs(t[4]) > 1e-9:
                    value = value + size4 * k(abs(t[4]))
                quadric = value if quadric is None else jnp.maximum(quadric, value)
            linear = jnp.maximum(linear, slope_floor)
            quadric = jnp.maximum(quadric, slope_floor)
            over = k(math.sqrt(2.0)) / (linear * quadric)
            sizes[(0, *at(row, c))] = over * quadric
            sizes[(1, *at(row, c))] = over * linear

    pipelined_groups(elems, (stage_a, stage_b), fetch, compute)


def limit_kernel(away, info, _, centre, rest, sizes, near, far, mtbl, out, *refs, section):
    if section == 0:
        mom, stage_a, stage_b = refs
        target = out
    else:
        stage_a, stage_b, target, sems = refs
    elems, vel = centre.shape
    chunks = vel // LANE
    slots = near.shape[0]

    def fill_border(row):
        for side, halo in zip(sides(info), (near, far)):
            for c in range(chunks):
                start = (elems + side * slots + row) * chunks + c
                mtbl[pl.ds(start, SUB, stride=chunks), :] = halo[at(row, c)]

    over_groups(slots, fill_border)

    def fetch(row, stage):
        for m in range(3):
            for i in range(SUB):
                copy_rows(mtbl, stage, away[m, row + i], (m * SUB + i) * chunks, chunks)

    def compute(row, stage):
        for c in range(chunks):
            z0 = centre[at(row, c)]
            gaps = [
                jnp.abs(stage[pl.ds(m * SUB * chunks + c, SUB, stride=chunks), :] - z0) for m in range(3)
            ]
            gap = jnp.maximum(jnp.maximum(gaps[0], gaps[1]), gaps[2])
            theta1 = jnp.minimum(1.0, gap * sizes[(0, *at(row, c))])
            theta2 = jnp.minimum(theta1, gap * sizes[(1, *at(row, c))])
            target[(0, *at(row, c))] = z0
            for j in range(1, MODES):
                target[(j, *at(row, c))] = rest[(j - 1, *at(row, c))] * (theta1 if j < 3 else theta2)

    if section == 0:
        pipelined_groups(elems, (stage_a, stage_b), fetch, compute)
        weights = weight_rows(info[0], vel)
        for j in range(MODES):
            mom[pl.ds(j * SUB, SUB), :] = mode_moments(weights, target[j])
    else:
        pieces = sems.shape[0]
        size = elems // pieces
        copies = []
        for piece in range(pieces):
            begin = piece * size

            def fetch_piece(row, stage, begin=begin):
                fetch(row + begin, stage)

            def compute_piece(row, stage, begin=begin):
                compute(pl.multiple_of(row + begin, SUB), stage)

            pipelined_groups(size, (stage_a, stage_b), fetch_piece, compute_piece, 2)
            part = pl.ds(begin, size)
            copy = pltpu.make_async_copy(target.at[:, part, :], out.at[:, part, :], sems.at[piece])
            copy.start()
            copies.append(copy)
        for copy in copies:
            copy.wait()


def traded(value, near):
    peers = lax.axis_size("space")
    pairs = []
    for i in range(0 if near else 1, peers - 1, 2):
        pairs += [(i, i + 1), (i + 1, i)]
    return lax.ppermute(value, "space", pairs)


def swapped(value, bits):
    peers = lax.axis_size("vel")
    return lax.ppermute(value, "vel", [(i, i ^ bits) for i in range(peers)])


def moment_parts(paired):
    peers = lax.axis_size("vel")
    done = 2
    while True:
        width = min(4, peers // done)
        parts = [paired] + [swapped(paired, bits * done) for bits in range(1, width)]
        done *= width
        if done >= peers:
            return parts
        paired = sum(parts[1:], parts[0])


def on_device(distribution, corners, neighbour, boundary_faces, collision_rate):
    modes, elems, vel = distribution.shape
    chunks = vel // LANE
    slots = boundary_faces.shape[2]
    lists = boundary_faces[0]
    info = jnp.stack([lax.axis_index("vel") * vel, lax.axis_index("space") % 2]).astype(jnp.int32)
    faces = 3 * elems
    rows = faces + 2 * slots
    S = jax.ShapeDtypeStruct
    state = S((modes, elems, vel), f32)
    one = S((slots, vel), f32)
    halo = S((3, slots, vel), f32)
    mom = S((modes * SUB, elems), f32)
    smem = pl.BlockSpec(memory_space=pltpu.SMEM)
    vmem = pl.BlockSpec(memory_space=pltpu.VMEM)
    hbm = pl.BlockSpec(memory_space=pltpu.HBM)

    def params(mib):
        return pltpu.CompilerParams(vmem_limit_bytes=mib << 20)

    def buffer(count):
        return pltpu.VMEM((count, LANE), f32)

    def evaluated():
        return [pltpu.VMEM((elems, 3 * vel), f32) for _ in range(3)]

    rate = collision_rate.reshape(1, elems)
    index = S(neighbour.shape, jnp.int32)
    src, away, offsets, basis, cols = pl.pallas_call(
        prepare_kernel,
        out_shape=(
            index,
            index,
            S((4, slots), jnp.int32),
            S((TERMS * SUB, modes * vel), bf16),
            S((4, elems, LANE), f32),
        ),
        in_specs=[smem, smem] + [vmem] * 3,
        out_specs=(vmem,) * 5,
        compiler_params=params(8),
        name="prepare",
    )(lists, info, neighbour, lists, corners.transpose(1, 0, 2))

    current = start = distribution
    partial = pl.pallas_call(
        first_kernel,
        out_shape=mom,
        in_specs=[smem, vmem],
        out_specs=vmem,
        compiler_params=params(8),
        name="first",
    )(info, current)

    for section in range(2):
        opening = section == 0
        paired = partial + swapped(partial, 1)
        tbl0, tbl12, near, far = pl.pallas_call(
            trace_kernel,
            out_shape=(S((rows * chunks, LANE), f32), S((2 * rows * chunks, LANE), f32), halo, halo),
            in_specs=[smem, smem, vmem],
            out_specs=(vmem,) * 4,
            scratch_shapes=[buffer(2 * slots * chunks), buffer(4 * slots * chunks)],
            compiler_params=params(8),
            name="trace",
        )(offsets, info, current)
        near, far, paired = lax.optimization_barrier((near, far, paired))
        near = traded(near, True)
        far = traded(far, False)
        parts = moment_parts(paired)

        base = [] if opening else [start]
        own = pl.pallas_call(
            lambda *refs, section=section: own_kernel(*refs, section=section),
            out_shape=state,
            in_specs=[smem] + [vmem] * (2 + len(base)),
            out_specs=vmem,
            compiler_params=params(4),
            name=f"own{section}",
        )(info, current, cols, *base)
        spreads, nus, *forms = pl.pallas_call(
            lambda *refs, section=section: form_kernel(*refs, parts=len(parts), section=section),
            out_shape=(S((3, elems, TERMS * SUB), bf16), S((modes, elems, LANE), f32)) + (S((elems, 3 * vel), f32),) * 3,
            in_specs=[vmem] * (len(parts) + 2),
            out_specs=(vmem,) * 5,
            compiler_params=params(16),
            name=f"form{section}",
        )(*parts, rate, basis)

        tbl0, mean_table, centre, high, near_mean, far_mean = pl.pallas_call(
            lambda *refs, section=section: mean_kernel(*refs, section=section),
            out_shape=(
                S((rows * chunks, LANE), f32),
                S(((elems + 2 * slots) * chunks, LANE), f32),
                S((elems, vel), f32),
                S((3, elems, vel), f32),
                one,
                one,
            ),
            input_output_aliases={3: 0},
            in_specs=[smem] * 3 + [vmem] * 10,
            out_specs=(vmem,) * 6,
            scratch_shapes=[buffer(3 * SUB * chunks)] * 2 + [buffer(2 * slots * chunks)],
            compiler_params=params(16),
            name=f"mean{section}",
        )(offsets, src, info, tbl0, current, own, near, far, cols, nus, *forms)
        near_mean = traded(near_mean, True)
        far_mean = traded(far_mean, False)

        _, rest, sizes = pl.pallas_call(
            lambda *refs, section=section: rest_kernel(*refs, section=section),
            out_shape=(S((2 * rows * chunks, LANE), f32), S((5, elems, vel), f32), S((2, elems, vel), f32)),
            input_output_aliases={3: 0},
            in_specs=[smem] * 2 + [vmem] * 11,
            out_specs=(vmem,) * 3,
            scratch_shapes=[buffer(9 * SUB * chunks)] * 2 + evaluated(),
            compiler_params=params(20),
            name=f"rest{section}",
        )(src, info, tbl0, tbl12, current, own, near, far, high, spreads, nus, basis, cols)

        scratch = [buffer(3 * SUB * chunks)] * 2
        if not opening:
            scratch += [pltpu.VMEM(state.shape, f32), pltpu.SemaphoreType.DMA((4,))]
        made = pl.pallas_call(
            lambda *refs, section=section: limit_kernel(*refs, section=section),
            out_shape=(S(mean_table.shape, f32), state) + ((mom,) if opening else ()),
            in_specs=[smem, smem] + [vmem] * 6,
            out_specs=(vmem,) * 3 if opening else (vmem, hbm),
            input_output_aliases={2: 0},
            scratch_shapes=scratch,
            compiler_params=params(8),
            name=f"limit{section}",
        )(away, info, mean_table, centre, rest, sizes, near_mean, far_mean)
        if opening:
            _, current, partial = made
    return made[1]


def solution(mesh):
    in_specs = (
        P(None, "space", "vel"),
        P(None, None, "space"),
        P(None, "space"),
        P("space", None, None),
        P("space"),
    )
    return jax.shard_map(
        on_device, mesh=mesh, in_specs=in_specs, out_specs=P(None, "space", "vel"), check_vma=False
    )
```

```python
import math

import jax
import jax.numpy as jnp
import numpy as np
from jax import lax
from jax.experimental import pallas as pl
from jax.experimental.pallas import tpu as pltpu
from jax.sharding import PartitionSpec as P

VGRID = 64
velocity_limit = 6.0
time_step = 0.012
viscous_conductive_ratio = 2.0 / 3.0
density_floor = 0.1
kelvin_lower_limit = 0.2
skew_multiplier_limit = 0.9
slope_floor = 0.01

LANE = 128
SUB = 8
MODES = 6
TERMS = 32
f32 = jnp.float32
bf16 = jnp.bfloat16


def monomial_integral(power_r, power_s):
    return math.factorial(power_r) * math.factorial(power_s) / math.factorial(power_r + power_s + 2)


def dg_tables():
    powers = [(0, 0), (1, 0), (0, 1), (2, 0), (1, 1), (0, 2)]
    gram = np.array(
        [[monomial_integral(a[0] + b[0], a[1] + b[1]) for b in powers] for a in powers]
    )
    coeffs = np.linalg.inv(np.linalg.cholesky(gram))
    deriv_r = np.zeros((6, 6))
    deriv_s = np.zeros((6, 6))
    for i, a in enumerate(powers):
        for j, b in enumerate(powers):
            if a[0] > 0:
                deriv_r[i, j] = a[0] * monomial_integral(a[0] - 1 + b[0], a[1] + b[1])
            if a[1] > 0:
                deriv_s[i, j] = a[1] * monomial_integral(a[0] + b[0], a[1] - 1 + b[1])
    stiff_r = coeffs @ deriv_r @ coeffs.T
    stiff_s = coeffs @ deriv_s @ coeffs.T

    def evaluate(location):
        return coeffs @ np.array([location[0] ** p[0] * location[1] ** p[1] for p in powers])

    vertices = np.array([[0.0, 0.0], [1.0, 0.0], [0.0, 1.0]])
    offset = math.sqrt(0.15)
    positions = np.array([0.5 - offset, 0.5, 0.5 + offset])
    weights = np.array([5.0, 8.0, 5.0]) / 18.0
    traces = np.zeros((3, 3, 6))
    for m in range(3):
        for q in range(3):
            along = positions[q]
            traces[m, q] = evaluate((1.0 - along) * vertices[m] + along * vertices[(m + 1) % 3])
    legendre = np.stack(
        [
            np.ones(3),
            math.sqrt(3.0) * (2.0 * positions - 1.0),
            math.sqrt(5.0) * (6.0 * positions**2 - 6.0 * positions + 1.0),
        ]
    )
    edge = np.einsum("lq,q,mqj->mlj", legendre, weights, traces)
    node_list = [(0.0, 0.0), (1.0, 0.0), (0.0, 1.0), (0.5, 0.0), (0.5, 0.5), (0.0, 0.5)]
    nodal = np.array([evaluate(np.array(n)) for n in node_list])
    inverse = np.linalg.inv(nodal)
    return stiff_r, stiff_s, traces, edge, nodal, inverse


KR, KS, TR, EDGE, NODAL, INVERSE = dg_tables()


def k(value):
    return float(np.float32(value))


def edge_parts(z):
    z0, z1, z2, z3, z4, z5 = z
    b = EDGE[0]
    a0 = z0 * k(b[0, 0])
    even = (
        a0 + z1 * k(b[0, 1]) + z3 * k(b[0, 3]) + z5 * k(b[0, 5]),
        z1 * k(b[1, 1]) + z3 * k(b[1, 3]) + z5 * k(b[1, 5]),
        z3 * k(b[2, 3]) + z5 * k(b[2, 5]),
    )
    odd = (
        z2 * k(-b[0, 2]) + z4 * k(-b[0, 4]),
        z2 * k(-b[1, 2]) + z4 * k(-b[1, 4]),
        z4 * k(-b[2, 4]),
    )
    c = EDGE[2]
    last = (
        a0 + z1 * k(c[0, 1]) + z3 * k(c[0, 3]),
        z2 * k(c[1, 2]) + z4 * k(c[1, 4]),
        z5 * k(c[2, 5]),
    )
    return even, odd, last


def table_values(z):
    even, odd, last = edge_parts(z)
    return (
        (even[0] - odd[0], odd[1] - even[1], even[2] - odd[2]),
        (even[0] + odd[0], even[1] + odd[1], even[2] + odd[2]),
        (last[0], -last[1], last[2]),
    )


def at(row, chunk):
    return pl.ds(row, SUB), pl.ds(chunk * LANE, LANE)


def modes_at(ref, row, chunk):
    return [ref[(j, *at(row, chunk))] for j in range(ref.shape[0])]


def over_groups(count, body, together=5):
    while count // SUB % together:
        together -= 1

    def step(g, _):
        for i in range(together):
            body(pl.multiple_of(g * (SUB * together) + i * SUB, SUB))
        return 0

    lax.fori_loop(0, count // (SUB * together), step, 0)


def copy_rows(source, target, start, to, count):
    for piece in range(0, count, SUB):
        rows = min(SUB, count - piece)
        target[pl.ds(to + piece, rows), :] = source[pl.ds(start + piece, rows), :]


def pipelined_groups(count, stages, fetch, compute, pairs=4):
    last = count - SUB
    span = 2 * SUB * pairs
    fetch(0, stages[0])

    def step(g, _):
        start = pl.multiple_of(g * span, span)
        for i in range(2 * pairs):
            row = pl.multiple_of(start + i * SUB, SUB)
            after = row + SUB
            if i + 1 == 2 * pairs:
                after = jnp.minimum(after, last)
            fetch(pl.multiple_of(after, SUB), stages[(i + 1) % 2])
            compute(row, stages[i % 2])
        return 0

    lax.fori_loop(0, count // span, step, 0)


def grid_rows(first, shape):
    index = first + lax.broadcasted_iota(jnp.int32, shape, len(shape) - 1)
    spacing = 2.0 * velocity_limit / VGRID
    x = -velocity_limit + ((index // VGRID).astype(f32) + 0.5) * spacing
    y = -velocity_limit + ((index % VGRID).astype(f32) + 0.5) * spacing
    return x, y, spacing


def split3(value):
    high = value.astype(bf16).astype(f32)
    rest = value - high
    middle = rest.astype(bf16).astype(f32)
    return high, middle, (rest - middle).astype(bf16).astype(f32)


def weight_rows(first, vel):
    x, y, spacing = grid_rows(first, (SUB, vel))
    row = lax.broadcasted_iota(jnp.int32, (SUB, vel), 0)
    square = x * x + y * y
    weights = jnp.ones_like(x)
    for index, value in enumerate((x, y, x * x, x * y, y * y, x * square, y * square)):
        weights = jnp.where(row == index + 1, value, weights)
    weights = weights * (spacing * spacing)
    return jnp.concatenate([*split3(weights), jnp.zeros_like(x)], axis=0).astype(bf16)


def mode_moments(weights, value):
    high = value.astype(bf16)
    low = (value - high.astype(f32)).astype(bf16)
    dims = (((1,), (1,)), ((), ()))
    total = lax.dot_general(weights, high, dims, preferred_element_type=f32)
    total = total + lax.dot_general(weights, low, dims, preferred_element_type=f32)
    return total[0:8] + total[8:16] + total[16:24]


def first_kernel(z_ref, mom):
    vel = z_ref.shape[2]
    weights = weight_rows(lax.axis_index("vel") * vel, vel)
    for j in range(MODES):
        mom[pl.ds(j * SUB, SUB), :] = mode_moments(weights, z_ref[j])


def put_index(neigh_ref, rows_ref, lists, src, away, offsets, elems, chunks):
    slots = rows_ref.shape[1]
    faces = 3 * elems
    shape = neigh_ref.shape
    face = lax.broadcasted_iota(jnp.int32, shape, 0) * elems + lax.broadcasted_iota(jnp.int32, shape, 1)

    def mark(group, found):
        for i in range(SUB):
            slot = group * SUB + i
            found = jnp.where(face == lists[0, slot], faces + slot, found)
            found = jnp.where(face == lists[1, slot], faces + slots + slot, found)
        return found

    found = jnp.maximum(lax.fori_loop(0, slots // SUB, mark, neigh_ref[...]), 0)
    src[...] = found * chunks
    away[...] = jnp.where(found < faces, found % elems, found - 2 * elems) * chunks
    known = jnp.maximum(rows_ref[...], 0)
    offsets[pl.ds(0, 2), :] = known * chunks
    offsets[pl.ds(2, 2), :] = known % elems * chunks


def put_columns(rows, out):
    elems = out.shape[1]
    turned = jnp.concatenate([*rows, jnp.zeros((LANE - out.shape[0], elems), f32)], axis=0).T
    for n in range(out.shape[0]):
        out[n] = jnp.broadcast_to(turned[:, n : n + 1], (elems, LANE))


def put_flows(corner, cols):
    cx = [corner[i, 0:1, :] for i in range(3)]
    cy = [corner[i, 1:2, :] for i in range(3)]
    det = (cx[1] - cx[0]) * (cy[2] - cy[0]) - (cx[2] - cx[0]) * (cy[1] - cy[0])
    step = time_step / det
    rows = [-step * (cy[1] - cy[0]), step * (cx[1] - cx[0]), -step * (cy[0] - cy[2]), step * (cx[0] - cx[2])]
    put_columns(rows, cols)


def sides():
    parity = lax.rem(lax.axis_index("space"), 2)
    return (1 - parity, parity)


def prepare_kernel(lists, neigh_ref, rows_ref, corner, src, away, offsets, basis, cols, weights):
    vel = basis.shape[1] // MODES
    put_index(neigh_ref, rows_ref, lists, src, away, offsets, cols.shape[1], vel // LANE)
    put_flows(corner, cols)
    first = lax.axis_index("vel") * vel
    put_basis(first, basis, vel)
    weights[...] = weight_rows(first, vel)


def trace_kernel(offsets, z_ref, tbl0, tbl12, near, far, stage0, stage12):
    elems, vel = z_ref.shape[1:]
    chunks = vel // LANE
    slots = near.shape[1]

    def fill(row):
        for c in range(chunks):
            for m, values in enumerate(table_values(modes_at(z_ref, row, c))):
                start = (m * elems + row) * chunks + c
                tbl0[pl.ds(start, SUB, stride=chunks), :] = values[0]
                for level in (1, 2):
                    start = ((m * elems + row) * 2 + level - 1) * chunks + c
                    tbl12[pl.ds(start, SUB, stride=2 * chunks), :] = values[level]

    over_groups(elems, fill, 2)

    def take(row):
        for place, side in enumerate(sides()):
            for i in range(SUB):
                start = offsets[side, row + i]
                to = (place * slots + row + i) * chunks
                copy_rows(tbl0, stage0, start, to, chunks)
                copy_rows(tbl12, stage12, 2 * start, 2 * to, 2 * chunks)

    over_groups(slots, take)

    def pack(row):
        for place, out in enumerate((near, far)):
            for c in range(chunks):
                start = (place * slots + row) * chunks
                out[(0, *at(row, c))] = stage0[pl.ds(start + c, SUB, stride=chunks), :]
                for level in range(2):
                    out[(level + 1, *at(row, c))] = stage12[
                        pl.ds(2 * start + level * chunks + c, SUB, stride=2 * chunks), :
                    ]

    over_groups(slots, pack)


def flow_forms(cols, grid, row, half=False):
    col = [cols[n, pl.ds(row, SUB), :] for n in range(4)]
    if half:
        col = [0.5 * value for value in col]
    flows = []
    for x, y in grid:
        g0 = col[0] * x + col[1] * y
        g2 = col[2] * x + col[3] * y
        flows.append((g0, -(g0 + g2), g2))
    return flows


def chunk_grid(first, chunks):
    return [grid_rows(first + c * LANE, (1, LANE))[:2] for c in range(chunks)]


def put_basis(first, basis, vel):
    x, y, _ = grid_rows(first, (1, vel))
    xx = x * x
    yy = y * y
    xx_high = xx.astype(bf16).astype(f32)
    yy_high = yy.astype(bf16).astype(f32)
    monomials = (jnp.ones_like(x), x, y, xx_high, xx - xx_high, yy_high, yy - yy_high)
    row = lax.broadcasted_iota(jnp.int32, (SUB, vel), 0)
    zero = jnp.zeros((SUB, vel), f32)
    for n in range(MODES):
        mine = row == n
        for pair in range(TERMS // 2):
            halves = []
            for term in (2 * pair, 2 * pair + 1):
                which = term // 3
                halves.append(jnp.where(mine, monomials[which], 0.0) if which < len(monomials) else zero)
            basis[pl.ds(pair * 2 * SUB, 2 * SUB), pl.ds(n * vel, vel)] = jnp.concatenate(
                halves, axis=0
            ).astype(bf16)


def node_parameters(mom, rate, elems, scale):
    shape = (SUB, elems)
    row = lax.broadcasted_iota(jnp.int32, shape, 0)

    def column(values):
        out = jnp.full(shape, k(values[0]), f32)
        for n in range(1, MODES):
            out = jnp.where(row == n, k(values[n]), out)
        return out

    columns = [column(NODAL[:, j]) for j in range(MODES)]
    R = []
    for index in range(8):
        total = columns[0] * mom[index : index + 1, :]
        for j in range(1, MODES):
            total = total + columns[j] * mom[j * SUB + index : j * SUB + index + 1, :]
        R.append(total)
    zeroth, mass_x, mass_y, flux_xx, flux_xy, flux_yy, third_x, third_y = R
    density = jnp.maximum(zeroth, density_floor)
    ux = mass_x / density
    uy = mass_y / density
    drift_sq = ux * ux + uy * uy
    drift_mass = ux * mass_x + uy * mass_y
    trace = flux_xx + flux_yy
    kelvin = jnp.maximum(
        (trace - 2.0 * drift_mass + drift_sq * zeroth) / (2.0 * density), kelvin_lower_limit
    )
    qx = 0.5 * (
        third_x
        - 2.0 * (flux_xx * ux + flux_xy * uy)
        + mass_x * drift_sq
        - ux * trace
        + 2.0 * ux * drift_mass
        - ux * drift_sq * zeroth
    )
    qy = 0.5 * (
        third_y
        - 2.0 * (flux_xy * ux + flux_yy * uy)
        + mass_y * drift_sq
        - uy * trace
        + 2.0 * uy * drift_mass
        - uy * drift_sq * zeroth
    )
    nu = scale * rate * density
    over = 1.0 / kelvin
    weight = (1.0 - viscous_conductive_ratio) / (4.0 * density * kelvin * kelvin)
    qx = qx * weight
    qy = qy * weight
    excess = (over * drift_sq - 4.0, -2.0 * over * ux, -2.0 * over * uy, over, over)
    amplitude = jnp.log(nu * density * over * k(1.0 / (2.0 * math.pi)))
    exponent = (
        amplitude - 0.5 * over * drift_sq,
        over * ux,
        over * uy,
        -0.5 * over,
        -0.5 * over,
    )
    skew = (-(qx * ux + qy * uy), qx, qy)
    return nu, (excess, exponent, skew)


def spread(form, elems):
    pieces = []
    for index, value in enumerate(form):
        parts = split3(value)
        pieces += parts
        if index >= 3:
            pieces += parts
    pieces.append(jnp.zeros((TERMS * SUB - SUB * len(pieces), elems), f32))
    return jnp.concatenate(pieces, axis=0).T.astype(bf16)


def relaxed(forms, slot, row, chunk, vel, nu, inside):
    def form(i):
        return forms[i][pl.ds(row, SUB), pl.ds(slot * vel + chunk * LANE, LANE)]

    skewed = jnp.minimum(jnp.maximum(form(2) * form(0), -skew_multiplier_limit), skew_multiplier_limit)
    return jnp.exp(form(1)) * (1.0 + skewed) - nu * inside


def form_kernel(*refs, parts, section):
    mom_refs = refs[:parts]
    rate, basis, spreads, nus, *forms = refs[parts:]
    elems = rate.shape[1]
    half = basis.shape[1] // 2
    scale = time_step if section == 0 else 0.5 * time_step
    moments = mom_refs[0][...]
    for ref in mom_refs[1:]:
        moments = moments + ref[...]
    nu, coefficients = node_parameters(moments, rate[...], elems, scale)
    put_columns([nu[n : n + 1, :] for n in range(MODES)], nus)
    for i, form in enumerate(coefficients):
        spreads[i] = spread(form, elems)
        forms[i][...] = jnp.dot(spreads[i], basis[:, pl.ds(half, half)], preferred_element_type=f32)


def lifted(V, W, X):
    B0, B2 = EDGE[0], EDGE[2]
    S = [a + b for a, b in zip(V, W)]
    D = [b - a for a, b in zip(V, W)]
    return (
        (S[0] + X[0]) * k(B0[0, 0]),
        S[0] * k(B0[0, 1]) + S[1] * k(B0[1, 1]) + X[0] * k(B2[0, 1]),
        D[0] * k(-B0[0, 2]) + D[1] * k(-B0[1, 2]) + X[1] * k(B2[1, 2]),
        S[0] * k(B0[0, 3]) + S[1] * k(B0[1, 3]) + S[2] * k(B0[2, 3]) + X[0] * k(B2[0, 3]),
        D[0] * k(-B0[0, 4]) + D[1] * k(-B0[1, 4]) + D[2] * k(-B0[2, 4]) + X[1] * k(B2[1, 4]),
        S[0] * k(B0[0, 5]) + S[1] * k(B0[1, 5]) + S[2] * k(B0[2, 5]) + X[2] * k(B2[2, 5]),
    )


def own_kernel(z_ref, cols, *refs, section):
    if section == 1:
        base_ref, out = refs
    else:
        (out,) = refs
    elems, vel = z_ref.shape[1:]
    chunks = vel // LANE
    grid = chunk_grid(lax.axis_index("vel") * vel, chunks)

    def compute(row):
        flows = flow_forms(cols, grid, row)
        for c in range(chunks):
            z = modes_at(z_ref, row, c)
            z0, z1, z2, z3, z4, z5 = z
            even, odd, last = edge_parts(z)
            gs, g1, gr = flows[c]
            out0, out1, out2 = [jnp.minimum(g, 0.0) for g in flows[c]]
            V = [out0 * (even[i] - odd[i]) for i in range(3)]
            W = [out1 * (even[i] + odd[i]) for i in range(3)]
            X = [out2 * last[i] for i in range(3)]
            h = gr + 2.0 * gs
            volume = (
                None,
                (gr * z0) * k(KR[1, 0]),
                (h * z0) * k(KR[2, 0]),
                gr * (z0 * k(KR[3, 0]) + z1 * k(KR[3, 1])),
                h * (z0 * k(KR[4, 0]) + z1 * k(KR[4, 1])) + gr * (z2 * k(KR[4, 2])),
                gr * (z0 * k(KR[5, 0]) + z1 * k(KR[5, 1])) + h * (z2 * k(KR[5, 2])),
            )
            surface = lifted(V, W, X)
            for j in range(MODES):
                value = z[j] + surface[j]
                if j:
                    value = value + volume[j]
                if section == 1:
                    value = 0.5 * (base_ref[(j, *at(row, c))] + value)
                out[(j, *at(row, c))] = value

    over_groups(elems, compute, 2)


def mean_kernel(offsets, src, _, z_ref, own, near_in, far_in, cols, nus, *refs, section):
    forms = refs[:3]
    refs = refs[3:]
    tbl, mtbl, centre, high, near, far, stage_a, stage_b, stage = refs
    elems, vel = z_ref.shape[1:]
    chunks = vel // LANE
    slots = near.shape[0]
    faces = 3 * elems

    def fill_border(row):
        for side, halo in zip(sides(), (near_in, far_in)):
            for c in range(chunks):
                start = (faces + side * slots + row) * chunks + c
                tbl[pl.ds(start, SUB, stride=chunks), :] = halo[(0, *at(row, c))]

    over_groups(slots, fill_border)

    N, V = NODAL, INVERSE
    grid = chunk_grid(lax.axis_index("vel") * vel, chunks)

    def fetch(row, stage):
        for m in range(3):
            for i in range(SUB):
                copy_rows(tbl, stage, src[m, row + i], (m * SUB + i) * chunks, chunks)

    def compute(row, stage):
        flows = flow_forms(cols, grid, row, section == 1)
        nu_cols = [nus[n, pl.ds(row, SUB), :] for n in range(3, MODES)]
        for c in range(chunks):
            z0, z1, z2, z3, z4, z5 = modes_at(z_ref, row, c)
            through = None
            for m in range(3):
                value = jnp.maximum(flows[c][m], 0.0) * stage[
                    pl.ds(m * SUB * chunks + c, SUB, stride=chunks), :
                ]
                through = value if through is None else through + value
            moved = own[(0, *at(row, c))] + through * k(EDGE[0, 0, 0])
            a0 = z0 * k(N[0, 0])
            e34 = a0 + z1 * k(N[3, 1]) + z3 * k(N[3, 3]) + z5 * k(N[3, 5])
            o34 = z2 * k(N[4, 2]) + z4 * k(N[4, 4])
            inside = (
                e34 - o34,
                e34 + o34,
                a0 + z1 * k(N[5, 1]) + z3 * k(N[5, 3]) + z5 * k(N[5, 5]),
            )
            H = [relaxed(forms, n, row, c, vel, nu_cols[n], inside[n]) for n in range(3)]
            value = moved + (H[0] + H[1] + H[2]) * k(V[0, 3])
            centre[at(row, c)] = value
            mtbl[pl.ds(row * chunks + c, SUB, stride=chunks), :] = value
            for n in range(3):
                high[(n, *at(row, c))] = H[n]

    pipelined_groups(elems, (stage_a, stage_b), fetch, compute)

    def take(row):
        for place, side in enumerate(sides()):
            for i in range(SUB):
                copy_rows(mtbl, stage, offsets[2 + side, row + i], (place * slots + row + i) * chunks, chunks)

    over_groups(slots, take)

    def pack(row):
        for place, out in enumerate((near, far)):
            for c in range(chunks):
                start = (place * slots + row) * chunks + c
                out[at(row, c)] = stage[pl.ds(start, SUB, stride=chunks), :]

    over_groups(slots, pack)


def rest_kernel(src, tbl0, _, z_ref, own, near, far, high, spreads, nus, basis, cols, *refs, section):
    tbl, out, sizes, stage_a, stage_b, *forms = refs
    elems, vel = z_ref.shape[1:]
    chunks = vel // LANE
    pitch = 3 * chunks
    slots = near.shape[1]
    faces = 3 * elems

    def fill_border(row):
        for side, halo in zip(sides(), (near, far)):
            for level in range(2):
                for c in range(chunks):
                    start = ((faces + side * slots + row) * 2 + level) * chunks + c
                    tbl[pl.ds(start, SUB, stride=2 * chunks), :] = halo[(level + 1, *at(row, c))]

    over_groups(slots, fill_border)

    for i in range(3):
        forms[i][...] = jnp.dot(
            spreads[i], basis[:, pl.ds(0, 3 * vel)], preferred_element_type=f32
        )
    N, V = NODAL, INVERSE
    grid = chunk_grid(lax.axis_index("vel") * vel, chunks)

    def fetch(row, stage):
        for m in range(3):
            for i in range(SUB):
                start = src[m, row + i]
                to = (m * SUB + i) * pitch
                copy_rows(tbl0, stage, start, to, chunks)
                copy_rows(tbl, stage, 2 * start, to + chunks, 2 * chunks)

    def compute(row, stage):
        flows = flow_forms(cols, grid, row, section == 1)
        nu_cols = [nus[n, pl.ds(row, SUB), :] for n in range(3)]
        for c in range(chunks):
            z = modes_at(z_ref, row, c)
            z0, z1, z2, z3, z4, z5 = z

            def beside(m, level):
                return stage[pl.ds(m * SUB * pitch + level * chunks + c, SUB, stride=pitch), :]

            in0, in1, in2 = [jnp.maximum(g, 0.0) for g in flows[c]]
            V_in = [in0 * beside(0, i) for i in range(3)]
            W_in = [in1 * beside(1, 0), -(in1 * beside(1, 1)), in1 * beside(1, 2)]
            X_in = [in2 * beside(2, i) for i in range(3)]
            surface = lifted(V_in, W_in, X_in)
            moved = [own[(j + 1, *at(row, c))] + surface[j + 1] for j in range(5)]
            a0 = z0 * k(N[0, 0])
            e02 = a0 + z1 * k(N[0, 1]) + z3 * k(N[0, 3]) + z5 * k(N[0, 5])
            o02 = z2 * k(N[2, 2]) + z4 * k(N[2, 4])
            inside = (e02 - o02, a0 + z1 * k(N[1, 1]) + z3 * k(N[1, 3]), e02 + o02)
            H = [relaxed(forms, n, row, c, vel, nu_cols[n], inside[n]) for n in range(3)]
            H += [high[(n, *at(row, c))] for n in range(3)]
            s02 = H[0] + H[2]
            d20 = H[2] - H[0]
            s34 = H[3] + H[4]
            d43 = H[4] - H[3]
            change = (
                s02 * k(V[1, 0]) + H[1] * k(V[1, 1]) + s34 * k(V[1, 3]) + H[5] * k(V[1, 5]),
                d20 * k(V[2, 2]) + d43 * k(V[2, 4]),
                (s02 + H[5]) * k(V[3, 0]) + (H[1] - s34) * k(V[3, 1]),
                d20 * k(V[4, 2]) + d43 * k(V[4, 4]),
                s02 * k(V[5, 0]) + H[5] * k(V[5, 5]),
            )
            z = [moved[j] + change[j] for j in range(5)]
            for j in range(5):
                out[(j, *at(row, c))] = z[j]
            size1 = jnp.abs(z[0])
            size2 = jnp.abs(z[1])
            size4 = jnp.abs(z[3])
            linear = None
            quadric = None
            for m, q in ((0, 0), (0, 1), (0, 2), (2, 0), (2, 1)):
                t = TR[m, q]
                if q != 1:
                    value = size1 * k(abs(t[1])) + size2 * k(abs(t[2]))
                    linear = value if linear is None else jnp.maximum(linear, value)
                value = jnp.abs(z[2] * k(t[3]) + z[4] * k(t[5]))
                if abs(t[4]) > 1e-9:
                    value = value + size4 * k(abs(t[4]))
                quadric = value if quadric is None else jnp.maximum(quadric, value)
            linear = jnp.maximum(linear, slope_floor)
            quadric = jnp.maximum(quadric, slope_floor)
            over = k(math.sqrt(2.0)) / (linear * quadric)
            sizes[(0, *at(row, c))] = over * quadric
            sizes[(1, *at(row, c))] = over * linear

    pipelined_groups(elems, (stage_a, stage_b), fetch, compute)


def limit_kernel(away, _, centre, rest, sizes, near, far, weights, mtbl, out, *refs, section):
    if section == 0:
        mom, stage_a, stage_b = refs
        target = out
    else:
        stage_a, stage_b, target, sems = refs
    elems, vel = centre.shape
    chunks = vel // LANE
    slots = near.shape[0]

    def fill_border(row):
        for side, halo in zip(sides(), (near, far)):
            for c in range(chunks):
                start = (elems + side * slots + row) * chunks + c
                mtbl[pl.ds(start, SUB, stride=chunks), :] = halo[at(row, c)]

    over_groups(slots, fill_border)

    def fetch(row, stage):
        for m in range(3):
            for i in range(SUB):
                copy_rows(mtbl, stage, away[m, row + i], (m * SUB + i) * chunks, chunks)

    def compute(row, stage):
        for c in range(chunks):
            z0 = centre[at(row, c)]
            gaps = [
                jnp.abs(stage[pl.ds(m * SUB * chunks + c, SUB, stride=chunks), :] - z0) for m in range(3)
            ]
            gap = jnp.maximum(jnp.maximum(gaps[0], gaps[1]), gaps[2])
            theta1 = jnp.minimum(1.0, gap * sizes[(0, *at(row, c))])
            theta2 = jnp.minimum(theta1, gap * sizes[(1, *at(row, c))])
            target[(0, *at(row, c))] = z0
            for j in range(1, MODES):
                target[(j, *at(row, c))] = rest[(j - 1, *at(row, c))] * (theta1 if j < 3 else theta2)

    if section == 0:
        pipelined_groups(elems, (stage_a, stage_b), fetch, compute)
        for j in range(MODES):
            mom[pl.ds(j * SUB, SUB), :] = mode_moments(weights[...], target[j])
    else:
        pieces = sems.shape[0]
        size = elems // pieces
        copies = []
        for piece in range(pieces):
            begin = piece * size

            def fetch_piece(row, stage, begin=begin):
                fetch(row + begin, stage)

            def compute_piece(row, stage, begin=begin):
                compute(pl.multiple_of(row + begin, SUB), stage)

            pipelined_groups(size, (stage_a, stage_b), fetch_piece, compute_piece, 2)
            part = pl.ds(begin, size)
            copy = pltpu.make_async_copy(target.at[:, part, :], out.at[:, part, :], sems.at[piece])
            copy.start()
            copies.append(copy)
        for copy in copies:
            copy.wait()


def traded(value, near):
    peers = lax.axis_size("space")
    pairs = []
    for i in range(0 if near else 1, peers - 1, 2):
        pairs += [(i, i + 1), (i + 1, i)]
    return lax.ppermute(value, "space", pairs)


def swapped(value, bits):
    peers = lax.axis_size("vel")
    return lax.ppermute(value, "vel", [(i, i ^ bits) for i in range(peers)])


def moment_parts(paired):
    peers = lax.axis_size("vel")
    done = 2
    while True:
        width = min(4, peers // done)
        parts = [paired] + [swapped(paired, bits * done) for bits in range(1, width)]
        done *= width
        if done >= peers:
            return parts
        paired = sum(parts[1:], parts[0])


def on_device(distribution, corners, neighbour, boundary_faces, collision_rate):
    modes, elems, vel = distribution.shape
    chunks = vel // LANE
    slots = boundary_faces.shape[2]
    lists = boundary_faces[0]
    faces = 3 * elems
    rows = faces + 2 * slots
    S = jax.ShapeDtypeStruct
    state = S((modes, elems, vel), f32)
    one = S((slots, vel), f32)
    halo = S((3, slots, vel), f32)
    mom = S((modes * SUB, elems), f32)
    smem = pl.BlockSpec(memory_space=pltpu.SMEM)
    vmem = pl.BlockSpec(memory_space=pltpu.VMEM)
    hbm = pl.BlockSpec(memory_space=pltpu.HBM)

    def params(mib):
        return pltpu.CompilerParams(vmem_limit_bytes=mib << 20)

    def buffer(count):
        return pltpu.VMEM((count, LANE), f32)

    def evaluated():
        return [pltpu.VMEM((elems, 3 * vel), f32) for _ in range(3)]

    rate = collision_rate.reshape(1, elems)
    index = S(neighbour.shape, jnp.int32)
    src, away, offsets, basis, cols, weights = pl.pallas_call(
        prepare_kernel,
        out_shape=(
            index,
            index,
            S((4, slots), jnp.int32),
            S((TERMS * SUB, modes * vel), bf16),
            S((4, elems, LANE), f32),
            S((4 * SUB, vel), bf16),
        ),
        in_specs=[smem] + [vmem] * 3,
        out_specs=(vmem,) * 6,
        compiler_params=params(8),
        name="prepare",
    )(lists, neighbour, lists, corners.transpose(1, 0, 2))

    current = start = distribution
    partial = pl.pallas_call(
        first_kernel,
        out_shape=mom,
        in_specs=[vmem],
        out_specs=vmem,
        compiler_params=params(8),
        name="first",
    )(current)

    for section in range(2):
        opening = section == 0
        paired = partial + swapped(partial, 1)
        tbl0, tbl12, near, far = pl.pallas_call(
            trace_kernel,
            out_shape=(S((rows * chunks, LANE), f32), S((2 * rows * chunks, LANE), f32), halo, halo),
            in_specs=[smem, vmem],
            out_specs=(vmem,) * 4,
            scratch_shapes=[buffer(2 * slots * chunks), buffer(4 * slots * chunks)],
            compiler_params=params(8),
            name="trace",
        )(offsets, current)
        near, far, paired = lax.optimization_barrier((near, far, paired))
        near = traded(near, True)
        far = traded(far, False)
        parts = moment_parts(paired)

        base = [] if opening else [start]
        own = pl.pallas_call(
            lambda *refs, section=section: own_kernel(*refs, section=section),
            out_shape=state,
            in_specs=[vmem] * (2 + len(base)),
            out_specs=vmem,
            compiler_params=params(4),
            name=f"own{section}",
        )(current, cols, *base)
        spreads, nus, *forms = pl.pallas_call(
            lambda *refs, section=section: form_kernel(*refs, parts=len(parts), section=section),
            out_shape=(S((3, elems, TERMS * SUB), bf16), S((modes, elems, LANE), f32)) + (S((elems, 3 * vel), f32),) * 3,
            in_specs=[vmem] * (len(parts) + 2),
            out_specs=(vmem,) * 5,
            compiler_params=params(16),
            name=f"form{section}",
        )(*parts, rate, basis)

        tbl0, mean_table, centre, high, near_mean, far_mean = pl.pallas_call(
            lambda *refs, section=section: mean_kernel(*refs, section=section),
            out_shape=(
                S((rows * chunks, LANE), f32),
                S(((elems + 2 * slots) * chunks, LANE), f32),
                S((elems, vel), f32),
                S((3, elems, vel), f32),
                one,
                one,
            ),
            input_output_aliases={2: 0},
            in_specs=[smem] * 2 + [vmem] * 10,
            out_specs=(vmem,) * 6,
            scratch_shapes=[buffer(3 * SUB * chunks)] * 2 + [buffer(2 * slots * chunks)],
            compiler_params=params(16),
            name=f"mean{section}",
        )(offsets, src, tbl0, current, own, near, far, cols, nus, *forms)
        near_mean = traded(near_mean, True)
        far_mean = traded(far_mean, False)

        _, rest, sizes = pl.pallas_call(
            lambda *refs, section=section: rest_kernel(*refs, section=section),
            out_shape=(S((2 * rows * chunks, LANE), f32), S((5, elems, vel), f32), S((2, elems, vel), f32)),
            input_output_aliases={2: 0},
            in_specs=[smem] + [vmem] * 11,
            out_specs=(vmem,) * 3,
            scratch_shapes=[buffer(9 * SUB * chunks)] * 2 + evaluated(),
            compiler_params=params(20),
            name=f"rest{section}",
        )(src, tbl0, tbl12, current, own, near, far, high, spreads, nus, basis, cols)

        scratch = [buffer(3 * SUB * chunks)] * 2
        if not opening:
            scratch += [pltpu.VMEM(state.shape, f32), pltpu.SemaphoreType.DMA((4,))]
        made = pl.pallas_call(
            lambda *refs, section=section: limit_kernel(*refs, section=section),
            out_shape=(S(mean_table.shape, f32), state) + ((mom,) if opening else ()),
            in_specs=[smem] + [vmem] * 7,
            out_specs=(vmem,) * 3 if opening else (vmem, hbm),
            input_output_aliases={1: 0},
            scratch_shapes=scratch,
            compiler_params=params(8),
            name=f"limit{section}",
        )(away, mean_table, centre, rest, sizes, near_mean, far_mean, weights)
        if opening:
            _, current, partial = made
    return made[1]


def solution(mesh):
    in_specs = (
        P(None, "space", "vel"),
        P(None, None, "space"),
        P(None, "space"),
        P("space", None, None),
        P("space"),
    )
    return jax.shard_map(
        on_device, mesh=mesh, in_specs=in_specs, out_specs=P(None, "space", "vel"), check_vma=False
    )
```

```python
import math

import jax
import jax.numpy as jnp
import numpy as np
from jax import lax
from jax.experimental import pallas as pl
from jax.experimental.pallas import tpu as pltpu
from jax.sharding import PartitionSpec as P

VGRID = 64
velocity_limit = 6.0
time_step = 0.012
viscous_conductive_ratio = 2.0 / 3.0
density_floor = 0.1
kelvin_lower_limit = 0.2
skew_multiplier_limit = 0.9
slope_floor = 0.01

LANE = 128
SUB = 8
MODES = 6
TERMS = 32
f32 = jnp.float32
bf16 = jnp.bfloat16


def monomial_integral(power_r, power_s):
    return math.factorial(power_r) * math.factorial(power_s) / math.factorial(power_r + power_s + 2)


def dg_tables():
    powers = [(0, 0), (1, 0), (0, 1), (2, 0), (1, 1), (0, 2)]
    gram = np.array(
        [[monomial_integral(a[0] + b[0], a[1] + b[1]) for b in powers] for a in powers]
    )
    coeffs = np.linalg.inv(np.linalg.cholesky(gram))
    deriv_r = np.zeros((6, 6))
    deriv_s = np.zeros((6, 6))
    for i, a in enumerate(powers):
        for j, b in enumerate(powers):
            if a[0] > 0:
                deriv_r[i, j] = a[0] * monomial_integral(a[0] - 1 + b[0], a[1] + b[1])
            if a[1] > 0:
                deriv_s[i, j] = a[1] * monomial_integral(a[0] + b[0], a[1] - 1 + b[1])
    stiff_r = coeffs @ deriv_r @ coeffs.T
    stiff_s = coeffs @ deriv_s @ coeffs.T

    def evaluate(location):
        return coeffs @ np.array([location[0] ** p[0] * location[1] ** p[1] for p in powers])

    vertices = np.array([[0.0, 0.0], [1.0, 0.0], [0.0, 1.0]])
    offset = math.sqrt(0.15)
    positions = np.array([0.5 - offset, 0.5, 0.5 + offset])
    weights = np.array([5.0, 8.0, 5.0]) / 18.0
    traces = np.zeros((3, 3, 6))
    for m in range(3):
        for q in range(3):
            along = positions[q]
            traces[m, q] = evaluate((1.0 - along) * vertices[m] + along * vertices[(m + 1) % 3])
    legendre = np.stack(
        [
            np.ones(3),
            math.sqrt(3.0) * (2.0 * positions - 1.0),
            math.sqrt(5.0) * (6.0 * positions**2 - 6.0 * positions + 1.0),
        ]
    )
    edge = np.einsum("lq,q,mqj->mlj", legendre, weights, traces)
    node_list = [(0.0, 0.0), (1.0, 0.0), (0.0, 1.0), (0.5, 0.0), (0.5, 0.5), (0.0, 0.5)]
    nodal = np.array([evaluate(np.array(n)) for n in node_list])
    inverse = np.linalg.inv(nodal)
    return stiff_r, stiff_s, traces, edge, nodal, inverse


KR, KS, TR, EDGE, NODAL, INVERSE = dg_tables()


def k(value):
    return float(np.float32(value))


def edge_parts(z):
    z0, z1, z2, z3, z4, z5 = z
    b = EDGE[0]
    a0 = z0 * k(b[0, 0])
    even = (
        a0 + z1 * k(b[0, 1]) + z3 * k(b[0, 3]) + z5 * k(b[0, 5]),
        z1 * k(b[1, 1]) + z3 * k(b[1, 3]) + z5 * k(b[1, 5]),
        z3 * k(b[2, 3]) + z5 * k(b[2, 5]),
    )
    odd = (
        z2 * k(-b[0, 2]) + z4 * k(-b[0, 4]),
        z2 * k(-b[1, 2]) + z4 * k(-b[1, 4]),
        z4 * k(-b[2, 4]),
    )
    c = EDGE[2]
    last = (
        a0 + z1 * k(c[0, 1]) + z3 * k(c[0, 3]),
        z2 * k(c[1, 2]) + z4 * k(c[1, 4]),
        z5 * k(c[2, 5]),
    )
    return even, odd, last


def table_values(z):
    even, odd, last = edge_parts(z)
    return (
        (even[0] - odd[0], odd[1] - even[1], even[2] - odd[2]),
        (even[0] + odd[0], even[1] + odd[1], even[2] + odd[2]),
        (last[0], -last[1], last[2]),
    )


def at(row, chunk):
    return pl.ds(row, SUB), pl.ds(chunk * LANE, LANE)


def modes_at(ref, row, chunk):
    return [ref[(j, *at(row, chunk))] for j in range(ref.shape[0])]


def over_groups(count, body, together=5):
    while count // SUB % together:
        together -= 1

    def step(g, _):
        for i in range(together):
            body(pl.multiple_of(g * (SUB * together) + i * SUB, SUB))
        return 0

    lax.fori_loop(0, count // (SUB * together), step, 0)


def copy_rows(source, target, start, to, count):
    for piece in range(0, count, SUB):
        rows = min(SUB, count - piece)
        target[pl.ds(to + piece, rows), :] = source[pl.ds(start + piece, rows), :]


def pipelined_groups(count, stages, fetch, compute, pairs=4):
    last = count - SUB
    span = 2 * SUB * pairs
    fetch(0, stages[0])

    def step(g, _):
        start = pl.multiple_of(g * span, span)
        for i in range(2 * pairs):
            row = pl.multiple_of(start + i * SUB, SUB)
            after = row + SUB
            if i + 1 == 2 * pairs:
                after = jnp.minimum(after, last)
            fetch(pl.multiple_of(after, SUB), stages[(i + 1) % 2])
            compute(row, stages[i % 2])
        return 0

    lax.fori_loop(0, count // span, step, 0)


def grid_rows(first, shape):
    index = first + lax.broadcasted_iota(jnp.int32, shape, len(shape) - 1)
    spacing = 2.0 * velocity_limit / VGRID
    x = -velocity_limit + ((index // VGRID).astype(f32) + 0.5) * spacing
    y = -velocity_limit + ((index % VGRID).astype(f32) + 0.5) * spacing
    return x, y, spacing


def split3(value):
    high = value.astype(bf16).astype(f32)
    rest = value - high
    middle = rest.astype(bf16).astype(f32)
    return high, middle, (rest - middle).astype(bf16).astype(f32)


def weight_rows(first, vel):
    x, y, spacing = grid_rows(first, (SUB, vel))
    row = lax.broadcasted_iota(jnp.int32, (SUB, vel), 0)
    square = x * x + y * y
    weights = jnp.ones_like(x)
    for index, value in enumerate((x, y, x * x, x * y, y * y, x * square, y * square)):
        weights = jnp.where(row == index + 1, value, weights)
    weights = weights * (spacing * spacing)
    return jnp.concatenate([*split3(weights), jnp.zeros_like(x)], axis=0).astype(bf16)


def mode_moments(weights, value):
    high = value.astype(bf16)
    low = (value - high.astype(f32)).astype(bf16)
    dims = (((1,), (1,)), ((), ()))
    total = lax.dot_general(weights, high, dims, preferred_element_type=f32)
    total = total + lax.dot_general(weights, low, dims, preferred_element_type=f32)
    return total[0:8] + total[8:16] + total[16:24]


def first_kernel(z_ref, mom):
    vel = z_ref.shape[2]
    weights = weight_rows(lax.axis_index("vel") * vel, vel)
    for j in range(MODES):
        mom[pl.ds(j * SUB, SUB), :] = mode_moments(weights, z_ref[j])


def put_index(neigh_ref, rows_ref, lists, src, away, offsets, elems, chunks):
    slots = rows_ref.shape[1]
    faces = 3 * elems
    shape = neigh_ref.shape
    face = lax.broadcasted_iota(jnp.int32, shape, 0) * elems + lax.broadcasted_iota(jnp.int32, shape, 1)

    def mark(group, found):
        for i in range(SUB):
            slot = group * SUB + i
            found = jnp.where(face == lists[0, slot], faces + slot, found)
            found = jnp.where(face == lists[1, slot], faces + slots + slot, found)
        return found

    found = jnp.maximum(lax.fori_loop(0, slots // SUB, mark, neigh_ref[...]), 0)
    src[...] = found * chunks
    away[...] = jnp.where(found < faces, found % elems, found - 2 * elems) * chunks
    known = jnp.maximum(rows_ref[...], 0)
    offsets[pl.ds(0, 2), :] = known * chunks
    offsets[pl.ds(2, 2), :] = known % elems * chunks


def put_columns(rows, out):
    elems = out.shape[1]
    turned = jnp.concatenate([*rows, jnp.zeros((LANE - out.shape[0], elems), f32)], axis=0).T
    for n in range(out.shape[0]):
        out[n] = jnp.broadcast_to(turned[:, n : n + 1], (elems, LANE))


def put_flows(corner, cols):
    cx = [corner[i, 0:1, :] for i in range(3)]
    cy = [corner[i, 1:2, :] for i in range(3)]
    det = (cx[1] - cx[0]) * (cy[2] - cy[0]) - (cx[2] - cx[0]) * (cy[1] - cy[0])
    step = time_step / det
    rows = [-step * (cy[1] - cy[0]), step * (cx[1] - cx[0]), -step * (cy[0] - cy[2]), step * (cx[0] - cx[2])]
    put_columns(rows, cols)


def sides():
    parity = lax.rem(lax.axis_index("space"), 2)
    return (1 - parity, parity)


def prepare_kernel(lists, neigh_ref, rows_ref, corner, src, away, offsets, basis, cols, weights):
    vel = basis.shape[1] // MODES
    put_index(neigh_ref, rows_ref, lists, src, away, offsets, cols.shape[1], vel // LANE)
    put_flows(corner, cols)
    first = lax.axis_index("vel") * vel
    put_basis(first, basis, vel)
    weights[...] = weight_rows(first, vel)


def trace_kernel(offsets, z_ref, tbl0, tbl12, near, far, stage0, stage12):
    elems, vel = z_ref.shape[1:]
    chunks = vel // LANE
    slots = near.shape[1]

    def fill(row):
        for c in range(chunks):
            for m, values in enumerate(table_values(modes_at(z_ref, row, c))):
                start = (m * elems + row) * chunks + c
                tbl0[pl.ds(start, SUB, stride=chunks), :] = values[0]
                for level in (1, 2):
                    start = ((m * elems + row) * 2 + level - 1) * chunks + c
                    tbl12[pl.ds(start, SUB, stride=2 * chunks), :] = values[level]

    over_groups(elems, fill, 2)

    def take(row):
        for place, side in enumerate(sides()):
            for i in range(SUB):
                start = offsets[side, row + i]
                to = (place * slots + row + i) * chunks
                copy_rows(tbl0, stage0, start, to, chunks)
                copy_rows(tbl12, stage12, 2 * start, 2 * to, 2 * chunks)

    over_groups(slots, take)

    def pack(row):
        for place, out in enumerate((near, far)):
            for c in range(chunks):
                start = (place * slots + row) * chunks
                out[(0, *at(row, c))] = stage0[pl.ds(start + c, SUB, stride=chunks), :]
                for level in range(2):
                    out[(level + 1, *at(row, c))] = stage12[
                        pl.ds(2 * start + level * chunks + c, SUB, stride=2 * chunks), :
                    ]

    over_groups(slots, pack)


def flow_forms(cols, grid, row, half=False):
    col = [cols[n, pl.ds(row, SUB), :] for n in range(4)]
    if half:
        col = [0.5 * value for value in col]
    flows = []
    for x, y in grid:
        g0 = col[0] * x + col[1] * y
        g2 = col[2] * x + col[3] * y
        flows.append((g0, -(g0 + g2), g2))
    return flows


def chunk_grid(first, chunks):
    return [grid_rows(first + c * LANE, (1, LANE))[:2] for c in range(chunks)]


def put_basis(first, basis, vel):
    x, y, _ = grid_rows(first, (1, vel))
    xx = x * x
    yy = y * y
    xx_high = xx.astype(bf16).astype(f32)
    yy_high = yy.astype(bf16).astype(f32)
    monomials = (jnp.ones_like(x), x, y, xx_high, xx - xx_high, yy_high, yy - yy_high)
    row = lax.broadcasted_iota(jnp.int32, (SUB, vel), 0)
    zero = jnp.zeros((SUB, vel), f32)
    for n in range(MODES):
        mine = row == n
        for pair in range(TERMS // 2):
            halves = []
            for term in (2 * pair, 2 * pair + 1):
                which = term // 3
                halves.append(jnp.where(mine, monomials[which], 0.0) if which < len(monomials) else zero)
            basis[pl.ds(pair * 2 * SUB, 2 * SUB), pl.ds(n * vel, vel)] = jnp.concatenate(
                halves, axis=0
            ).astype(bf16)


def node_parameters(mom, rate, elems, scale):
    shape = (SUB, elems)
    row = lax.broadcasted_iota(jnp.int32, shape, 0)

    def column(values):
        out = jnp.full(shape, k(values[0]), f32)
        for n in range(1, MODES):
            out = jnp.where(row == n, k(values[n]), out)
        return out

    columns = [column(NODAL[:, j]) for j in range(MODES)]
    R = []
    for index in range(8):
        total = columns[0] * mom[index : index + 1, :]
        for j in range(1, MODES):
            total = total + columns[j] * mom[j * SUB + index : j * SUB + index + 1, :]
        R.append(total)
    zeroth, mass_x, mass_y, flux_xx, flux_xy, flux_yy, third_x, third_y = R
    density = jnp.maximum(zeroth, density_floor)
    ux = mass_x / density
    uy = mass_y / density
    drift_sq = ux * ux + uy * uy
    drift_mass = ux * mass_x + uy * mass_y
    trace = flux_xx + flux_yy
    kelvin = jnp.maximum(
        (trace - 2.0 * drift_mass + drift_sq * zeroth) / (2.0 * density), kelvin_lower_limit
    )
    qx = 0.5 * (
        third_x
        - 2.0 * (flux_xx * ux + flux_xy * uy)
        + mass_x * drift_sq
        - ux * trace
        + 2.0 * ux * drift_mass
        - ux * drift_sq * zeroth
    )
    qy = 0.5 * (
        third_y
        - 2.0 * (flux_xy * ux + flux_yy * uy)
        + mass_y * drift_sq
        - uy * trace
        + 2.0 * uy * drift_mass
        - uy * drift_sq * zeroth
    )
    nu = scale * rate * density
    over = 1.0 / kelvin
    weight = (1.0 - viscous_conductive_ratio) / (4.0 * density * kelvin * kelvin)
    qx = qx * weight
    qy = qy * weight
    excess = (over * drift_sq - 4.0, -2.0 * over * ux, -2.0 * over * uy, over, over)
    amplitude = jnp.log(nu * density * over * k(1.0 / (2.0 * math.pi)))
    skew = (-(qx * ux + qy * uy), qx, qy)
    return nu, amplitude - 2.0, (excess, skew)


def spread(form, elems):
    pieces = []
    for index, value in enumerate(form):
        parts = split3(value)
        pieces += parts
        if index >= 3:
            pieces += parts
    pieces.append(jnp.zeros((TERMS * SUB - SUB * len(pieces), elems), f32))
    return jnp.concatenate(pieces, axis=0).T.astype(bf16)


def relaxed(forms, slot, row, chunk, vel, nu, amplitude, inside):
    def form(i):
        return forms[i][pl.ds(row, SUB), pl.ds(slot * vel + chunk * LANE, LANE)]

    excess = form(0)
    skewed = jnp.minimum(jnp.maximum(form(1) * excess, -skew_multiplier_limit), skew_multiplier_limit)
    return jnp.exp(amplitude - 0.5 * excess) * (1.0 + skewed) - nu * inside


def form_kernel(*refs, parts, section):
    mom_refs = refs[:parts]
    rate, basis, spreads, nus, *forms = refs[parts:]
    elems = rate.shape[1]
    half = basis.shape[1] // 2
    scale = time_step if section == 0 else 0.5 * time_step
    moments = mom_refs[0][...]
    for ref in mom_refs[1:]:
        moments = moments + ref[...]
    nu, amplitude, coefficients = node_parameters(moments, rate[...], elems, scale)
    put_columns([value[n : n + 1, :] for value in (nu, amplitude) for n in range(MODES)], nus)
    for i, form in enumerate(coefficients):
        spreads[i] = spread(form, elems)
        forms[i][...] = jnp.dot(spreads[i], basis[:, pl.ds(half, half)], preferred_element_type=f32)


def lifted(V, W, X):
    B0, B2 = EDGE[0], EDGE[2]
    S = [a + b for a, b in zip(V, W)]
    D = [b - a for a, b in zip(V, W)]
    return (
        (S[0] + X[0]) * k(B0[0, 0]),
        S[0] * k(B0[0, 1]) + S[1] * k(B0[1, 1]) + X[0] * k(B2[0, 1]),
        D[0] * k(-B0[0, 2]) + D[1] * k(-B0[1, 2]) + X[1] * k(B2[1, 2]),
        S[0] * k(B0[0, 3]) + S[1] * k(B0[1, 3]) + S[2] * k(B0[2, 3]) + X[0] * k(B2[0, 3]),
        D[0] * k(-B0[0, 4]) + D[1] * k(-B0[1, 4]) + D[2] * k(-B0[2, 4]) + X[1] * k(B2[1, 4]),
        S[0] * k(B0[0, 5]) + S[1] * k(B0[1, 5]) + S[2] * k(B0[2, 5]) + X[2] * k(B2[2, 5]),
    )


def own_kernel(z_ref, cols, *refs, section):
    if section == 1:
        base_ref, out = refs
    else:
        (out,) = refs
    elems, vel = z_ref.shape[1:]
    chunks = vel // LANE
    grid = chunk_grid(lax.axis_index("vel") * vel, chunks)

    def compute(row):
        flows = flow_forms(cols, grid, row)
        for c in range(chunks):
            z = modes_at(z_ref, row, c)
            z0, z1, z2, z3, z4, z5 = z
            even, odd, last = edge_parts(z)
            gs, g1, gr = flows[c]
            out0, out1, out2 = [jnp.minimum(g, 0.0) for g in flows[c]]
            V = [out0 * (even[i] - odd[i]) for i in range(3)]
            W = [out1 * (even[i] + odd[i]) for i in range(3)]
            X = [out2 * last[i] for i in range(3)]
            h = gr + 2.0 * gs
            volume = (
                None,
                (gr * z0) * k(KR[1, 0]),
                (h * z0) * k(KR[2, 0]),
                gr * (z0 * k(KR[3, 0]) + z1 * k(KR[3, 1])),
                h * (z0 * k(KR[4, 0]) + z1 * k(KR[4, 1])) + gr * (z2 * k(KR[4, 2])),
                gr * (z0 * k(KR[5, 0]) + z1 * k(KR[5, 1])) + h * (z2 * k(KR[5, 2])),
            )
            surface = lifted(V, W, X)
            for j in range(MODES):
                value = z[j] + surface[j]
                if j:
                    value = value + volume[j]
                if section == 1:
                    value = 0.5 * (base_ref[(j, *at(row, c))] + value)
                out[(j, *at(row, c))] = value

    over_groups(elems, compute, 2)


def mean_kernel(offsets, src, _, z_ref, own, near_in, far_in, cols, nus, *refs, section):
    forms = refs[:2]
    refs = refs[2:]
    tbl, mtbl, centre, high, near, far, stage_a, stage_b, stage = refs
    elems, vel = z_ref.shape[1:]
    chunks = vel // LANE
    slots = near.shape[0]
    faces = 3 * elems

    def fill_border(row):
        for side, halo in zip(sides(), (near_in, far_in)):
            for c in range(chunks):
                start = (faces + side * slots + row) * chunks + c
                tbl[pl.ds(start, SUB, stride=chunks), :] = halo[(0, *at(row, c))]

    over_groups(slots, fill_border)

    N, V = NODAL, INVERSE
    grid = chunk_grid(lax.axis_index("vel") * vel, chunks)

    def fetch(row, stage):
        for m in range(3):
            for i in range(SUB):
                copy_rows(tbl, stage, src[m, row + i], (m * SUB + i) * chunks, chunks)

    def compute(row, stage):
        flows = flow_forms(cols, grid, row, section == 1)
        nu_cols = [nus[n, pl.ds(row, SUB), :] for n in range(3, MODES)]
        amp_cols = [nus[MODES + n, pl.ds(row, SUB), :] for n in range(3, MODES)]
        for c in range(chunks):
            z0, z1, z2, z3, z4, z5 = modes_at(z_ref, row, c)
            through = None
            for m in range(3):
                value = jnp.maximum(flows[c][m], 0.0) * stage[
                    pl.ds(m * SUB * chunks + c, SUB, stride=chunks), :
                ]
                through = value if through is None else through + value
            moved = own[(0, *at(row, c))] + through * k(EDGE[0, 0, 0])
            a0 = z0 * k(N[0, 0])
            e34 = a0 + z1 * k(N[3, 1]) + z3 * k(N[3, 3]) + z5 * k(N[3, 5])
            o34 = z2 * k(N[4, 2]) + z4 * k(N[4, 4])
            inside = (
                e34 - o34,
                e34 + o34,
                a0 + z1 * k(N[5, 1]) + z3 * k(N[5, 3]) + z5 * k(N[5, 5]),
            )
            H = [relaxed(forms, n, row, c, vel, nu_cols[n], amp_cols[n], inside[n]) for n in range(3)]
            value = moved + (H[0] + H[1] + H[2]) * k(V[0, 3])
            centre[at(row, c)] = value
            mtbl[pl.ds(row * chunks + c, SUB, stride=chunks), :] = value
            for n in range(3):
                high[(n, *at(row, c))] = H[n]

    pipelined_groups(elems, (stage_a, stage_b), fetch, compute)

    def take(row):
        for place, side in enumerate(sides()):
            for i in range(SUB):
                copy_rows(mtbl, stage, offsets[2 + side, row + i], (place * slots + row + i) * chunks, chunks)

    over_groups(slots, take)

    def pack(row):
        for place, out in enumerate((near, far)):
            for c in range(chunks):
                start = (place * slots + row) * chunks + c
                out[at(row, c)] = stage[pl.ds(start, SUB, stride=chunks), :]

    over_groups(slots, pack)


def rest_kernel(src, tbl0, _, z_ref, own, near, far, high, spreads, nus, basis, cols, *refs, section):
    tbl, out, sizes, stage_a, stage_b, *forms = refs
    elems, vel = z_ref.shape[1:]
    chunks = vel // LANE
    pitch = 3 * chunks
    slots = near.shape[1]
    faces = 3 * elems

    def fill_border(row):
        for side, halo in zip(sides(), (near, far)):
            for level in range(2):
                for c in range(chunks):
                    start = ((faces + side * slots + row) * 2 + level) * chunks + c
                    tbl[pl.ds(start, SUB, stride=2 * chunks), :] = halo[(level + 1, *at(row, c))]

    over_groups(slots, fill_border)

    for i in range(2):
        forms[i][...] = jnp.dot(
            spreads[i], basis[:, pl.ds(0, 3 * vel)], preferred_element_type=f32
        )
    N, V = NODAL, INVERSE
    grid = chunk_grid(lax.axis_index("vel") * vel, chunks)

    def fetch(row, stage):
        for m in range(3):
            for i in range(SUB):
                start = src[m, row + i]
                to = (m * SUB + i) * pitch
                copy_rows(tbl0, stage, start, to, chunks)
                copy_rows(tbl, stage, 2 * start, to + chunks, 2 * chunks)

    def compute(row, stage):
        flows = flow_forms(cols, grid, row, section == 1)
        nu_cols = [nus[n, pl.ds(row, SUB), :] for n in range(3)]
        amp_cols = [nus[MODES + n, pl.ds(row, SUB), :] for n in range(3)]
        for c in range(chunks):
            z = modes_at(z_ref, row, c)
            z0, z1, z2, z3, z4, z5 = z

            def beside(m, level):
                return stage[pl.ds(m * SUB * pitch + level * chunks + c, SUB, stride=pitch), :]

            in0, in1, in2 = [jnp.maximum(g, 0.0) for g in flows[c]]
            V_in = [in0 * beside(0, i) for i in range(3)]
            W_in = [in1 * beside(1, 0), -(in1 * beside(1, 1)), in1 * beside(1, 2)]
            X_in = [in2 * beside(2, i) for i in range(3)]
            surface = lifted(V_in, W_in, X_in)
            moved = [own[(j + 1, *at(row, c))] + surface[j + 1] for j in range(5)]
            a0 = z0 * k(N[0, 0])
            e02 = a0 + z1 * k(N[0, 1]) + z3 * k(N[0, 3]) + z5 * k(N[0, 5])
            o02 = z2 * k(N[2, 2]) + z4 * k(N[2, 4])
            inside = (e02 - o02, a0 + z1 * k(N[1, 1]) + z3 * k(N[1, 3]), e02 + o02)
            H = [relaxed(forms, n, row, c, vel, nu_cols[n], amp_cols[n], inside[n]) for n in range(3)]
            H += [high[(n, *at(row, c))] for n in range(3)]
            s02 = H[0] + H[2]
            d20 = H[2] - H[0]
            s34 = H[3] + H[4]
            d43 = H[4] - H[3]
            change = (
                s02 * k(V[1, 0]) + H[1] * k(V[1, 1]) + s34 * k(V[1, 3]) + H[5] * k(V[1, 5]),
                d20 * k(V[2, 2]) + d43 * k(V[2, 4]),
                (s02 + H[5]) * k(V[3, 0]) + (H[1] - s34) * k(V[3, 1]),
                d20 * k(V[4, 2]) + d43 * k(V[4, 4]),
                s02 * k(V[5, 0]) + H[5] * k(V[5, 5]),
            )
            z = [moved[j] + change[j] for j in range(5)]
            for j in range(5):
                out[(j, *at(row, c))] = z[j]
            size1 = jnp.abs(z[0])
            size2 = jnp.abs(z[1])
            size4 = jnp.abs(z[3])
            linear = None
            quadric = None
            for m, q in ((0, 0), (0, 1), (0, 2), (2, 0), (2, 1)):
                t = TR[m, q]
                if q != 1:
                    value = size1 * k(abs(t[1])) + size2 * k(abs(t[2]))
                    linear = value if linear is None else jnp.maximum(linear, value)
                value = jnp.abs(z[2] * k(t[3]) + z[4] * k(t[5]))
                if abs(t[4]) > 1e-9:
                    value = value + size4 * k(abs(t[4]))
                quadric = value if quadric is None else jnp.maximum(quadric, value)
            linear = jnp.maximum(linear, slope_floor)
            quadric = jnp.maximum(quadric, slope_floor)
            over = k(math.sqrt(2.0)) / (linear * quadric)
            sizes[(0, *at(row, c))] = over * quadric
            sizes[(1, *at(row, c))] = over * linear

    pipelined_groups(elems, (stage_a, stage_b), fetch, compute)


def limit_kernel(away, _, centre, rest, sizes, near, far, weights, mtbl, out, *refs, section):
    if section == 0:
        mom, stage_a, stage_b = refs
        target = out
    else:
        stage_a, stage_b, target, sems = refs
    elems, vel = centre.shape
    chunks = vel // LANE
    slots = near.shape[0]

    def fill_border(row):
        for side, halo in zip(sides(), (near, far)):
            for c in range(chunks):
                start = (elems + side * slots + row) * chunks + c
                mtbl[pl.ds(start, SUB, stride=chunks), :] = halo[at(row, c)]

    over_groups(slots, fill_border)

    def fetch(row, stage):
        for m in range(3):
            for i in range(SUB):
                copy_rows(mtbl, stage, away[m, row + i], (m * SUB + i) * chunks, chunks)

    def compute(row, stage):
        for c in range(chunks):
            z0 = centre[at(row, c)]
            gaps = [
                jnp.abs(stage[pl.ds(m * SUB * chunks + c, SUB, stride=chunks), :] - z0) for m in range(3)
            ]
            gap = jnp.maximum(jnp.maximum(gaps[0], gaps[1]), gaps[2])
            theta1 = jnp.minimum(1.0, gap * sizes[(0, *at(row, c))])
            theta2 = jnp.minimum(theta1, gap * sizes[(1, *at(row, c))])
            target[(0, *at(row, c))] = z0
            for j in range(1, MODES):
                target[(j, *at(row, c))] = rest[(j - 1, *at(row, c))] * (theta1 if j < 3 else theta2)

    if section == 0:
        pipelined_groups(elems, (stage_a, stage_b), fetch, compute)
        for j in range(MODES):
            mom[pl.ds(j * SUB, SUB), :] = mode_moments(weights[...], target[j])
    else:
        pieces = sems.shape[0]
        size = elems // pieces
        copies = []
        for piece in range(pieces):
            begin = piece * size

            def fetch_piece(row, stage, begin=begin):
                fetch(row + begin, stage)

            def compute_piece(row, stage, begin=begin):
                compute(pl.multiple_of(row + begin, SUB), stage)

            pipelined_groups(size, (stage_a, stage_b), fetch_piece, compute_piece, 2)
            part = pl.ds(begin, size)
            copy = pltpu.make_async_copy(target.at[:, part, :], out.at[:, part, :], sems.at[piece])
            copy.start()
            copies.append(copy)
        for copy in copies:
            copy.wait()


def traded(value, near):
    peers = lax.axis_size("space")
    pairs = []
    for i in range(0 if near else 1, peers - 1, 2):
        pairs += [(i, i + 1), (i + 1, i)]
    return lax.ppermute(value, "space", pairs)


def swapped(value, bits):
    peers = lax.axis_size("vel")
    return lax.ppermute(value, "vel", [(i, i ^ bits) for i in range(peers)])


def moment_parts(paired):
    peers = lax.axis_size("vel")
    done = 2
    while True:
        width = min(4, peers // done)
        parts = [paired] + [swapped(paired, bits * done) for bits in range(1, width)]
        done *= width
        if done >= peers:
            return parts
        paired = sum(parts[1:], parts[0])


def on_device(distribution, corners, neighbour, boundary_faces, collision_rate):
    modes, elems, vel = distribution.shape
    chunks = vel // LANE
    slots = boundary_faces.shape[2]
    lists = boundary_faces[0]
    faces = 3 * elems
    rows = faces + 2 * slots
    S = jax.ShapeDtypeStruct
    state = S((modes, elems, vel), f32)
    one = S((slots, vel), f32)
    halo = S((3, slots, vel), f32)
    mom = S((modes * SUB, elems), f32)
    smem = pl.BlockSpec(memory_space=pltpu.SMEM)
    vmem = pl.BlockSpec(memory_space=pltpu.VMEM)
    hbm = pl.BlockSpec(memory_space=pltpu.HBM)

    def params(mib):
        return pltpu.CompilerParams(vmem_limit_bytes=mib << 20)

    def buffer(count):
        return pltpu.VMEM((count, LANE), f32)

    def evaluated():
        return [pltpu.VMEM((elems, 3 * vel), f32) for _ in range(2)]

    rate = collision_rate.reshape(1, elems)
    index = S(neighbour.shape, jnp.int32)
    src, away, offsets, basis, cols, weights = pl.pallas_call(
        prepare_kernel,
        out_shape=(
            index,
            index,
            S((4, slots), jnp.int32),
            S((TERMS * SUB, modes * vel), bf16),
            S((4, elems, LANE), f32),
            S((4 * SUB, vel), bf16),
        ),
        in_specs=[smem] + [vmem] * 3,
        out_specs=(vmem,) * 6,
        compiler_params=params(8),
        name="prepare",
    )(lists, neighbour, lists, corners.transpose(1, 0, 2))

    current = start = distribution
    partial = pl.pallas_call(
        first_kernel,
        out_shape=mom,
        in_specs=[vmem],
        out_specs=vmem,
        compiler_params=params(8),
        name="first",
    )(current)

    for section in range(2):
        opening = section == 0
        paired = partial + swapped(partial, 1)
        tbl0, tbl12, near, far = pl.pallas_call(
            trace_kernel,
            out_shape=(S((rows * chunks, LANE), f32), S((2 * rows * chunks, LANE), f32), halo, halo),
            in_specs=[smem, vmem],
            out_specs=(vmem,) * 4,
            scratch_shapes=[buffer(2 * slots * chunks), buffer(4 * slots * chunks)],
            compiler_params=params(8),
            name="trace",
        )(offsets, current)
        near, far, paired = lax.optimization_barrier((near, far, paired))
        near = traded(near, True)
        far = traded(far, False)
        parts = moment_parts(paired)

        base = [] if opening else [start]
        own = pl.pallas_call(
            lambda *refs, section=section: own_kernel(*refs, section=section),
            out_shape=state,
            in_specs=[vmem] * (2 + len(base)),
            out_specs=vmem,
            compiler_params=params(4),
            name=f"own{section}",
        )(current, cols, *base)
        spreads, nus, *forms = pl.pallas_call(
            lambda *refs, section=section: form_kernel(*refs, parts=len(parts), section=section),
            out_shape=(S((2, elems, TERMS * SUB), bf16), S((2 * modes, elems, LANE), f32))
            + (S((elems, 3 * vel), f32),) * 2,
            in_specs=[vmem] * (len(parts) + 2),
            out_specs=(vmem,) * 4,
            compiler_params=params(16),
            name=f"form{section}",
        )(*parts, rate, basis)

        tbl0, mean_table, centre, high, near_mean, far_mean = pl.pallas_call(
            lambda *refs, section=section: mean_kernel(*refs, section=section),
            out_shape=(
                S((rows * chunks, LANE), f32),
                S(((elems + 2 * slots) * chunks, LANE), f32),
                S((elems, vel), f32),
                S((3, elems, vel), f32),
                one,
                one,
            ),
            input_output_aliases={2: 0},
            in_specs=[smem] * 2 + [vmem] * 9,
            out_specs=(vmem,) * 6,
            scratch_shapes=[buffer(3 * SUB * chunks)] * 2 + [buffer(2 * slots * chunks)],
            compiler_params=params(16),
            name=f"mean{section}",
        )(offsets, src, tbl0, current, own, near, far, cols, nus, *forms)
        near_mean = traded(near_mean, True)
        far_mean = traded(far_mean, False)

        _, rest, sizes = pl.pallas_call(
            lambda *refs, section=section: rest_kernel(*refs, section=section),
            out_shape=(S((2 * rows * chunks, LANE), f32), S((5, elems, vel), f32), S((2, elems, vel), f32)),
            input_output_aliases={2: 0},
            in_specs=[smem] + [vmem] * 11,
            out_specs=(vmem,) * 3,
            scratch_shapes=[buffer(9 * SUB * chunks)] * 2 + evaluated(),
            compiler_params=params(20),
            name=f"rest{section}",
        )(src, tbl0, tbl12, current, own, near, far, high, spreads, nus, basis, cols)

        scratch = [buffer(3 * SUB * chunks)] * 2
        if not opening:
            scratch += [pltpu.VMEM(state.shape, f32), pltpu.SemaphoreType.DMA((4,))]
        made = pl.pallas_call(
            lambda *refs, section=section: limit_kernel(*refs, section=section),
            out_shape=(S(mean_table.shape, f32), state) + ((mom,) if opening else ()),
            in_specs=[smem] + [vmem] * 7,
            out_specs=(vmem,) * 3 if opening else (vmem, hbm),
            input_output_aliases={1: 0},
            scratch_shapes=scratch,
            compiler_params=params(8),
            name=f"limit{section}",
        )(away, mean_table, centre, rest, sizes, near_mean, far_mean, weights)
        if opening:
            _, current, partial = made
    return made[1]


def solution(mesh):
    in_specs = (
        P(None, "space", "vel"),
        P(None, None, "space"),
        P(None, "space"),
        P("space", None, None),
        P("space"),
    )
    return jax.shard_map(
        on_device, mesh=mesh, in_specs=in_specs, out_specs=P(None, "space", "vel"), check_vma=False
    )
```
